128 devices in a mesh: row: 16 (over z_lo, x, core), col: 8 (over y, z_hi).
Axes of the slice: x: 4, y: 4, z: 4 (z_hi: 2, z_lo: 2; z = z_hi * 2 + z_lo), core: 2. Of those that a mesh axis runs over, the one named last changes fastest.
Arguments:
- tokens: bfloat16 [12288, 4096], P('row', 'col'), may hold values from -6 to 6
- norm_gain: bfloat16 [4096], P('col'), may hold values from 0.099609375 to 1.8984375
- qkv_weight: bfloat16 [4096, 6144], P('row', 'col'), may hold values from -1 to 1
- q_gain: float32 [128], replicated, may hold values from 2 to 8
- k_gain: float32 [128], replicated, may hold values from 1 to 3
- out_weight: bfloat16 [4096, 4096], P('row', 'col'), may hold values from -0.09375 to 0.09375
Outputs:
- attn_out: bfloat16 [12288, 4096], P('row', 'col')
The draws below stay inside these ranges and needn't reach their ends.
All inputs are finite; a program needn't handle non-finite values.
Results may differ from the reference program's by a relative error of at most 0.013.
The reference program's roundings to bfloat16 on the way count: a program that leaves them out, or rounds other values in their place, can miss the bound.
Values may be sent and summed in bfloat16 or wider, within the bound.
A program may use at most 128 MiB of HBM per device.

```python
import jax
import jax.numpy as jnp
from jax import lax

D = 4096
QH = 32
KV = 8
HD = 128
GROUP = 4
QKVW = 6144
TOKENS = 12288


def draw_qkv_weight(key, part):
    base = jax.random.truncated_normal(key, -4.0, 4.0, (D, QKVW), jnp.float32) * D ** (-0.5)
    return base.astype(jnp.bfloat16)


def draw_q_gain(key, part):
    return jax.random.uniform(key, (HD,), jnp.float32, 2.0, 3.2)


def draw_k_gain(key, part):
    return jax.random.uniform(key, (HD,), jnp.float32, 1.0, 1.4)


def level_of(key, extent, split, smallest, largest):
    loudness, own = 1.0, jax.random.fold_in(key, 6)
    for position, blocks in split:
        heights = jnp.exp(jax.random.uniform(jax.random.fold_in(own, position), (blocks,), jnp.float32, smallest / len(split), largest / len(split)))
        loudness = loudness * jnp.repeat(heights, extent[position] // blocks).reshape([-1 if axis == position else 1 for axis in range(len(extent))])
    return loudness


def gaussian(key, extent, width, most, shards=(), kind=jnp.bfloat16):
    values = jax.random.normal(key, extent, jnp.float32) * width
    if len(shards) > 0:
        values = level_of(key, extent, shards, -0.22, 0.18) * values
    return jnp.clip(values, min=-most, max=most).astype(kind)


def setup_inputs(seed: int = 0) -> dict:
    arg_keys = jax.random.split(jax.random.key(seed), 7)
    tokens = gaussian(arg_keys[0], (TOKENS, D), 1.0, 6.0, ((0, 16), (1, 8)))
    norm_gain = jnp.clip(1.0 + 0.18 * jax.random.normal(arg_keys[1], (D,), jnp.float32), 0.099609375, 1.8984375).astype(jnp.bfloat16)
    qkv_weight = draw_qkv_weight(jax.random.fold_in(arg_keys[6], 71), 0)
    q_gain = draw_q_gain(jax.random.fold_in(arg_keys[6], 71), 0)
    k_gain = draw_k_gain(jax.random.fold_in(arg_keys[6], 71), 0)
    out_weight = gaussian(arg_keys[5], (QH * HD, D), (QH * HD) ** -0.5, 0.09375, ((0, 16), (1, 8)))
    return dict(tokens=tokens, norm_gain=norm_gain, qkv_weight=qkv_weight, q_gain=q_gain, k_gain=k_gain, out_weight=out_weight)


EPSILON = 1e-06
ROPE_BASE = 1000000.0

def rms_scale(values, gain):
    mean_sq = lax.optimization_barrier(jnp.mean(values * values, axis=-1, keepdims=True))
    return values * lax.rsqrt(mean_sq + EPSILON) * gain

def rotate(values, positions):
    half = values.shape[-1] // 2
    freqs = jnp.power(jnp.float32(ROPE_BASE), -jnp.arange(half, dtype=jnp.float32) * 2.0 / values.shape[-1])
    angles = positions.astype(jnp.float32)[:, None] * freqs[None, :]
    shape_b = (values.shape[0],) + (1,) * (values.ndim - 2) + (half,)
    cosine = jnp.cos(angles).reshape(shape_b)
    sine = jnp.sin(angles).reshape(shape_b)
    first = values[..., :half]
    second = values[..., half:]
    return jnp.concatenate([first * cosine - second * sine, second * cosine + first * sine], axis=-1)

def reference(tokens, norm_gain, qkv_weight, q_gain, k_gain, out_weight):
    total = tokens.shape[0]
    normed = rms_scale(tokens.astype(jnp.float32), norm_gain.astype(jnp.float32)).astype(jnp.bfloat16)
    projected = jnp.dot(normed, qkv_weight, preferred_element_type=jnp.float32)
    blocks = projected.reshape(total, KV, GROUP + 2, HD)
    positions = jnp.arange(total, dtype=jnp.int32)
    queries = rotate(rms_scale(blocks[:, :, :GROUP], q_gain), positions).astype(jnp.bfloat16)
    keys_all = rotate(rms_scale(blocks[:, :, GROUP], k_gain), positions).astype(jnp.bfloat16)
    values_all = blocks[:, :, GROUP + 1].astype(jnp.bfloat16)
    block = min(512, total)
    count = total // block
    keys_wide = keys_all.astype(jnp.float32)
    values_wide = values_all.astype(jnp.float32)

    def one_block(index):
        start = (index * block).astype(jnp.int32)
        query_block = lax.dynamic_slice_in_dim(queries, start, block, 0).astype(jnp.float32)
        query_pos = start + jnp.arange(block, dtype=jnp.int32)
        scores = jnp.einsum('qghd,kgd->ghqk', query_block, keys_wide) * HD ** (-0.5)
        allowed = positions[None, :] <= query_pos[:, None]
        masked = jnp.where(allowed, scores, -1e+30)
        top = lax.optimization_barrier(jnp.max(masked, axis=-1))
        weights = jnp.where(allowed, jnp.exp(masked - top[..., None]), 0.0)
        denom = lax.optimization_barrier(jnp.sum(weights, axis=-1))
        rounded = weights.astype(jnp.bfloat16).astype(jnp.float32)
        numer = jnp.einsum('ghqk,kgd->ghqd', rounded, values_wide)
        result = numer / denom[..., None]
        return result.transpose(2, 0, 1, 3).reshape(block, QH * HD).astype(jnp.bfloat16)
    attended = lax.map(one_block, jnp.arange(count, dtype=jnp.int32)).reshape(total, QH * HD)
    return jnp.dot(attended, out_weight, preferred_element_type=jnp.float32).astype(jnp.bfloat16)
```

```python
import functools
import math

import jax
import jax.numpy as jnp
from jax import lax
from jax.experimental import pallas as pl
from jax.experimental.pallas import tpu as pltpu
from jax.sharding import PartitionSpec as P

D = 4096
GROUP = 4
EPSILON = 1e-06
ROPE_BASE = 1000000.0
KEY_BLOCK = 768


def rms_scale(values, gain):
    mean_sq = jnp.mean(values * values, axis=-1, keepdims=True)
    return values * lax.rsqrt(mean_sq + EPSILON) * gain


def rotate(values, cosine, sine):
    half = values.shape[-1] // 2
    first = values[..., :half]
    second = values[..., half:]
    return jnp.concatenate(
        [first * cosine - second * sine, second * cosine + first * sine], axis=-1
    )


def flash_kernel(devices, scale, q_ref, kv_ref, o_ref, acc, top):
    rows = q_ref.shape[0]
    head_dim = kv_ref.shape[1] // 2
    chunk = pl.program_id(0)
    me = lax.axis_index("row")
    index = jnp.where(chunk == 0, 2 * me, 2 * devices - 1 - 2 * me)
    acc[...] = jnp.zeros_like(acc)
    top[...] = jnp.full_like(top, -1e30)
    factor_log2 = scale * math.log2(math.e)
    ones = jnp.ones((KEY_BLOCK, head_dim), jnp.bfloat16)

    def scores(h, keys):
        return lax.dot_general(
            q_ref[:, h * head_dim : (h + 1) * head_dim],
            keys,
            (((1,), (1,)), ((), ())),
            preferred_element_type=jnp.float32,
        )

    def step(block, allowed):
        start = pl.multiple_of(block * KEY_BLOCK, KEY_BLOCK)
        keys = kv_ref[pl.ds(start, KEY_BLOCK), :head_dim]
        values = kv_ref[pl.ds(start, KEY_BLOCK), head_dim:]
        wide = jnp.concatenate([values, ones], axis=1)
        following = scores(0, keys)
        for h in range(GROUP):
            raw = following
            if h + 1 < GROUP:
                following = scores(h + 1, keys)
            if allowed is not None:
                raw = jnp.where(allowed, raw, -1e30)
            before = top[h]
            now = jnp.maximum(before, jnp.max(raw, axis=-1, keepdims=True))
            shift = now[:, :1] * factor_log2
            weights = jnp.exp2(raw * factor_log2 - shift).astype(jnp.bfloat16)
            fade = jnp.exp2((before - now) * factor_log2)
            added = jnp.dot(weights, wide, preferred_element_type=jnp.float32)
            acc[h] = acc[h] * jnp.concatenate([fade, fade], axis=1) + added
            top[h] = now

    full = index // 2

    @pl.loop(0, full)
    def _(block):
        step(block, None)

    key_pos = full * KEY_BLOCK + lax.broadcasted_iota(jnp.int32, (rows, KEY_BLOCK), 1)
    query_pos = index * rows + lax.broadcasted_iota(jnp.int32, (rows, KEY_BLOCK), 0)
    step(full, key_pos <= query_pos)
    for h in range(GROUP):
        o_ref[:, h * head_dim : (h + 1) * head_dim] = (
            acc[h, :, :head_dim] / acc[h, :, head_dim:]
        ).astype(o_ref.dtype)


def flash(devices, scale, queries, keys_values):
    rows, width = queries.shape
    half = rows // 2
    head_dim = width // GROUP
    return pl.pallas_call(
        functools.partial(flash_kernel, devices, scale),
        out_shape=jax.ShapeDtypeStruct(queries.shape, jnp.bfloat16),
        grid=(2,),
        in_specs=[
            pl.BlockSpec((half, width), lambda i: (i, 0)),
            pl.BlockSpec(keys_values.shape, lambda i: (0, 0), pipeline_mode=pl.Buffered(1)),
        ],
        out_specs=pl.BlockSpec((half, width), lambda i: (i, 0)),
        scratch_shapes=[
            pltpu.VMEM((GROUP, half, 2 * head_dim), jnp.float32),
            pltpu.VMEM((GROUP, half, head_dim), jnp.float32),
        ],
        compiler_params=pltpu.CompilerParams(vmem_limit_bytes=48 * 1024 * 1024),
        cost_estimate=pl.CostEstimate(
            flops=10_000_000_000, bytes_accessed=8_000_000, transcendentals=20_000_000
        ),
    )(queries, keys_values)


def per_device(devices, tokens, norm_gain, qkv_weight, q_gain, k_gain, out_weight):
    rows = tokens.shape[0]
    half = rows // 2
    head_dim = q_gain.shape[0]
    tokens_full = lax.all_gather(tokens, "col", axis=1, tiled=True)
    gain_full = lax.all_gather(norm_gain, "col", axis=0, tiled=True)
    qkv_full = lax.all_gather(qkv_weight, "row", axis=0, tiled=True)
    widened = tokens_full.astype(jnp.float32)
    mean_sq = jnp.mean(widened * widened, axis=1, keepdims=True)
    normed = (widened * lax.rsqrt(mean_sq + EPSILON) * gain_full.astype(jnp.float32)).astype(
        jnp.bfloat16
    )
    projected = jnp.dot(normed, qkv_full, preferred_element_type=jnp.float32)
    me = lax.axis_index("row")
    positions = me * rows + jnp.arange(rows, dtype=jnp.int32)
    freqs = jnp.power(
        jnp.float32(ROPE_BASE),
        -jnp.arange(head_dim // 2, dtype=jnp.float32) * 2.0 / head_dim,
    )
    angles = positions.astype(jnp.float32)[:, None] * freqs[None, :]
    cosine, sine = jnp.cos(angles), jnp.sin(angles)
    pieces = [projected[:, i * head_dim : (i + 1) * head_dim] for i in range(GROUP + 2)]
    queries = jnp.concatenate(
        [rotate(rms_scale(u, q_gain), cosine, sine).astype(jnp.bfloat16) for u in pieces[:GROUP]],
        axis=1,
    )
    keys = rotate(rms_scale(pieces[GROUP], k_gain), cosine, sine).astype(jnp.bfloat16)
    values = pieces[GROUP + 1].astype(jnp.bfloat16)
    swap = [(i, devices - 1 - i) for i in range(devices)]
    keys_values = lax.all_gather(
        jnp.concatenate([keys, values], axis=1), "row", axis=0, tiled=True
    )
    balanced = jnp.concatenate(
        [queries[:half], lax.ppermute(queries[half:], "row", swap)], axis=0
    )
    attended = flash(devices, head_dim ** (-0.5), balanced, keys_values)
    attended = jnp.concatenate(
        [attended[:half], lax.ppermute(attended[half:], "row", swap)], axis=0
    )
    out_full = lax.all_gather(out_weight, "row", axis=0, tiled=True)
    result = jnp.dot(
        lax.all_gather(attended, "col", axis=1, tiled=True),
        out_full,
        preferred_element_type=jnp.float32,
    )
    return result.astype(jnp.bfloat16)


def solution(mesh):
    placed = (P("row", "col"), P("col"), P("row", "col"), P(), P(), P("row", "col"))
    return jax.shard_map(
        functools.partial(per_device, mesh.shape["row"]),
        mesh=mesh,
        in_specs=placed,
        out_specs=P("row", "col"),
        check_vma=False,
    )
```

```python
import functools
import math

import jax
import jax.numpy as jnp
from jax import lax
from jax.experimental import pallas as pl
from jax.experimental.pallas import tpu as pltpu
from jax.sharding import PartitionSpec as P

D = 4096
GROUP = 4
EPSILON = 1e-06
ROPE_BASE = 1000000.0
KEY_BLOCK = 768
MESH = pl.DeviceIdType.MESH


def ring(value, shift):
    return (value + shift + 4) % 4


class Place:
    def __init__(self):
        row, col = lax.axis_index("row"), lax.axis_index("col")
        self.z_lo, self.x, self.core = row // 8, (row // 2) % 4, row % 2
        self.y, self.z_hi = col // 2, col % 2
        self.z = 2 * self.z_hi + self.z_lo

    def device(self, **at):
        z = at.get("z", self.z)
        z_lo, z_hi = at.get("z_lo", z % 2), at.get("z_hi", z // 2)
        x, y, core = at.get("x", self.x), at.get("y", self.y), at.get("core", self.core)
        return {"row": 8 * z_lo + 2 * x + core, "col": 2 * y + z_hi}

    def step(self, axis, shift):
        return self.device(**{axis: ring(getattr(self, axis), shift)})

    def other_core(self):
        return self.device(core=1 - self.core)

    def turned(self):
        return self.device(core=self.z_hi, z_hi=self.core, z_lo=self.z_lo)

    def mirrored(self, bit):
        return self.z_lo + bit - 2 * bit * self.z_lo, self.x + bit * (3 - 2 * self.x)

    def chunk_to(self, half):
        z_lo, x = self.mirrored(self.core)
        return self.device(z_lo=z_lo, x=x, core=self.z_hi, z_hi=(self.core + half) % 2)

    def chunk_from(self, half):
        core = (self.z_hi + half) % 2
        z_lo, x = self.mirrored(core)
        return self.device(z_lo=z_lo, x=x, core=core, z_hi=self.core)

    def column(self, y=None, core=None):
        y = self.y if y is None else y
        return 2 * y + (self.core if core is None else core)

    def location(self, x, z):
        return 8 * (z % 2) + 2 * x + z // 2

    def chunk(self, half, x, z):
        first = 16 * (z % 2) + 4 * x + z // 2
        return first if half == 0 else 31 - first


class Net:
    def __init__(self, sent, landed, base=0):
        self.sent, self.landed, self.base, self.copies = sent, landed, base, []

    def send(self, ref, to, target=None):
        i = self.base + len(self.copies)
        copy = pltpu.make_async_remote_copy(
            src_ref=ref,
            dst_ref=ref if target is None else target,
            send_sem=self.sent.at[i],
            recv_sem=self.landed.at[i],
            device_id=to,
            device_id_type=MESH,
        )
        copy.start()
        self.copies.append(copy)
        return copy

    def finish(self):
        for copy in self.copies:
            copy.wait_send()


def greet(partners):
    barrier = pltpu.get_barrier_semaphore()
    for partner in partners:
        pl.semaphore_signal(barrier, inc=1, device_id=partner, device_id_type=MESH)
    pl.semaphore_wait(barrier, len(partners))


def plane_gather(net, here, full, rows, spot, own=None):
    axes = (("x", "z"), ("z", "x"))
    piece = rows // 2

    def at(half, first, second):
        x = ring(here.x, first if half == 0 else second)
        z = ring(here.z, second if half == 0 else first)
        return pl.multiple_of(spot(half, x, z), rows)

    def block(half, first, second):
        return full.at[pl.ds(at(half, first, second), rows), :]

    def part(half, first, second, way):
        start = at(half, first, second) + (0 if way == 1 else piece)
        return full.at[pl.ds(pl.multiple_of(start, piece), piece), :]

    def mine(half):
        return block(half, 0, 0) if own is None else own(half)

    one, two, onward, last = {}, {}, {}, {}
    both = [(half, way) for half in (0, 1) for way in (1, -1)]
    for half, way in both:
        one[half, way] = net.send(
            mine(half), here.step(axes[half][0], way), block(half, 0, 0)
        )
    for half, way in both:
        two[half, 0, way] = net.send(
            mine(half), here.step(axes[half][1], way), block(half, 0, 0)
        )
    yield
    for half, way in both:
        one[half, way].wait_recv()
        onward[half, way] = net.send(
            part(half, -way, 0, way), here.step(axes[half][0], way)
        )
    for half, way in both:
        for turn in (1, -1):
            two[half, -way, turn] = net.send(
                block(half, -way, 0), here.step(axes[half][1], turn)
            )
    yield
    for half, way in both:
        two[half, 0, way].wait_recv()
        last[half, 0, way] = net.send(
            part(half, 0, -way, way), here.step(axes[half][1], way)
        )
    yield
    for half, way in both:
        onward[half, way].wait_recv()
    for half, way in both:
        two[half, 2, way] = net.send(block(half, 2, 0), here.step(axes[half][1], way))
    yield
    for where in (-1, 1, 2):
        for half, way in both:
            two[half, where, way].wait_recv()
            last[half, where, way] = net.send(
                part(half, where, -way, way), here.step(axes[half][1], way)
            )
        yield
    for copy in last.values():
        copy.wait_recv()


def column_gather(net, here, full, width, own=None):
    rows = full.shape[0]
    piece = rows // 2

    def part(y, which):
        start = pl.multiple_of(here.column(y) * width, width)
        rows_of = slice(which * piece, (which + 1) * piece) if which < 2 else slice(None)
        return full.at[rows_of, pl.ds(start, width)]

    def mine(which):
        if own is None:
            return part(here.y, which)
        return own.at[slice(which * piece, (which + 1) * piece) if which < 2 else slice(None), :]

    far = {1: 0, -1: 1}
    near, onward, across = {}, {}, []
    for late in (0, 1):
        for way in (1, -1):
            which = far[way] if late == 0 else 1 - far[way]
            near[way, late] = net.send(mine(which), here.step("y", way), part(here.y, which))
    across.append(net.send(mine(2), here.other_core(), part(here.y, 2)))
    yield
    for way in (1, -1):
        near[way, 0].wait_recv()
        onward[way] = net.send(part(ring(here.y, -way), far[way]), here.step("y", way))
    yield
    for way in (1, -1):
        near[way, 1].wait_recv()
        across.append(net.send(part(ring(here.y, -way), 2), here.other_core()))
    yield
    yield
    for way in (1, -1):
        onward[way].wait_recv()
        across.append(net.send(part(ring(here.y, 2), far[way]), here.other_core()))
    yield
    for copy in across:
        copy.wait_recv()


def together(*gathers):
    gathers = list(gathers)
    while gathers:
        for gather in list(gathers):
            if next(gather, gathers) is gathers:
                gathers.remove(gather)


def plane_partners(here):
    return [here.step(axis, way) for axis in ("x", "z") for way in (1, -1)]


def column_partners(here):
    return [here.step("y", 1), here.step("y", -1), here.other_core()]


def small_gather(net, here, full, width):
    def part(y):
        return full.at[:, pl.ds(pl.multiple_of(here.column(y) * width, width), width)]

    near = {way: net.send(part(here.y), here.step("y", way)) for way in (1, -1)}
    across = [net.send(part(here.y), here.other_core())]
    yield
    near[1].wait_recv()
    onward = net.send(part(ring(here.y, -1)), here.step("y", 1))
    near[-1].wait_recv()
    for way in (1, -1):
        across.append(net.send(part(ring(here.y, -way)), here.other_core()))
    yield
    onward.wait_recv()
    across.append(net.send(part(ring(here.y, 2)), here.other_core()))
    yield
    for copy in across:
        copy.wait_recv()


class Exchange:
    def __init__(self, moves, sent, landed):
        self.moves = []
        for i, (source, target, to, keep) in enumerate(moves):
            copy = pltpu.make_async_remote_copy(
                src_ref=source,
                dst_ref=target,
                send_sem=sent.at[i],
                recv_sem=landed.at[i],
                device_id=to,
                device_id_type=MESH,
            )
            local = pltpu.make_async_copy(source, target, landed.at[i])
            self.moves.append((copy, local, keep))
            if keep is None:
                copy.start()
            else:
                pl.when(keep)(local.start)
                pl.when(jnp.logical_not(keep))(copy.start)

    def wait(self, i):
        copy, local, keep = self.moves[i]
        if keep is None:
            copy.wait()
        else:
            pl.when(keep)(local.wait)
            pl.when(jnp.logical_not(keep))(copy.wait)


def weight_move(here, weight, full):
    depth = weight.shape[0]
    mine = pl.multiple_of((8 * here.z_lo + 2 * here.x + here.core) * depth, depth)
    return weight, full.at[pl.ds(mine, depth), :], here.turned(), here.core == here.z_hi


def weight_gather(net, here, full, depth):
    half = depth // 2
    return plane_gather(
        net, here, full, half, lambda which, x, z: here.location(x, z) * depth + which * half
    )


def entry_kernel(tokens, gain, weight, tokens_full, gain_full, weight_full, sent, landed):
    here = Place()
    half_rows, width = tokens.shape[0] // 2, tokens.shape[1]
    greet(
        plane_partners(here)
        + column_partners(here)
        + [here.turned()]
        + [here.chunk_to(half) for half in (0, 1)]
        + [here.chunk_from(half) for half in (0, 1)]
    )
    columns = pl.ds(pl.multiple_of((2 * here.y + here.z_hi) * width, width), width)
    rows_to = pl.ds(pl.multiple_of(here.core * half_rows, half_rows), half_rows)
    landing = tokens_full.at[rows_to, columns]
    stays = jnp.logical_and(here.core == 0, here.z_hi == 0)
    first = Exchange(
        [
            weight_move(here, weight, weight_full),
            (tokens.at[:half_rows, :], landing, here.chunk_to(0), stays),
            (tokens.at[half_rows:, :], landing, here.chunk_to(1), None),
            (gain, gain_full.at[:, columns], here.turned(), here.core == here.z_hi),
        ],
        sent,
        landed,
    )
    net = Net(sent, landed, 4)
    first.wait(0)
    weights = weight_gather(net, here, weight_full, weight.shape[0])
    next(weights)
    first.wait(1)
    first.wait(2)
    features = column_gather(net, here, tokens_full, width)
    next(features)
    first.wait(3)
    gains = small_gather(net, here, gain_full, width)
    together(features, weights, gains)
    net.finish()


def keys_kernel(block, full, sent, landed, kept):
    here = Place()
    half_rows = block.shape[0] // 2
    greet(plane_partners(here))
    copies = []
    for half in (0, 1):
        start = pl.multiple_of(here.chunk(half, here.x, here.z) * half_rows, half_rows)
        copies.append(
            pltpu.make_async_copy(
                block.at[half * half_rows : (half + 1) * half_rows, :],
                full.at[pl.ds(start, half_rows), :],
                kept.at[half],
            )
        )
        copies[half].start()
    net = Net(sent, landed)
    together(
        plane_gather(
            net, here, full, half_rows,
            lambda half, x, z: here.chunk(half, x, z) * half_rows,
            own=lambda half: block.at[half * half_rows : (half + 1) * half_rows, :],
        )
    )
    for copy in copies:
        copy.wait()
    net.finish()


def heads_kernel(block, weight, full, weight_full, sent, landed, kept):
    here = Place()
    width = block.shape[1]
    greet(plane_partners(here) + column_partners(here) + [here.turned()])
    first = Exchange([weight_move(here, weight, weight_full)], sent, landed)
    net = Net(sent, landed, 1)
    start = pl.multiple_of(here.column() * width, width)
    copy = pltpu.make_async_copy(block, full.at[:, pl.ds(start, width)], kept.at[0])
    copy.start()
    heads = column_gather(net, here, full, width, own=block)
    next(heads)
    first.wait(0)
    together(weight_gather(net, here, weight_full, weight.shape[0]), heads)
    copy.wait()
    net.finish()


def exit_kernel(block, home, sent, landed):
    here = Place()
    half_rows = block.shape[0] // 2
    greet([f(half) for f in (here.chunk_to, here.chunk_from) for half in (0, 1)])
    moves = []
    for half in (0, 1):
        slot = pl.multiple_of(((here.z_hi + half) % 2) * half_rows, half_rows)
        stays = jnp.logical_and(here.core == 0, here.z_hi == 0) if half == 0 else None
        moves.append(
            (
                block.at[pl.ds(slot, half_rows), :],
                home.at[half * half_rows : (half + 1) * half_rows, :],
                here.chunk_from(half),
                stays,
            )
        )
    last = Exchange(moves, sent, landed)
    last.wait(0)
    last.wait(1)


PLANE, COLUMN, SMALL = 40, 11, 7


def remote_call(kernel, number, copies, kept, shapes, *operands):
    return pl.pallas_call(
        kernel,
        out_shape=[jax.ShapeDtypeStruct(shape, jnp.bfloat16) for shape in shapes],
        in_specs=[pl.BlockSpec(memory_space=pl.ANY)] * len(operands),
        out_specs=[pl.BlockSpec(memory_space=pl.ANY)] * len(shapes),
        scratch_shapes=[
            pltpu.SemaphoreType.DMA((copies,)),
            pltpu.SemaphoreType.DMA((copies,)),
        ]
        + ([pltpu.SemaphoreType.DMA((kept,))] if kept else []),
        compiler_params=pltpu.CompilerParams(collective_id=number, has_side_effects=True),
        name=kernel.__name__,
    )(*operands)


def flash_kernel(scale, q_ref, kv_ref, o_ref, acc, top):
    rows = q_ref.shape[0]
    head_dim = kv_ref.shape[1] // 2
    here = Place()
    index = jnp.where(
        pl.program_id(0) == 0, here.chunk(0, here.x, here.z), here.chunk(1, here.x, here.z)
    )
    acc[...] = jnp.zeros_like(acc)
    top[...] = jnp.full_like(top, -1e30)
    factor_log2 = scale * math.log2(math.e)
    ones = jnp.ones((KEY_BLOCK, head_dim), jnp.bfloat16)

    def scores(h, keys):
        return lax.dot_general(
            q_ref[:, h * head_dim : (h + 1) * head_dim],
            keys,
            (((1,), (1,)), ((), ())),
            preferred_element_type=jnp.float32,
        )

    def step(block, allowed):
        start = pl.multiple_of(block * KEY_BLOCK, KEY_BLOCK)
        keys = kv_ref[pl.ds(start, KEY_BLOCK), :head_dim]
        values = kv_ref[pl.ds(start, KEY_BLOCK), head_dim:]
        wide = jnp.concatenate([values, ones], axis=1)
        following = scores(0, keys)
        for h in range(GROUP):
            raw = following
            if h + 1 < GROUP:
                following = scores(h + 1, keys)
            if allowed is not None:
                raw = jnp.where(allowed, raw, -1e30)
            before = top[h]
            now = jnp.maximum(before, jnp.max(raw, axis=-1, keepdims=True))
            shift = now[:, :1] * factor_log2
            weights = jnp.exp2(raw * factor_log2 - shift).astype(jnp.bfloat16)
            fade = jnp.exp2((before - now) * factor_log2)
            added = jnp.dot(weights, wide, preferred_element_type=jnp.float32)
            acc[h] = acc[h] * jnp.concatenate([fade, fade], axis=1) + added
            top[h] = now

    full = index // 2

    @pl.loop(0, full)
    def _(block):
        step(block, None)

    key_pos = full * KEY_BLOCK + lax.broadcasted_iota(jnp.int32, (rows, KEY_BLOCK), 1)
    query_pos = index * rows + lax.broadcasted_iota(jnp.int32, (rows, KEY_BLOCK), 0)
    step(full, key_pos <= query_pos)
    for h in range(GROUP):
        o_ref[:, h * head_dim : (h + 1) * head_dim] = (
            acc[h, :, :head_dim] / acc[h, :, head_dim:]
        ).astype(o_ref.dtype)


def flash(scale, queries, keys_values):
    rows, width = queries.shape
    half = rows // 2
    head_dim = width // GROUP
    return pl.pallas_call(
        functools.partial(flash_kernel, scale),
        out_shape=jax.ShapeDtypeStruct(queries.shape, jnp.bfloat16),
        grid=(2,),
        in_specs=[
            pl.BlockSpec((half, width), lambda i: (i, 0)),
            pl.BlockSpec(keys_values.shape, lambda i: (0, 0), pipeline_mode=pl.Buffered(1)),
        ],
        out_specs=pl.BlockSpec((half, width), lambda i: (i, 0)),
        scratch_shapes=[
            pltpu.VMEM((GROUP, half, 2 * head_dim), jnp.float32),
            pltpu.VMEM((GROUP, half, head_dim), jnp.float32),
        ],
        compiler_params=pltpu.CompilerParams(vmem_limit_bytes=48 * 1024 * 1024),
        cost_estimate=pl.CostEstimate(
            flops=10_000_000_000, bytes_accessed=8_000_000, transcendentals=20_000_000
        ),
    )(queries, keys_values)


def rms_scale(values, gain):
    mean_sq = jnp.mean(values * values, axis=-1, keepdims=True)
    return values * lax.rsqrt(mean_sq + EPSILON) * gain


def rotate(values, cosine, sine):
    half = values.shape[-1] // 2
    first = values[..., :half]
    second = values[..., half:]
    return jnp.concatenate(
        [first * cosine - second * sine, second * cosine + first * sine], axis=-1
    )


def per_device(sizes, tokens, norm_gain, qkv_weight, q_gain, k_gain, out_weight):
    n_row, n_col = sizes
    rows, width = tokens.shape
    half = rows // 2
    head_dim = q_gain.shape[0]
    tokens_full, gain_full, qkv_full = remote_call(
        entry_kernel, 1, 4 + PLANE + COLUMN + SMALL, 0,
        [(rows, n_col * width), (16, n_col * width), (n_row * qkv_weight.shape[0], qkv_weight.shape[1])],
        tokens, jnp.broadcast_to(norm_gain[None, :], (16, width)), qkv_weight,
    )
    widened = tokens_full.astype(jnp.float32)
    mean_sq = jnp.mean(widened * widened, axis=1, keepdims=True)
    normed = (
        widened * lax.rsqrt(mean_sq + EPSILON) * gain_full[:1].astype(jnp.float32)
    ).astype(jnp.bfloat16)
    projected = jnp.dot(normed, qkv_full, preferred_element_type=jnp.float32)
    here = Place()
    chunks = [here.chunk(which, here.x, here.z) for which in (0, 1)]
    within = jnp.arange(half, dtype=jnp.int32)
    positions = jnp.concatenate([chunk * half + within for chunk in chunks])
    freqs = jnp.power(
        jnp.float32(ROPE_BASE),
        -jnp.arange(head_dim // 2, dtype=jnp.float32) * 2.0 / head_dim,
    )
    angles = positions.astype(jnp.float32)[:, None] * freqs[None, :]
    cosine, sine = jnp.cos(angles), jnp.sin(angles)
    pieces = [projected[:, i * head_dim : (i + 1) * head_dim] for i in range(GROUP + 2)]
    queries = jnp.concatenate(
        [rotate(rms_scale(u, q_gain), cosine, sine).astype(jnp.bfloat16) for u in pieces[:GROUP]],
        axis=1,
    )
    keys = rotate(rms_scale(pieces[GROUP], k_gain), cosine, sine).astype(jnp.bfloat16)
    values = pieces[GROUP + 1].astype(jnp.bfloat16)
    (keys_values,) = remote_call(
        keys_kernel, 2, PLANE, 2, [(n_row * rows, 2 * head_dim)],
        jnp.concatenate([keys, values], axis=1),
    )
    attended = flash(head_dim ** (-0.5), queries, keys_values)
    attended_full, out_full = remote_call(
        heads_kernel, 3, 1 + PLANE + COLUMN, 1,
        [(rows, n_col * attended.shape[1]), (n_row * out_weight.shape[0], out_weight.shape[1])],
        attended, out_weight,
    )
    result = jnp.dot(attended_full, out_full, preferred_element_type=jnp.float32)
    (home,) = remote_call(
        exit_kernel, 4, 2, 0, [(rows, out_weight.shape[1])], result.astype(jnp.bfloat16)
    )
    return home


def solution(mesh):
    placed = (P("row", "col"), P("col"), P("row", "col"), P(), P(), P("row", "col"))
    return jax.shard_map(
        functools.partial(per_device, (mesh.shape["row"], mesh.shape["col"])),
        mesh=mesh,
        in_specs=placed,
        out_specs=P("row", "col"),
        check_vma=False,
    )
```

```python
import functools
import math

import jax
import jax.numpy as jnp
from jax import lax
from jax.experimental import pallas as pl
from jax.experimental.pallas import tpu as pltpu
from jax.sharding import PartitionSpec as P

D = 4096
GROUP = 4
EPSILON = 1e-06
ROPE_BASE = 1000000.0
MESH = pl.DeviceIdType.MESH


def ring(value, shift):
    return (value + shift + 4) % 4


class Place:
    def __init__(self):
        row, col = lax.axis_index("row"), lax.axis_index("col")
        self.z_lo, self.x, self.core = row // 8, (row // 2) % 4, row % 2
        self.y, self.z_hi = col // 2, col % 2
        self.z = 2 * self.z_hi + self.z_lo

    def device(self, **at):
        z = at.get("z", self.z)
        z_lo, z_hi = at.get("z_lo", z % 2), at.get("z_hi", z // 2)
        x, y, core = at.get("x", self.x), at.get("y", self.y), at.get("core", self.core)
        return {"row": 8 * z_lo + 2 * x + core, "col": 2 * y + z_hi}

    def step(self, axis, shift):
        return self.device(**{axis: ring(getattr(self, axis), shift)})

    def other_core(self):
        return self.device(core=1 - self.core)

    def turned(self):
        return self.device(core=self.z_hi, z_hi=self.core, z_lo=self.z_lo)

    def mirrored(self, bit):
        return self.z_lo + bit - 2 * bit * self.z_lo, self.x + bit * (3 - 2 * self.x)

    def chunk_to(self, half):
        z_lo, x = self.mirrored(self.core)
        return self.device(z_lo=z_lo, x=x, core=self.z_hi, z_hi=(self.core + half) % 2)

    def chunk_from(self, half):
        core = (self.z_hi + half) % 2
        z_lo, x = self.mirrored(core)
        return self.device(z_lo=z_lo, x=x, core=core, z_hi=self.core)

    def column(self, y=None, core=None):
        y = self.y if y is None else y
        return 2 * y + (self.core if core is None else core)

    def location(self, x, z):
        return 8 * (z % 2) + 2 * x + z // 2

    def chunk(self, half, x, z):
        first = 16 * (z % 2) + 4 * x + z // 2
        return first if half == 0 else 31 - first


class Net:
    def __init__(self, sent, landed, base=0):
        self.sent, self.landed, self.base, self.copies = sent, landed, base, []

    def send(self, ref, to, target=None):
        i = self.base + len(self.copies)
        copy = pltpu.make_async_remote_copy(
            src_ref=ref,
            dst_ref=ref if target is None else target,
            send_sem=self.sent.at[i],
            recv_sem=self.landed.at[i],
            device_id=to,
            device_id_type=MESH,
        )
        copy.start()
        self.copies.append(copy)
        return copy

    def send_built(self, build):
        copy = Built(self, self.base + len(self.copies), build)
        copy.copy().start()
        self.copies.append(copy)
        return copy

    def finish(self):
        for copy in self.copies:
            copy.wait_send()


class Built:
    def __init__(self, net, i, build):
        self.net, self.i, self.build = net, i, build

    def copy(self):
        ref, to, target = self.build()
        return pltpu.make_async_remote_copy(
            src_ref=ref,
            dst_ref=target,
            send_sem=self.net.sent.at[self.i],
            recv_sem=self.net.landed.at[self.i],
            device_id=to,
            device_id_type=MESH,
        )

    def wait_recv(self):
        self.copy().wait_recv()

    def wait_send(self):
        self.copy().wait_send()


def greet(partners):
    barrier = pltpu.get_barrier_semaphore()
    for partner in partners:
        pl.semaphore_signal(barrier, inc=1, device_id=partner, device_id_type=MESH)
    pl.semaphore_wait(barrier, len(partners))


def plane_gather(net, here, full, rows, spot, own=None):
    axes = (("x", "z"), ("z", "x"))
    piece = rows // 2

    def at(half, first, second):
        x = ring(here.x, first if half == 0 else second)
        z = ring(here.z, second if half == 0 else first)
        return pl.multiple_of(spot(half, x, z), rows)

    def block(half, first, second):
        return full[half].at[pl.ds(at(half, first, second), rows), :]

    def part(half, first, second, way):
        start = at(half, first, second) + (0 if way == 1 else piece)
        return full[half].at[pl.ds(pl.multiple_of(start, piece), piece), :]

    def whole(half, where, way, axis=1):
        def build():
            target = block(half, where, 0)
            source = own[half] if where == 0 and own is not None else target
            return source, here.step(axes[half][axis], way), target

        return net.send_built(build)

    def share(half, first, second, way, axis):
        def build():
            ref = part(half, first, second, way)
            return ref, here.step(axes[half][axis], way), ref

        return net.send_built(build)

    one, two, onward, last = {}, {}, {}, {}
    both = [(half, way) for half in (0, 1) for way in (1, -1)]
    for half, way in both:
        one[half, way] = whole(half, 0, way, 0)
    for half, way in both:
        two[half, 0, way] = whole(half, 0, way)
    yield
    for half, way in both:
        one[half, way].wait_recv()
        onward[half, way] = share(half, -way, 0, way, 0)
    for half, way in both:
        for turn in (1, -1):
            two[half, -way, turn] = whole(half, -way, turn)
    for half, way in both:
        two[half, 0, way].wait_recv()
        last[half, 0, way] = share(half, 0, -way, way, 1)
    yield
    for half, way in both:
        onward[half, way].wait_recv()
    for half, way in both:
        two[half, 2, way] = whole(half, 2, way)
    yield
    for where in (-1, 1):
        for half, way in both:
            two[half, where, way].wait_recv()
            last[half, where, way] = share(half, where, -way, way, 1)
    yield
    for half, way in both:
        last[half, 0, way].wait_recv()
    for half, way in both:
        two[half, 2, way].wait_recv()
        last[half, 2, way] = share(half, 2, -way, way, 1)
    yield
    for where in (-1, 1):
        for half, way in both:
            last[half, where, way].wait_recv()
    yield
    for half, way in both:
        last[half, 2, way].wait_recv()


def column_gather(net, here, full, width, own=None):
    rows = full.shape[0]
    piece = rows // 2

    def part(y, which):
        start = pl.multiple_of(here.column(y) * width, width)
        rows_of = slice(which * piece, (which + 1) * piece) if which < 2 else slice(None)
        return full.at[rows_of, pl.ds(start, width)]

    def mine(which):
        if own is None:
            return part(here.y, which)
        return own.at[slice(which * piece, (which + 1) * piece) if which < 2 else slice(None), :]

    far = {1: 0, -1: 1}
    near, onward, across = {}, {}, []
    for late in (0, 1):
        for way in (1, -1):
            which = far[way] if late == 0 else 1 - far[way]
            near[way, late] = net.send(mine(which), here.step("y", way), part(here.y, which))
    across.append(net.send(mine(2), here.other_core(), part(here.y, 2)))
    yield
    for way in (1, -1):
        near[way, 0].wait_recv()
        onward[way] = net.send(part(ring(here.y, -way), far[way]), here.step("y", way))
    yield
    for way in (1, -1):
        near[way, 1].wait_recv()
        across.append(net.send(part(ring(here.y, -way), 2), here.other_core()))
    yield
    yield
    for way in (1, -1):
        onward[way].wait_recv()
        across.append(net.send(part(ring(here.y, 2), far[way]), here.other_core()))
    yield
    for copy in across:
        copy.wait_recv()


def together(*gathers):
    gathers = list(gathers)
    while gathers:
        for gather in list(gathers):
            if next(gather, gathers) is gathers:
                gathers.remove(gather)


def plane_partners(here):
    return [here.step(axis, way) for axis in ("x", "z") for way in (1, -1)]


def column_partners(here):
    return [here.step("y", 1), here.step("y", -1), here.other_core()]


def small_gather(net, here, full, width):
    def part(y):
        return full.at[:, pl.ds(pl.multiple_of(here.column(y) * width, width), width)]

    near = {way: net.send(part(here.y), here.step("y", way)) for way in (1, -1)}
    across = [net.send(part(here.y), here.other_core())]
    yield
    near[1].wait_recv()
    onward = net.send(part(ring(here.y, -1)), here.step("y", 1))
    near[-1].wait_recv()
    for way in (1, -1):
        across.append(net.send(part(ring(here.y, -way)), here.other_core()))
    yield
    onward.wait_recv()
    across.append(net.send(part(ring(here.y, 2)), here.other_core()))
    yield
    for copy in across:
        copy.wait_recv()


class Exchange:
    def __init__(self, moves, sent, landed):
        self.moves = []
        for i, (source, target, to, keep) in enumerate(moves):
            copy = pltpu.make_async_remote_copy(
                src_ref=source,
                dst_ref=target,
                send_sem=sent.at[i],
                recv_sem=landed.at[i],
                device_id=to,
                device_id_type=MESH,
            )
            local = pltpu.make_async_copy(source, target, landed.at[i])
            self.moves.append((copy, local, keep))
            if keep is None:
                copy.start()
            else:
                pl.when(keep)(local.start)
                pl.when(jnp.logical_not(keep))(copy.start)

    def wait(self, i):
        copy, local, keep = self.moves[i]
        if keep is None:
            copy.wait()
        else:
            pl.when(keep)(local.wait)
            pl.when(jnp.logical_not(keep))(copy.wait)


def weight_move(here, weight, full):
    depth = weight.shape[0]
    mine = pl.multiple_of((8 * here.z_lo + 2 * here.x + here.core) * depth, depth)
    return weight, full.at[pl.ds(mine, depth), :], here.turned(), here.core == here.z_hi


def weight_gather(net, here, full, depth):
    half = depth // 2
    return plane_gather(
        net, here, (full, full), half,
        lambda which, x, z: here.location(x, z) * depth + which * half,
    )


def entry_kernel(tokens, gain, weight, tokens_full, gain_full, weight_full, sent, landed):
    here = Place()
    half_rows, width = tokens.shape[0] // 2, tokens.shape[1]
    greet(
        plane_partners(here)
        + column_partners(here)
        + [here.turned()]
        + [here.chunk_to(half) for half in (0, 1)]
        + [here.chunk_from(half) for half in (0, 1)]
    )
    columns = pl.ds(pl.multiple_of((2 * here.y + here.z_hi) * width, width), width)
    rows_to = pl.ds(pl.multiple_of(here.core * half_rows, half_rows), half_rows)
    landing = tokens_full.at[rows_to, columns]
    stays = jnp.logical_and(here.core == 0, here.z_hi == 0)
    first = Exchange(
        [
            weight_move(here, weight, weight_full),
            (tokens.at[:half_rows, :], landing, here.chunk_to(0), stays),
            (tokens.at[half_rows:, :], landing, here.chunk_to(1), None),
            (gain, gain_full.at[:, columns], here.turned(), here.core == here.z_hi),
        ],
        sent,
        landed,
    )
    net = Net(sent, landed, 4)
    first.wait(0)
    weights = weight_gather(net, here, weight_full, weight.shape[0])
    next(weights)
    first.wait(1)
    first.wait(2)
    features = column_gather(net, here, tokens_full, width)
    next(features)
    first.wait(3)
    gains = small_gather(net, here, gain_full, width)
    together(features, weights, gains)
    net.finish()


def heads_kernel(block, weight, full, weight_full, sent, landed, kept):
    here = Place()
    width = block.shape[1]
    greet(plane_partners(here) + column_partners(here) + [here.turned()])
    first = Exchange([weight_move(here, weight, weight_full)], sent, landed)
    net = Net(sent, landed, 1)
    start = pl.multiple_of(here.column() * width, width)
    copy = pltpu.make_async_copy(block, full.at[:, pl.ds(start, width)], kept.at[0])
    copy.start()
    heads = column_gather(net, here, full, width, own=block)
    next(heads)
    first.wait(0)
    together(weight_gather(net, here, weight_full, weight.shape[0]), heads)
    copy.wait()
    net.finish()


def exit_kernel(block, home, sent, landed):
    here = Place()
    half_rows = block.shape[0] // 2
    greet([f(half) for f in (here.chunk_to, here.chunk_from) for half in (0, 1)])
    moves = []
    for half in (0, 1):
        slot = pl.multiple_of(((here.z_hi + half) % 2) * half_rows, half_rows)
        stays = jnp.logical_and(here.core == 0, here.z_hi == 0) if half == 0 else None
        moves.append(
            (
                block.at[pl.ds(slot, half_rows), :],
                home.at[half * half_rows : (half + 1) * half_rows, :],
                here.chunk_from(half),
                stays,
            )
        )
    last = Exchange(moves, sent, landed)
    last.wait(0)
    last.wait(1)


PLANE, COLUMN, SMALL = 40, 11, 7


def remote_call(kernel, number, copies, kept, shapes, *operands):
    return pl.pallas_call(
        kernel,
        out_shape=[jax.ShapeDtypeStruct(shape, jnp.bfloat16) for shape in shapes],
        in_specs=[pl.BlockSpec(memory_space=pl.ANY)] * len(operands),
        out_specs=[pl.BlockSpec(memory_space=pl.ANY)] * len(shapes),
        scratch_shapes=[
            pltpu.SemaphoreType.DMA((copies,)),
            pltpu.SemaphoreType.DMA((copies,)),
        ]
        + ([pltpu.SemaphoreType.DMA((kept,))] if kept else []),
        compiler_params=pltpu.CompilerParams(collective_id=number, has_side_effects=True),
        name=kernel.__name__,
    )(*operands)


def attention_kernel(
    scale, q_ref, k_ref, v_ref, o_ref, keys, values, acc, top, sent, landed
):
    rows, head_dim = k_ref.shape
    half_rows = rows // 2
    here = Place()
    factor_log2 = scale * math.log2(math.e)
    acc[...] = jnp.zeros_like(acc)
    top[...] = jnp.full_like(top, -1e30)

    def unit(which, key_parts, value_parts, allowed=None):
        key_block = [ref[...] for ref in key_parts]
        value_block = [ref[...] for ref in value_parts]
        key_block = key_block[0] if len(key_block) == 1 else jnp.concatenate(key_block, axis=0)
        value_block = (
            value_block[0] if len(value_block) == 1 else jnp.concatenate(value_block, axis=0)
        )
        wide = jnp.concatenate([value_block, jnp.ones_like(value_block)], axis=1)
        asked = q_ref.at[pl.ds(pl.multiple_of(which * half_rows, half_rows), half_rows), :]

        def scores(h):
            return lax.dot_general(
                asked[:, h * head_dim : (h + 1) * head_dim],
                key_block,
                (((1,), (1,)), ((), ())),
                preferred_element_type=jnp.float32,
            )

        following = scores(0)
        for h in range(GROUP):
            raw = following
            if h + 1 < GROUP:
                following = scores(h + 1)
            if allowed is not None:
                raw = jnp.where(allowed, raw, -1e30)
            before = top[which, h]
            now = jnp.maximum(before, jnp.max(raw, axis=-1, keepdims=True))
            shift = now[:, :1] * factor_log2
            weights = jnp.exp2(raw * factor_log2 - shift).astype(jnp.bfloat16)
            fade = jnp.exp2((before - now) * factor_log2)
            added = jnp.dot(weights, wide, preferred_element_type=jnp.float32)
            acc[which, h] = acc[which, h] * jnp.concatenate([fade, fade], axis=1) + added
            top[which, h] = now

    low, high = here.z_lo, 1 - here.z_lo

    def low_chunk(x, z):
        chunk = here.chunk(0, x, z)
        return chunk + (z % 2) * (31 - 2 * chunk)

    def part(full, x, z, which):
        start = (4 * x + z) * rows + which * half_rows
        return full.at[pl.ds(pl.multiple_of(start, half_rows), half_rows), :]

    def at_once(places):
        spots = [(ring(here.x, dx), ring(here.z, dz)) for dx, dz in places]
        unit(
            high,
            [part(keys, x, z, z % 2) for x, z in spots],
            [part(values, x, z, z % 2) for x, z in spots],
        )
        for x, z in spots:
            before = (31 + low_chunk(here.x, here.z) - low_chunk(x, z)) // 32
            which = high + before * (low - high)
            theirs = 1 - z % 2 + before * (2 * (z % 2) - 1)
            unit(which, [part(keys, x, z, theirs)], [part(values, x, z, theirs)])

    greet(plane_partners(here))
    net = Net(sent, landed)
    arrivals = plane_gather(
        net, here, (keys, values), rows, lambda half, x, z: (4 * x + z) * rows, (k_ref, v_ref)
    )
    next(arrivals)

    def own(ref, which):
        return ref.at[pl.ds(pl.multiple_of(which * half_rows, half_rows), half_rows), :]

    square = (half_rows, half_rows)
    allowed = lax.broadcasted_iota(jnp.int32, square, 1) <= lax.broadcasted_iota(
        jnp.int32, square, 0
    )
    unit(low, [own(k_ref, low)], [own(v_ref, low)], allowed)
    unit(high, [own(k_ref, high)], [own(v_ref, high)], allowed)
    unit(high, [own(k_ref, low)], [own(v_ref, low)])
    pairs = [
        ((1, 0), (3, 0)), ((0, 1), (0, 3)), ((1, 1), (1, 3)), ((3, 1), (3, 3)),
        ((2, 0), (0, 2)), ((2, 1), (2, 3)), ((1, 2), (3, 2)),
    ]
    steps = (0, 1, 2, 4, 5)

    tables = tuple(
        sum(pair[i][j] * 4**n for n, pair in enumerate(pairs)) for i in (0, 1) for j in (0, 1)
    )

    def stage(n, rest):
        for when in steps:
            pl.when(n == when)(lambda: next(arrivals) and None)
        digits = [r % 4 for r in rest]
        at_once([digits[:2], digits[2:]])
        return tuple(r // 4 for r in rest)

    lax.fori_loop(0, len(pairs), stage, tuple(jnp.int32(t) for t in tables))
    next(arrivals, None)
    at_once([(2, 2)])
    net.finish()
    for which in (0, 1):
        for h in range(GROUP):
            o_ref[
                which * half_rows : (which + 1) * half_rows, h * head_dim : (h + 1) * head_dim
            ] = (acc[which, h, :, :head_dim] / acc[which, h, :, head_dim:]).astype(o_ref.dtype)


def attention(scale, places, queries, keys, values):
    rows, width = queries.shape
    head_dim = keys.shape[1]
    return pl.pallas_call(
        functools.partial(attention_kernel, scale),
        out_shape=jax.ShapeDtypeStruct(queries.shape, jnp.bfloat16),
        in_specs=[pl.BlockSpec(memory_space=pltpu.VMEM)] * 3,
        out_specs=pl.BlockSpec(memory_space=pltpu.VMEM),
        scratch_shapes=[
            pltpu.VMEM((places * rows, head_dim), jnp.bfloat16),
            pltpu.VMEM((places * rows, head_dim), jnp.bfloat16),
            pltpu.VMEM((2, GROUP, rows // 2, 2 * head_dim), jnp.float32),
            pltpu.VMEM((2, GROUP, rows // 2, head_dim), jnp.float32),
            pltpu.SemaphoreType.DMA((PLANE,)),
            pltpu.SemaphoreType.DMA((PLANE,)),
        ],
        compiler_params=pltpu.CompilerParams(
            collective_id=2, has_side_effects=True, vmem_limit_bytes=48 * 1024 * 1024
        ),
        name="attention_kernel",
    )(queries, keys, values)


def project_kernel(
    tokens, gain, weight, cosine, sine, q_gain, k_gain, q_ref, k_ref, v_ref
):
    rows, depth = tokens.shape
    head_dim = k_ref.shape[1]
    half = head_dim // 2
    step = 512
    spans = [slice(i, i + step) for i in range(0, depth, step)]
    squares = jnp.zeros((rows, 128), jnp.float32)
    for span in spans:
        part = tokens[:, span].astype(jnp.float32)
        part = part * part
        for i in range(0, step, 128):
            squares = squares + part[:, i : i + 128]
    inverse = lax.rsqrt(jnp.sum(squares, axis=1, keepdims=True) / depth + EPSILON)
    total = None
    for span in spans:
        part = tokens[:, span].astype(jnp.float32) * inverse
        part = (part * gain[:1, span].astype(jnp.float32)).astype(jnp.bfloat16)
        added = jnp.dot(part, weight[span, :], preferred_element_type=jnp.float32)
        total = added if total is None else total + added
    cos, sin = cosine[...], sine[...]

    def turned(slot, head_gain):
        u = total[:, slot * head_dim : (slot + 1) * head_dim]
        mean_sq = jnp.mean(u * u, axis=-1, keepdims=True)
        u = u * lax.rsqrt(mean_sq + EPSILON) * head_gain
        return (u * cos + pltpu.roll(u, half, 1) * sin).astype(jnp.bfloat16)

    for slot in range(GROUP):
        q_ref[:, slot * head_dim : (slot + 1) * head_dim] = turned(slot, q_gain[...])
    k_ref[...] = turned(GROUP, k_gain[...])
    v_ref[...] = total[:, (GROUP + 1) * head_dim :].astype(jnp.bfloat16)


def project(tokens, gain, weight, cosine, sine, q_gain, k_gain):
    rows, depth = tokens.shape
    head_dim = q_gain.shape[1]
    block = rows // 4

    def by_rows(width):
        return pl.BlockSpec((block, width), lambda i: (i, 0))

    def whole(array):
        return pl.BlockSpec(array.shape, lambda i: (0, 0), pipeline_mode=pl.Buffered(1))

    widths = [GROUP * head_dim, head_dim, head_dim]
    return pl.pallas_call(
        project_kernel,
        out_shape=[jax.ShapeDtypeStruct((rows, w), jnp.bfloat16) for w in widths],
        grid=(4,),
        in_specs=[
            by_rows(depth), whole(gain), whole(weight), by_rows(head_dim), by_rows(head_dim),
            whole(q_gain), whole(k_gain),
        ],
        out_specs=[by_rows(w) for w in widths],
        compiler_params=pltpu.CompilerParams(vmem_limit_bytes=40 * 1024 * 1024),
        name="project_kernel",
    )(tokens, gain, weight, cosine, sine, q_gain, k_gain)


def per_device(sizes, tokens, norm_gain, qkv_weight, q_gain, k_gain, out_weight):
    n_row, n_col = sizes
    rows, width = tokens.shape
    half = rows // 2
    head_dim = q_gain.shape[0]
    tokens_full, gain_full, qkv_full = remote_call(
        entry_kernel, 1, 4 + PLANE + COLUMN + SMALL, 0,
        [(rows, n_col * width), (16, n_col * width), (n_row * qkv_weight.shape[0], qkv_weight.shape[1])],
        tokens, jnp.broadcast_to(norm_gain[None, :], (16, width)), qkv_weight,
    )
    here = Place()
    chunks = [here.chunk(which, here.x, here.z) for which in (0, 1)]
    within = jnp.arange(half, dtype=jnp.int32)
    positions = jnp.concatenate([chunk * half + within for chunk in chunks])
    freqs = jnp.power(
        jnp.float32(ROPE_BASE),
        -jnp.arange(head_dim // 2, dtype=jnp.float32) * 2.0 / head_dim,
    )
    angles = positions.astype(jnp.float32)[:, None] * freqs[None, :]
    cosine, sine = jnp.cos(angles), jnp.sin(angles)
    queries, keys, values = project(
        tokens_full,
        gain_full,
        qkv_full,
        jnp.concatenate([cosine, cosine], axis=1),
        jnp.concatenate([-sine, sine], axis=1),
        q_gain[None, :],
        k_gain[None, :],
    )
    attended = attention(head_dim ** (-0.5), n_row, queries, keys, values)
    attended_full, out_full = remote_call(
        heads_kernel, 3, 1 + PLANE + COLUMN, 1,
        [(rows, n_col * attended.shape[1]), (n_row * out_weight.shape[0], out_weight.shape[1])],
        attended, out_weight,
    )
    result = jnp.dot(attended_full, out_full, preferred_element_type=jnp.float32)
    (home,) = remote_call(
        exit_kernel, 4, 2, 0, [(rows, out_weight.shape[1])], result.astype(jnp.bfloat16)
    )
    return home


def solution(mesh):
    placed = (P("row", "col"), P("col"), P("row", "col"), P(), P(), P("row", "col"))
    return jax.shard_map(
        functools.partial(per_device, (mesh.shape["row"], mesh.shape["col"])),
        mesh=mesh,
        in_specs=placed,
        out_specs=P("row", "col"),
        check_vma=False,
    )
```

```python
import functools
import math

import jax
import jax.numpy as jnp
from jax import lax
from jax.experimental import pallas as pl
from jax.experimental.pallas import tpu as pltpu
from jax.sharding import PartitionSpec as P

D = 4096
GROUP = 4
EPSILON = 1e-06
ROPE_BASE = 1000000.0
MESH = pl.DeviceIdType.MESH


def ring(value, shift):
    return (value + shift + 4) % 4


class Place:
    def __init__(self):
        row, col = lax.axis_index("row"), lax.axis_index("col")
        self.z_lo, self.x, self.core = row // 8, (row // 2) % 4, row % 2
        self.y, self.z_hi = col // 2, col % 2
        self.z = 2 * self.z_hi + self.z_lo

    def device(self, **at):
        z = at.get("z", self.z)
        z_lo, z_hi = at.get("z_lo", z % 2), at.get("z_hi", z // 2)
        x, y, core = at.get("x", self.x), at.get("y", self.y), at.get("core", self.core)
        return {"row": 8 * z_lo + 2 * x + core, "col": 2 * y + z_hi}

    def step(self, axis, shift):
        return self.device(**{axis: ring(getattr(self, axis), shift)})

    def other_core(self):
        return self.device(core=1 - self.core)

    def turned(self):
        return self.device(core=self.z_hi, z_hi=self.core, z_lo=self.z_lo)

    def mirrored(self, bit):
        return self.z_lo + bit - 2 * bit * self.z_lo, self.x + bit * (3 - 2 * self.x)

    def chunk_to(self, half):
        z_lo, x = self.mirrored(self.core)
        return self.device(z_lo=z_lo, x=x, core=self.z_hi, z_hi=(self.core + half) % 2)

    def chunk_from(self, half):
        core = (self.z_hi + half) % 2
        z_lo, x = self.mirrored(core)
        return self.device(z_lo=z_lo, x=x, core=core, z_hi=self.core)

    def column(self, y=None, core=None):
        y = self.y if y is None else y
        return 2 * y + (self.core if core is None else core)

    def location(self, x, z):
        return 8 * (z % 2) + 2 * x + z // 2

    def chunk(self, half, x, z):
        first = 16 * (z % 2) + 4 * x + z // 2
        return first if half == 0 else 31 - first


class Net:
    def __init__(self, sent, landed, base=0):
        self.sent, self.landed, self.base, self.copies = sent, landed, base, []

    def send(self, ref, to, target=None):
        i = self.base + len(self.copies)
        copy = pltpu.make_async_remote_copy(
            src_ref=ref,
            dst_ref=ref if target is None else target,
            send_sem=self.sent.at[i],
            recv_sem=self.landed.at[i],
            device_id=to,
            device_id_type=MESH,
        )
        copy.start()
        self.copies.append(copy)
        return copy

    def send_built(self, build):
        copy = Built(self, self.base + len(self.copies), build)
        copy.copy().start()
        self.copies.append(copy)
        return copy

    def finish(self):
        for copy in self.copies:
            copy.wait_send()


class Built:
    def __init__(self, net, i, build):
        self.net, self.i, self.build = net, i, build

    def copy(self):
        ref, to, target = self.build()
        return pltpu.make_async_remote_copy(
            src_ref=ref,
            dst_ref=target,
            send_sem=self.net.sent.at[self.i],
            recv_sem=self.net.landed.at[self.i],
            device_id=to,
            device_id_type=MESH,
        )

    def wait_recv(self):
        self.copy().wait_recv()

    def wait_send(self):
        self.copy().wait_send()


def greet(partners):
    barrier = pltpu.get_barrier_semaphore()
    for partner in partners:
        pl.semaphore_signal(barrier, inc=1, device_id=partner, device_id_type=MESH)
    pl.semaphore_wait(barrier, len(partners))


def plane_gather(net, here, full, rows, spot, own=None):
    axes = (("x", "z"), ("z", "x"))
    piece = rows // 2

    def at(half, first, second):
        x = ring(here.x, first if half == 0 else second)
        z = ring(here.z, second if half == 0 else first)
        return pl.multiple_of(spot(half, x, z), rows)

    def block(half, first, second):
        return full[half].at[pl.ds(at(half, first, second), rows), :]

    def part(half, first, second, way):
        start = at(half, first, second) + (0 if way == 1 else piece)
        return full[half].at[pl.ds(pl.multiple_of(start, piece), piece), :]

    def whole(half, where, way, axis=1):
        def build():
            target = block(half, where, 0)
            source = own[half] if where == 0 and own is not None else target
            return source, here.step(axes[half][axis], way), target

        return net.send_built(build)

    def share(half, first, second, way, axis):
        def build():
            ref = part(half, first, second, way)
            return ref, here.step(axes[half][axis], way), ref

        return net.send_built(build)

    one, two, onward, last = {}, {}, {}, {}
    both = [(half, way) for half in (0, 1) for way in (1, -1)]
    for half, way in both:
        one[half, way] = whole(half, 0, way, 0)
    for half, way in both:
        two[half, 0, way] = whole(half, 0, way)
    yield
    for half, way in both:
        one[half, way].wait_recv()
        onward[half, way] = share(half, -way, 0, way, 0)
    for half, way in both:
        for turn in (1, -1):
            two[half, -way, turn] = whole(half, -way, turn)
    for half, way in both:
        two[half, 0, way].wait_recv()
        last[half, 0, way] = share(half, 0, -way, way, 1)
    yield
    for half, way in both:
        onward[half, way].wait_recv()
    for half, way in both:
        two[half, 2, way] = whole(half, 2, way)
    yield
    for where in (-1, 1):
        for half, way in both:
            two[half, where, way].wait_recv()
            last[half, where, way] = share(half, where, -way, way, 1)
    yield
    for half, way in both:
        last[half, 0, way].wait_recv()
    for half, way in both:
        two[half, 2, way].wait_recv()
        last[half, 2, way] = share(half, 2, -way, way, 1)
    yield
    for where in (-1, 1):
        for half, way in both:
            last[half, where, way].wait_recv()
    yield
    for half, way in both:
        last[half, 2, way].wait_recv()


def column_gather(net, here, part):
    far = {1: 0, -1: 1}
    near, onward, across = {}, {}, []
    for late in (0, 1):
        for way in (1, -1):
            which = far[way] if late == 0 else 1 - far[way]
            near[way, late] = net.send(part(here.y, which), here.step("y", way))
    across.append(net.send(part(here.y, 2), here.other_core()))
    yield
    for way in (1, -1):
        near[way, 0].wait_recv()
        onward[way] = net.send(part(ring(here.y, -way), far[way]), here.step("y", way))
    yield
    for way in (1, -1):
        near[way, 1].wait_recv()
        across.append(net.send(part(ring(here.y, -way), 2), here.other_core()))
    yield
    for way in (1, -1):
        onward[way].wait_recv()
        across.append(net.send(part(ring(here.y, 2), far[way]), here.other_core()))
    yield
    across[0].wait_recv()
    yield
    across[1].wait_recv()
    across[2].wait_recv()
    yield
    across[3].wait_recv()
    across[4].wait_recv()


def rows_of(rows, which):
    return slice(None) if which == 2 else slice(which * (rows // 2), (which + 1) * (rows // 2))


def together(*gathers):
    gathers = list(gathers)
    while gathers:
        for gather in list(gathers):
            if next(gather, gathers) is gathers:
                gathers.remove(gather)


def plane_partners(here):
    return [here.step(axis, way) for axis in ("x", "z") for way in (1, -1)]


def column_partners(here):
    return [here.step("y", 1), here.step("y", -1), here.other_core()]


def small_gather(net, here, full, width):
    def part(y):
        return full.at[:, pl.ds(pl.multiple_of(here.column(y) * width, width), width)]

    near = {way: net.send(part(here.y), here.step("y", way)) for way in (1, -1)}
    across = [net.send(part(here.y), here.other_core())]
    yield
    near[1].wait_recv()
    onward = net.send(part(ring(here.y, -1)), here.step("y", 1))
    near[-1].wait_recv()
    for way in (1, -1):
        across.append(net.send(part(ring(here.y, -way)), here.other_core()))
    yield
    onward.wait_recv()
    across.append(net.send(part(ring(here.y, 2)), here.other_core()))
    yield
    for copy in across:
        copy.wait_recv()


class Exchange:
    def __init__(self, moves, sent, landed, base=0):
        self.moves = []
        for i, (source, target, to, keep) in enumerate(moves, base):
            copy = pltpu.make_async_remote_copy(
                src_ref=source,
                dst_ref=target,
                send_sem=sent.at[i],
                recv_sem=landed.at[i],
                device_id=to,
                device_id_type=MESH,
            )
            local = pltpu.make_async_copy(source, target, landed.at[i])
            self.moves.append((copy, local, keep))
            if keep is None:
                copy.start()
            else:
                pl.when(keep)(local.start)
                pl.when(jnp.logical_not(keep))(copy.start)

    def wait(self, i):
        copy, local, keep = self.moves[i]
        if keep is None:
            copy.wait()
        else:
            pl.when(keep)(local.wait)
            pl.when(jnp.logical_not(keep))(copy.wait)


def weight_move(here, weight, full):
    depth = weight.shape[0]
    mine = pl.multiple_of((8 * here.z_lo + 2 * here.x + here.core) * depth, depth)
    return weight, full.at[pl.ds(mine, depth), :], here.turned(), here.core == here.z_hi


def weight_gather(net, here, full, depth):
    half = depth // 2
    return plane_gather(
        net, here, (full, full), half,
        lambda which, x, z: here.location(x, z) * depth + which * half,
    )


def entry_kernel(tokens, gain, weight, tokens_full, gain_full, weight_full, sent, landed):
    here = Place()
    half_rows, width = tokens.shape[0] // 2, tokens.shape[1]
    greet(
        plane_partners(here)
        + column_partners(here)
        + [here.turned()]
        + [here.chunk_to(half) for half in (0, 1)]
        + [here.chunk_from(half) for half in (0, 1)]
    )
    columns = pl.ds(pl.multiple_of((2 * here.y + here.z_hi) * width, width), width)
    rows_to = pl.ds(pl.multiple_of(here.core * half_rows, half_rows), half_rows)
    landing = tokens_full.at[rows_to, columns]
    stays = jnp.logical_and(here.core == 0, here.z_hi == 0)
    first = Exchange(
        [
            weight_move(here, weight, weight_full),
            (tokens.at[:half_rows, :], landing, here.chunk_to(0), stays),
            (tokens.at[half_rows:, :], landing, here.chunk_to(1), None),
            (gain, gain_full.at[:, columns], here.turned(), here.core == here.z_hi),
        ],
        sent,
        landed,
    )
    net = Net(sent, landed, 4)
    first.wait(0)
    weights = weight_gather(net, here, weight_full, weight.shape[0])
    next(weights)
    first.wait(1)
    first.wait(2)

    def part(y, which):
        start = pl.multiple_of(here.column(y) * width, width)
        return tokens_full.at[rows_of(2 * half_rows, which), pl.ds(start, width)]

    features = column_gather(net, here, part)
    next(features)
    first.wait(3)
    gains = small_gather(net, here, gain_full, width)
    together(features, weights, gains)
    net.finish()


PLANE, COLUMN, SMALL = 40, 11, 7


def remote_call(kernel, number, copies, kept, shapes, *operands):
    return pl.pallas_call(
        kernel,
        out_shape=[jax.ShapeDtypeStruct(shape, jnp.bfloat16) for shape in shapes],
        in_specs=[pl.BlockSpec(memory_space=pl.ANY)] * len(operands),
        out_specs=[pl.BlockSpec(memory_space=pl.ANY)] * len(shapes),
        scratch_shapes=[
            pltpu.SemaphoreType.DMA((copies,)),
            pltpu.SemaphoreType.DMA((copies,)),
        ]
        + ([pltpu.SemaphoreType.DMA((kept,))] if kept else []),
        compiler_params=pltpu.CompilerParams(collective_id=number, has_side_effects=True),
        name=kernel.__name__,
    )(*operands)


def attention_kernel(
    scale, q_hbm, k_hbm, v_hbm, weight, home,
    q_ref, k_ref, v_ref, keys, values, acc, top, heads, out_weight, total, result,
    sent, landed, kept,
):
    rows, head_dim = k_ref.shape
    half_rows = rows // 2
    here = Place()
    factor_log2 = scale * math.log2(math.e)
    loads = [
        pltpu.make_async_copy(source, target, kept.at[i])
        for i, (source, target) in enumerate(((k_hbm, k_ref), (v_hbm, v_ref), (q_hbm, q_ref)))
    ]
    for load in loads:
        load.start()
    greet(
        plane_partners(here)
        + column_partners(here)
        + [here.turned()]
        + [f(half) for f in (here.chunk_to, here.chunk_from) for half in (0, 1)]
    )
    net = Net(sent, landed, 3)
    arrivals = plane_gather(
        net, here, (keys, values), rows, lambda half, x, z: (4 * x + z) * rows, (k_hbm, v_hbm)
    )
    next(arrivals)
    acc[...] = jnp.zeros_like(acc)
    top[...] = jnp.full_like(top, -1e30)

    def unit(which, key_parts, value_parts, allowed=None, among=range(GROUP)):
        key_block = [ref[...] for ref in key_parts]
        value_block = [ref[...] for ref in value_parts]
        key_block = key_block[0] if len(key_block) == 1 else jnp.concatenate(key_block, axis=0)
        value_block = (
            value_block[0] if len(value_block) == 1 else jnp.concatenate(value_block, axis=0)
        )
        wide = jnp.concatenate([value_block, jnp.ones_like(value_block)], axis=1)
        asked = q_ref.at[pl.ds(pl.multiple_of(which * half_rows, half_rows), half_rows), :]

        def scores(h):
            return lax.dot_general(
                asked[:, h * head_dim : (h + 1) * head_dim],
                key_block,
                (((1,), (1,)), ((), ())),
                preferred_element_type=jnp.float32,
            )

        following = scores(among[0])
        for h in among:
            raw = following
            if h != among[-1]:
                following = scores(h + 1)
            if allowed is not None:
                raw = jnp.where(allowed, raw, -1e30)
            before = top[which, h]
            now = jnp.maximum(before, jnp.max(raw, axis=-1, keepdims=True))
            shift = now[:, :1] * factor_log2
            weights = jnp.exp2(raw * factor_log2 - shift).astype(jnp.bfloat16)
            fade = jnp.exp2((before - now) * factor_log2)
            added = jnp.dot(weights, wide, preferred_element_type=jnp.float32)
            acc[which, h] = acc[which, h] * jnp.concatenate([fade, fade], axis=1) + added
            top[which, h] = now

    low, high = here.z_lo, 1 - here.z_lo

    def low_chunk(x, z):
        chunk = here.chunk(0, x, z)
        return chunk + (z % 2) * (31 - 2 * chunk)

    def part(full, x, z, which):
        start = (4 * x + z) * rows + which * half_rows
        return full.at[pl.ds(pl.multiple_of(start, half_rows), half_rows), :]

    def at_once(places, among=range(GROUP)):
        spots = [(ring(here.x, dx), ring(here.z, dz)) for dx, dz in places]
        unit(
            high,
            [part(keys, x, z, z % 2) for x, z in spots],
            [part(values, x, z, z % 2) for x, z in spots],
            among=among,
        )
        for x, z in spots:
            before = (31 + low_chunk(here.x, here.z) - low_chunk(x, z)) // 32
            which = high + before * (low - high)
            theirs = 1 - z % 2 + before * (2 * (z % 2) - 1)
            unit(which, [part(keys, x, z, theirs)], [part(values, x, z, theirs)], among=among)

    def own(ref, which):
        return ref.at[pl.ds(pl.multiple_of(which * half_rows, half_rows), half_rows), :]

    for load in loads:
        load.wait()
    square = (half_rows, half_rows)
    allowed = lax.broadcasted_iota(jnp.int32, square, 1) <= lax.broadcasted_iota(
        jnp.int32, square, 0
    )
    unit(low, [own(k_ref, low)], [own(v_ref, low)], allowed)
    unit(high, [own(k_ref, high)], [own(v_ref, high)], allowed)
    unit(high, [own(k_ref, low)], [own(v_ref, low)])
    pairs = [
        ((1, 0), (3, 0)), ((0, 1), (0, 3)), ((1, 1), (1, 3)), ((3, 1), (3, 3)),
        ((2, 0), (0, 2)), ((2, 1), (2, 3)),
    ]
    steps = (0, 1, 2, 4, 5)

    tables = tuple(
        sum(pair[i][j] * 4**n for n, pair in enumerate(pairs)) for i in (0, 1) for j in (0, 1)
    )

    def stage(n, rest):
        for when in steps:
            pl.when(n == when)(lambda: next(arrivals) and None)
        digits = [r % 4 for r in rest]
        at_once([digits[:2], digits[2:]])
        return tuple(r // 4 for r in rest)

    lax.fori_loop(0, len(pairs), stage, tuple(jnp.int32(t) for t in tables))

    turn = Exchange([weight_move(here, weight, out_weight)], sent, landed)
    next(arrivals, None)
    spread, weights = [], None
    for h in range(GROUP):
        at_once([(1, 2), (3, 2)], [h])
        at_once([(2, 2)], [h])
        for which in (0, 1):
            heads[here.column() * GROUP + h, which * half_rows : (which + 1) * half_rows, :] = (
                acc[which, h, :, :head_dim] / acc[which, h, :, head_dim:]
            ).astype(heads.dtype)
        spread.append(
            column_gather(
                net, here,
                lambda y, which, h=h: heads.at[
                    here.column(y) * GROUP + h, rows_of(rows, which), :
                ],
            )
        )
        next(spread[h])
        if h == 1:
            turn.wait(0)
            weights = weight_gather(net, here, out_weight, weight.shape[0])
            next(weights)
    queue = [0, None, 1, 0, None, 2, 1, None, 3, 2, None, 3, 0, None, 1, 2, 3, None]
    for h in queue:
        next(weights if h is None else spread[h], None)

    span = 2 * GROUP * head_dim
    block = half_rows // 2

    def product(y, start):
        left = [
            heads[2 * GROUP * y + i, pl.ds(pl.multiple_of(start, block), block), :]
            for i in range(2 * GROUP)
        ]
        right = out_weight[pl.ds(pl.multiple_of(y * span, span), span), :]
        return jnp.dot(
            jnp.concatenate(left, axis=1), right, preferred_element_type=jnp.float32
        )

    for i, group in enumerate(((0,), (1, -1))):
        for h in range(GROUP):
            next(spread[h])
        for shift in group:

            @pl.loop(0, rows // block)
            def _(n):
                where = pl.ds(pl.multiple_of(n * block, block), block)
                added = product(ring(here.y, shift), n * block)
                total[where, :] = added if i == 0 else total[where, :] + added

    for h in range(GROUP):
        next(spread[h], None)
    last = []
    for half in (0, 1):
        slot = pl.multiple_of(((here.z_hi + half) % 2) * half_rows, half_rows)

        @pl.loop(0, half_rows // block)
        def _(n):
            start = slot + n * block
            where = pl.ds(pl.multiple_of(start, block), block)
            added = product(ring(here.y, 2), start)
            result[where, :] = (total[where, :] + added).astype(result.dtype)

        stays = jnp.logical_and(here.core == 0, here.z_hi == 0) if half == 0 else None
        last.append(
            Exchange(
                [
                    (
                        result.at[pl.ds(slot, half_rows), :],
                        home.at[half * half_rows : (half + 1) * half_rows, :],
                        here.chunk_from(half),
                        stays,
                    )
                ],
                sent, landed, 1 + half,
            )
        )
    for half in (0, 1):
        last[half].wait(0)
    net.finish()


def attention(scale, places, columns, queries, keys, values, weight):
    rows, width = queries.shape
    head_dim = keys.shape[1]
    copies = 3 + 2 * PLANE + GROUP * COLUMN
    bf16, f32 = jnp.bfloat16, jnp.float32
    return pl.pallas_call(
        functools.partial(attention_kernel, scale),
        out_shape=jax.ShapeDtypeStruct((rows, weight.shape[1]), bf16),
        in_specs=[pl.BlockSpec(memory_space=pl.ANY)] * 4,
        out_specs=pl.BlockSpec(memory_space=pl.ANY),
        scratch_shapes=[
            pltpu.VMEM(queries.shape, bf16),
            pltpu.VMEM(keys.shape, bf16),
            pltpu.VMEM(values.shape, bf16),
            pltpu.VMEM((places * rows, head_dim), bf16),
            pltpu.VMEM((places * rows, head_dim), bf16),
            pltpu.VMEM((2, GROUP, rows // 2, 2 * head_dim), f32),
            pltpu.VMEM((2, GROUP, rows // 2, head_dim), f32),
            pltpu.VMEM((columns * GROUP, rows, head_dim), bf16),
            pltpu.VMEM((places * weight.shape[0], weight.shape[1]), bf16),
            pltpu.VMEM((rows, weight.shape[1]), f32),
            pltpu.VMEM((rows, weight.shape[1]), bf16),
            pltpu.SemaphoreType.DMA((copies,)),
            pltpu.SemaphoreType.DMA((copies,)),
            pltpu.SemaphoreType.DMA((3,)),
        ],
        compiler_params=pltpu.CompilerParams(
            collective_id=2, has_side_effects=True, vmem_limit_bytes=48 * 1024 * 1024
        ),
        name="attention_kernel",
    )(queries, keys, values, weight)


def project_kernel(
    tokens, gain, weight, cosine, sine, q_gain, k_gain, q_ref, k_ref, v_ref
):
    rows, depth = tokens.shape
    head_dim = k_ref.shape[1]
    half = head_dim // 2
    step = 512
    spans = [slice(i, i + step) for i in range(0, depth, step)]
    squares = jnp.zeros((rows, 128), jnp.float32)
    for span in spans:
        part = tokens[:, span].astype(jnp.float32)
        part = part * part
        for i in range(0, step, 128):
            squares = squares + part[:, i : i + 128]
    inverse = lax.rsqrt(jnp.sum(squares, axis=1, keepdims=True) / depth + EPSILON)
    total = None
    for span in spans:
        part = tokens[:, span].astype(jnp.float32) * inverse
        part = (part * gain[:1, span].astype(jnp.float32)).astype(jnp.bfloat16)
        added = jnp.dot(part, weight[span, :], preferred_element_type=jnp.float32)
        total = added if total is None else total + added
    cos, sin = cosine[...], sine[...]

    def turned(slot, head_gain):
        u = total[:, slot * head_dim : (slot + 1) * head_dim]
        mean_sq = jnp.mean(u * u, axis=-1, keepdims=True)
        u = u * lax.rsqrt(mean_sq + EPSILON) * head_gain
        return (u * cos + pltpu.roll(u, half, 1) * sin).astype(jnp.bfloat16)

    for slot in range(GROUP):
        q_ref[:, slot * head_dim : (slot + 1) * head_dim] = turned(slot, q_gain[...])
    k_ref[...] = turned(GROUP, k_gain[...])
    v_ref[...] = total[:, (GROUP + 1) * head_dim :].astype(jnp.bfloat16)


def project(tokens, gain, weight, cosine, sine, q_gain, k_gain):
    rows, depth = tokens.shape
    head_dim = q_gain.shape[1]
    block = rows // 4

    def by_rows(width):
        return pl.BlockSpec((block, width), lambda i: (i, 0))

    def whole(array):
        return pl.BlockSpec(array.shape, lambda i: (0, 0), pipeline_mode=pl.Buffered(1))

    widths = [GROUP * head_dim, head_dim, head_dim]
    return pl.pallas_call(
        project_kernel,
        out_shape=[jax.ShapeDtypeStruct((rows, w), jnp.bfloat16) for w in widths],
        grid=(4,),
        in_specs=[
            by_rows(depth), whole(gain), whole(weight), by_rows(head_dim), by_rows(head_dim),
            whole(q_gain), whole(k_gain),
        ],
        out_specs=[by_rows(w) for w in widths],
        compiler_params=pltpu.CompilerParams(vmem_limit_bytes=40 * 1024 * 1024),
        name="project_kernel",
    )(tokens, gain, weight, cosine, sine, q_gain, k_gain)


def per_device(sizes, tokens, norm_gain, qkv_weight, q_gain, k_gain, out_weight):
    n_row, n_col = sizes
    rows, width = tokens.shape
    half = rows // 2
    head_dim = q_gain.shape[0]
    tokens_full, gain_full, qkv_full = remote_call(
        entry_kernel, 1, 4 + PLANE + COLUMN + SMALL, 0,
        [(rows, n_col * width), (16, n_col * width), (n_row * qkv_weight.shape[0], qkv_weight.shape[1])],
        tokens, jnp.broadcast_to(norm_gain[None, :], (16, width)), qkv_weight,
    )
    here = Place()
    chunks = [here.chunk(which, here.x, here.z) for which in (0, 1)]
    within = jnp.arange(half, dtype=jnp.int32)
    positions = jnp.concatenate([chunk * half + within for chunk in chunks])
    freqs = jnp.power(
        jnp.float32(ROPE_BASE),
        -jnp.arange(head_dim // 2, dtype=jnp.float32) * 2.0 / head_dim,
    )
    angles = positions.astype(jnp.float32)[:, None] * freqs[None, :]
    cosine, sine = jnp.cos(angles), jnp.sin(angles)
    queries, keys, values = project(
        tokens_full,
        gain_full,
        qkv_full,
        jnp.concatenate([cosine, cosine], axis=1),
        jnp.concatenate([-sine, sine], axis=1),
        q_gain[None, :],
        k_gain[None, :],
    )
    return attention(head_dim ** (-0.5), n_row, n_col, queries, keys, values, out_weight)


def solution(mesh):
    placed = (P("row", "col"), P("col"), P("row", "col"), P(), P(), P("row", "col"))
    return jax.shard_map(
        functools.partial(per_device, (mesh.shape["row"], mesh.shape["col"])),
        mesh=mesh,
        in_specs=placed,
        out_specs=P("row", "col"),
        check_vma=False,
    )
```

```python
import functools
import math

import jax
import jax.numpy as jnp
from jax import lax
from jax.experimental import pallas as pl
from jax.experimental.pallas import tpu as pltpu
from jax.sharding import PartitionSpec as P

D = 4096
GROUP = 4
EPSILON = 1e-06
ROPE_BASE = 1000000.0
MESH = pl.DeviceIdType.MESH


def ring(value, shift):
    return (value + shift + 4) % 4


class Place:
    def __init__(self):
        row, col = lax.axis_index("row"), lax.axis_index("col")
        self.z_lo, self.x, self.core = row // 8, (row // 2) % 4, row % 2
        self.y, self.z_hi = col // 2, col % 2
        self.z = 2 * self.z_hi + self.z_lo

    def device(self, **at):
        z = at.get("z", self.z)
        z_lo, z_hi = at.get("z_lo", z % 2), at.get("z_hi", z // 2)
        x, y, core = at.get("x", self.x), at.get("y", self.y), at.get("core", self.core)
        return {"row": 8 * z_lo + 2 * x + core, "col": 2 * y + z_hi}

    def step(self, axis, shift):
        return self.device(**{axis: ring(getattr(self, axis), shift)})

    def other_core(self):
        return self.device(core=1 - self.core)

    def turned(self):
        return self.device(core=self.z_hi, z_hi=self.core, z_lo=self.z_lo)

    def mirrored(self, bit):
        return self.z_lo + bit - 2 * bit * self.z_lo, self.x + bit * (3 - 2 * self.x)

    def chunk_to(self, half):
        z_lo, x = self.mirrored(self.core)
        return self.device(z_lo=z_lo, x=x, core=self.z_hi, z_hi=(self.core + half) % 2)

    def chunk_from(self, half):
        core = (self.z_hi + half) % 2
        z_lo, x = self.mirrored(core)
        return self.device(z_lo=z_lo, x=x, core=core, z_hi=self.core)

    def column(self, y=None, core=None):
        y = self.y if y is None else y
        return 2 * y + (self.core if core is None else core)

    def location(self, x, z):
        return 8 * (z % 2) + 2 * x + z // 2

    def chunk(self, half, x, z):
        first = 16 * (z % 2) + 4 * x + z // 2
        return first if half == 0 else 31 - first


class Net:
    def __init__(self, sent, landed, base=0):
        self.sent, self.landed, self.base, self.copies = sent, landed, base, []

    def send(self, ref, to, target=None):
        i = self.base + len(self.copies)
        copy = pltpu.make_async_remote_copy(
            src_ref=ref,
            dst_ref=ref if target is None else target,
            send_sem=self.sent.at[i],
            recv_sem=self.landed.at[i],
            device_id=to,
            device_id_type=MESH,
        )
        copy.start()
        self.copies.append(copy)
        return copy

    def send_built(self, build):
        copy = Built(self, self.base + len(self.copies), build)
        copy.copy().start()
        self.copies.append(copy)
        return copy

    def finish(self):
        for copy in self.copies:
            copy.wait_send()


class Built:
    def __init__(self, net, i, build):
        self.net, self.i, self.build = net, i, build

    def copy(self):
        ref, to, target = self.build()
        return pltpu.make_async_remote_copy(
            src_ref=ref,
            dst_ref=target,
            send_sem=self.net.sent.at[self.i],
            recv_sem=self.net.landed.at[self.i],
            device_id=to,
            device_id_type=MESH,
        )

    def wait_recv(self):
        self.copy().wait_recv()

    def wait_send(self):
        self.copy().wait_send()


def greet(partners):
    barrier = pltpu.get_barrier_semaphore()
    for partner in partners:
        pl.semaphore_signal(barrier, inc=1, device_id=partner, device_id_type=MESH)
    pl.semaphore_wait(barrier, len(partners))


def plane_gather(net, here, full, rows, spot, own=None):
    axes = (("x", "z"), ("z", "x"))
    piece = rows // 2

    def at(half, first, second):
        x = ring(here.x, first if half == 0 else second)
        z = ring(here.z, second if half == 0 else first)
        return pl.multiple_of(spot(half, x, z), rows)

    def block(half, first, second):
        return full[half].at[pl.ds(at(half, first, second), rows), :]

    def part(half, first, second, way):
        start = at(half, first, second) + (0 if way == 1 else piece)
        return full[half].at[pl.ds(pl.multiple_of(start, piece), piece), :]

    def whole(half, where, way, axis=1):
        def build():
            target = block(half, where, 0)
            source = own[half] if where == 0 and own is not None else target
            return source, here.step(axes[half][axis], way), target

        return net.send_built(build)

    def share(half, first, second, way, axis):
        def build():
            ref = part(half, first, second, way)
            return ref, here.step(axes[half][axis], way), ref

        return net.send_built(build)

    one, two, onward, last = {}, {}, {}, {}
    both = [(half, way) for half in (0, 1) for way in (1, -1)]
    for half, way in both:
        one[half, way] = whole(half, 0, way, 0)
    for half, way in both:
        two[half, 0, way] = whole(half, 0, way)
    yield
    for half, way in both:
        one[half, way].wait_recv()
        onward[half, way] = share(half, -way, 0, way, 0)
    for half, way in both:
        for turn in (1, -1):
            two[half, -way, turn] = whole(half, -way, turn)
    for half, way in both:
        two[half, 0, way].wait_recv()
        last[half, 0, way] = share(half, 0, -way, way, 1)
    yield
    for half, way in both:
        onward[half, way].wait_recv()
    for half, way in both:
        two[half, 2, way] = whole(half, 2, way)
    yield
    for where in (-1, 1):
        for half, way in both:
            two[half, where, way].wait_recv()
            last[half, where, way] = share(half, where, -way, way, 1)
    yield
    for half, way in both:
        last[half, 0, way].wait_recv()
    for half, way in both:
        two[half, 2, way].wait_recv()
        last[half, 2, way] = share(half, 2, -way, way, 1)
    yield
    for where in (-1, 1):
        for half, way in both:
            last[half, where, way].wait_recv()
    yield
    for half, way in both:
        last[half, 2, way].wait_recv()


def column_gather(net, here, part):
    far = {1: 0, -1: 1}
    near, onward, across = {}, {}, []
    for late in (0, 1):
        for way in (1, -1):
            which = far[way] if late == 0 else 1 - far[way]
            near[way, late] = net.send(part(here.y, which), here.step("y", way))
    across.append(net.send(part(here.y, 2), here.other_core()))
    yield
    for way in (1, -1):
        near[way, 0].wait_recv()
        onward[way] = net.send(part(ring(here.y, -way), far[way]), here.step("y", way))
    yield
    for way in (1, -1):
        near[way, 1].wait_recv()
        across.append(net.send(part(ring(here.y, -way), 2), here.other_core()))
    yield
    for way in (1, -1):
        onward[way].wait_recv()
        across.append(net.send(part(ring(here.y, 2), far[way]), here.other_core()))
    yield
    across[0].wait_recv()
    yield
    across[1].wait_recv()
    across[2].wait_recv()
    yield
    across[3].wait_recv()
    across[4].wait_recv()


def token_gather(net, here, part, arrived):
    near, onward, across = {}, {}, []
    for piece in (0, 1):
        arrived(piece)
        for way in (1, -1):
            near[way, piece] = net.send(part(here.y, piece), here.step("y", way))
        across.append(net.send(part(here.y, piece), here.other_core()))
        yield
    for piece in (0, 1):
        for way in (1, -1):
            near[way, piece].wait_recv()
            if (way, piece) in ((1, 0), (-1, 1)):
                onward[way] = net.send(part(ring(here.y, -way), piece), here.step("y", way))
            across.append(net.send(part(ring(here.y, -way), piece), here.other_core()))
        yield
    for way, piece in ((1, 0), (-1, 1)):
        onward[way].wait_recv()
        across.append(net.send(part(ring(here.y, 2), piece), here.other_core()))
    yield
    for copy in across:
        copy.wait_recv()


def rows_of(rows, which):
    return slice(None) if which == 2 else slice(which * (rows // 2), (which + 1) * (rows // 2))


def together(*gathers):
    gathers = list(gathers)
    while gathers:
        for gather in list(gathers):
            if next(gather, gathers) is gathers:
                gathers.remove(gather)


def plane_partners(here):
    return [here.step(axis, way) for axis in ("x", "z") for way in (1, -1)]


def column_partners(here):
    return [here.step("y", 1), here.step("y", -1), here.other_core()]


def small_gather(net, here, full, width):
    def part(y):
        return full.at[:, pl.ds(pl.multiple_of(here.column(y) * width, width), width)]

    near = {way: net.send(part(here.y), here.step("y", way)) for way in (1, -1)}
    across = [net.send(part(here.y), here.other_core())]
    yield
    near[1].wait_recv()
    onward = net.send(part(ring(here.y, -1)), here.step("y", 1))
    near[-1].wait_recv()
    for way in (1, -1):
        across.append(net.send(part(ring(here.y, -way)), here.other_core()))
    yield
    onward.wait_recv()
    across.append(net.send(part(ring(here.y, 2)), here.other_core()))
    yield
    for copy in across:
        copy.wait_recv()


class Exchange:
    def __init__(self, moves, sent, landed, base=0):
        self.moves = []
        for i, (source, target, to, keep) in enumerate(moves, base):
            copy = pltpu.make_async_remote_copy(
                src_ref=source,
                dst_ref=target,
                send_sem=sent.at[i],
                recv_sem=landed.at[i],
                device_id=to,
                device_id_type=MESH,
            )
            local = pltpu.make_async_copy(source, target, landed.at[i])
            self.moves.append((copy, local, keep))
            if keep is None:
                copy.start()
            else:
                pl.when(keep)(local.start)
                pl.when(jnp.logical_not(keep))(copy.start)

    def wait(self, i):
        copy, local, keep = self.moves[i]
        if keep is None:
            copy.wait()
        else:
            pl.when(keep)(local.wait)
            pl.when(jnp.logical_not(keep))(copy.wait)


def weight_move(here, weight, full):
    depth = weight.shape[0]
    mine = pl.multiple_of((8 * here.z_lo + 2 * here.x + here.core) * depth, depth)
    return weight, full.at[pl.ds(mine, depth), :], here.turned(), here.core == here.z_hi


def weight_gather(net, here, full, depth):
    half = depth // 2
    return plane_gather(
        net, here, (full, full), half,
        lambda which, x, z: here.location(x, z) * depth + which * half,
    )


PLANE, TOKEN, COLUMN, SMALL = 40, 14, 11, 7
SINGLE = 7


def layer_kernel(
    scale, tokens, gain, qkv_weight, weight, cosine, sine, q_gain, k_gain, home,
    tokens_full, gain_full, qkv_full, normed,
    q_ref, k_ref, v_ref, keys, values, acc, top, heads, out_weight, total, result,
    sent, landed,
):
    rows, head_dim = k_ref.shape
    half_rows = rows // 2
    width, depth = tokens.shape[1], tokens_full.shape[1]
    here = Place()
    factor_log2 = scale * math.log2(math.e)
    greet(
        plane_partners(here)
        + column_partners(here)
        + [here.turned()]
        + [f(half) for f in (here.chunk_to, here.chunk_from) for half in (0, 1)]
    )

    columns = pl.ds(pl.multiple_of((2 * here.y + here.z_hi) * width, width), width)
    rows_to = pl.ds(pl.multiple_of(here.core * half_rows, half_rows), half_rows)
    landing = tokens_full.at[rows_to, columns]
    stays = jnp.logical_and(here.core == 0, here.z_hi == 0)
    first = Exchange(
        [
            weight_move(here, qkv_weight, qkv_full),
            (tokens.at[:half_rows, :], landing, here.chunk_to(0), stays),
            (tokens.at[half_rows:, :], landing, here.chunk_to(1), None),
            (gain, gain_full.at[:, columns], here.turned(), here.core == here.z_hi),
        ],
        sent,
        landed,
    )
    net = Net(sent, landed, SINGLE)

    def token_part(y, piece):
        slot = pl.multiple_of(((here.z_hi + piece) % 2) * half_rows, half_rows)
        start = pl.multiple_of(here.column(y) * width, width)
        return tokens_full.at[pl.ds(slot, half_rows), pl.ds(start, width)]

    first.wait(0)
    weights = weight_gather(net, here, qkv_full, qkv_weight.shape[0])
    next(weights)
    features = token_gather(net, here, token_part, lambda piece: first.wait(1 + piece))
    next(features)
    next(features)
    first.wait(3)
    together(features, weights, small_gather(net, here, gain_full, width))

    step, span = 64, 512
    spans = [slice(i, i + span) for i in range(0, depth, span)]

    @pl.loop(0, rows // step)
    def _(n):
        where = pl.ds(pl.multiple_of(n * step, step), step)
        squares = jnp.zeros((step, 128), jnp.float32)
        for cut in spans:
            part = tokens_full[where, cut].astype(jnp.float32)
            part = part * part
            for i in range(0, span, 128):
                squares = squares + part[:, i : i + 128]
        inverse = lax.rsqrt(jnp.sum(squares, axis=1, keepdims=True) / depth + EPSILON)
        for cut in spans:
            part = tokens_full[where, cut].astype(jnp.float32) * inverse
            normed[where, cut] = (part * gain_full[:1, cut].astype(jnp.float32)).astype(
                normed.dtype
            )

    def turned(u, head_gain, where):
        mean_sq = jnp.mean(u * u, axis=-1, keepdims=True)
        u = u * lax.rsqrt(mean_sq + EPSILON) * head_gain
        turn = pltpu.roll(u, head_dim // 2, 1)
        return (u * cosine[where, :] + turn * sine[where, :]).astype(jnp.bfloat16)

    block = half_rows // 2
    q_width = GROUP * head_dim

    @pl.loop(0, rows // block)
    def _(n):
        where = pl.ds(pl.multiple_of(n * block, block), block)
        both = jnp.dot(
            normed[where, :], qkv_full[:, q_width:], preferred_element_type=jnp.float32
        )
        k_ref[where, :] = turned(both[:, :head_dim], k_gain[...], where)
        v_ref[where, :] = both[:, head_dim:].astype(v_ref.dtype)

    arrivals = plane_gather(
        net, here, (keys, values), rows, lambda half, x, z: (4 * x + z) * rows, (k_ref, v_ref)
    )
    next(arrivals)

    @pl.loop(0, rows // block)
    def _(n):
        where = pl.ds(pl.multiple_of(n * block, block), block)
        four = jnp.dot(
            normed[where, :], qkv_full[:, :q_width], preferred_element_type=jnp.float32
        )
        for h in range(GROUP):
            cut = slice(h * head_dim, (h + 1) * head_dim)
            q_ref[where, cut] = turned(four[:, cut], q_gain[...], where)

    acc[...] = jnp.zeros_like(acc)
    top[...] = jnp.full_like(top, -1e30)

    def unit(which, key_parts, value_parts, allowed=None, among=range(GROUP)):
        key_block = [ref[...] for ref in key_parts]
        value_block = [ref[...] for ref in value_parts]
        key_block = key_block[0] if len(key_block) == 1 else jnp.concatenate(key_block, axis=0)
        value_block = (
            value_block[0] if len(value_block) == 1 else jnp.concatenate(value_block, axis=0)
        )
        wide = jnp.concatenate([value_block, jnp.ones_like(value_block)], axis=1)
        asked = q_ref.at[pl.ds(pl.multiple_of(which * half_rows, half_rows), half_rows), :]

        def scores(h):
            return lax.dot_general(
                asked[:, h * head_dim : (h + 1) * head_dim],
                key_block,
                (((1,), (1,)), ((), ())),
                preferred_element_type=jnp.float32,
            )

        following = scores(among[0])
        for h in among:
            raw = following
            if h != among[-1]:
                following = scores(h + 1)
            if allowed is not None:
                raw = jnp.where(allowed, raw, -1e30)
            before = top[which, h]
            now = jnp.maximum(before, jnp.max(raw, axis=-1, keepdims=True))
            shift = now[:, :1] * factor_log2
            weights = jnp.exp2(raw * factor_log2 - shift).astype(jnp.bfloat16)
            fade = jnp.exp2((before - now) * factor_log2)
            added = jnp.dot(weights, wide, preferred_element_type=jnp.float32)
            acc[which, h] = acc[which, h] * jnp.concatenate([fade, fade], axis=1) + added
            top[which, h] = now

    low, high = here.z_lo, 1 - here.z_lo

    def low_chunk(x, z):
        chunk = here.chunk(0, x, z)
        return chunk + (z % 2) * (31 - 2 * chunk)

    def part(full, x, z, which):
        start = (4 * x + z) * rows + which * half_rows
        return full.at[pl.ds(pl.multiple_of(start, half_rows), half_rows), :]

    def at_once(places, among=range(GROUP)):
        spots = [(ring(here.x, dx), ring(here.z, dz)) for dx, dz in places]
        unit(
            high,
            [part(keys, x, z, z % 2) for x, z in spots],
            [part(values, x, z, z % 2) for x, z in spots],
            among=among,
        )
        for x, z in spots:
            before = (31 + low_chunk(here.x, here.z) - low_chunk(x, z)) // 32
            which = high + before * (low - high)
            theirs = 1 - z % 2 + before * (2 * (z % 2) - 1)
            unit(which, [part(keys, x, z, theirs)], [part(values, x, z, theirs)], among=among)

    def own(ref, which):
        return ref.at[pl.ds(pl.multiple_of(which * half_rows, half_rows), half_rows), :]

    square = (half_rows, half_rows)
    allowed = lax.broadcasted_iota(jnp.int32, square, 1) <= lax.broadcasted_iota(
        jnp.int32, square, 0
    )
    unit(low, [own(k_ref, low)], [own(v_ref, low)], allowed)
    unit(high, [own(k_ref, high)], [own(v_ref, high)], allowed)
    unit(high, [own(k_ref, low)], [own(v_ref, low)])
    pairs = [
        ((1, 0), (3, 0)), ((0, 1), (0, 3)), ((1, 1), (1, 3)), ((3, 1), (3, 3)),
        ((2, 0), (0, 2)), ((2, 1), (2, 3)),
    ]
    steps = (0, 1, 2, 4, 5)

    tables = tuple(
        sum(pair[i][j] * 4**n for n, pair in enumerate(pairs)) for i in (0, 1) for j in (0, 1)
    )

    def stage(n, rest):
        for when in steps:
            pl.when(n == when)(lambda: next(arrivals) and None)
        digits = [r % 4 for r in rest]
        at_once([digits[:2], digits[2:]])
        return tuple(r // 4 for r in rest)

    lax.fori_loop(0, len(pairs), stage, tuple(jnp.int32(t) for t in tables))

    turn = Exchange([weight_move(here, weight, out_weight)], sent, landed, 4)
    next(arrivals, None)
    spread, weights = [], None
    for h in range(GROUP):
        at_once([(1, 2), (3, 2)], [h])
        at_once([(2, 2)], [h])
        for which in (0, 1):
            heads[here.column() * GROUP + h, which * half_rows : (which + 1) * half_rows, :] = (
                acc[which, h, :, :head_dim] / acc[which, h, :, head_dim:]
            ).astype(heads.dtype)
        spread.append(
            column_gather(
                net, here,
                lambda y, which, h=h: heads.at[
                    here.column(y) * GROUP + h, rows_of(rows, which), :
                ],
            )
        )
        next(spread[h])
        if h == 1:
            turn.wait(0)
            weights = weight_gather(net, here, out_weight, weight.shape[0])
            next(weights)
    queue = [0, None, 1, 0, None, 2, 1, None, 3, 2, None, 3, 0, None, 1, 2, 3, None]
    for h in queue:
        next(weights if h is None else spread[h], None)

    span = 2 * GROUP * head_dim

    def product(y, start):
        left = [
            heads[2 * GROUP * y + i, pl.ds(pl.multiple_of(start, block), block), :]
            for i in range(2 * GROUP)
        ]
        right = out_weight[pl.ds(pl.multiple_of(y * span, span), span), :]
        return jnp.dot(
            jnp.concatenate(left, axis=1), right, preferred_element_type=jnp.float32
        )

    for i, group in enumerate(((0,), (1, -1))):
        for h in range(GROUP):
            next(spread[h])
        for shift in group:

            @pl.loop(0, rows // block)
            def _(n):
                where = pl.ds(pl.multiple_of(n * block, block), block)
                added = product(ring(here.y, shift), n * block)
                total[where, :] = added if i == 0 else total[where, :] + added

    for h in range(GROUP):
        next(spread[h], None)
    last = []
    for half in (0, 1):
        slot = pl.multiple_of(((here.z_hi + half) % 2) * half_rows, half_rows)

        @pl.loop(0, half_rows // block)
        def _(n):
            start = slot + n * block
            where = pl.ds(pl.multiple_of(start, block), block)
            added = product(ring(here.y, 2), start)
            result[where, :] = (total[where, :] + added).astype(result.dtype)

        stays = jnp.logical_and(here.core == 0, here.z_hi == 0) if half == 0 else None
        last.append(
            Exchange(
                [
                    (
                        result.at[pl.ds(slot, half_rows), :],
                        home.at[half * half_rows : (half + 1) * half_rows, :],
                        here.chunk_from(half),
                        stays,
                    )
                ],
                sent, landed, 5 + half,
            )
        )
    for half in (0, 1):
        last[half].wait(0)
    net.finish()


def per_device(sizes, tokens, norm_gain, qkv_weight, q_gain, k_gain, out_weight):
    n_row, n_col = sizes
    rows, width = tokens.shape
    half = rows // 2
    head_dim = q_gain.shape[0]
    here = Place()
    chunks = [here.chunk(which, here.x, here.z) for which in (0, 1)]
    within = jnp.arange(half, dtype=jnp.int32)
    positions = jnp.concatenate([chunk * half + within for chunk in chunks])
    freqs = jnp.power(
        jnp.float32(ROPE_BASE),
        -jnp.arange(head_dim // 2, dtype=jnp.float32) * 2.0 / head_dim,
    )
    angles = positions.astype(jnp.float32)[:, None] * freqs[None, :]
    cosine, sine = jnp.cos(angles), jnp.sin(angles)
    bf16, f32 = jnp.bfloat16, jnp.float32
    copies = SINGLE + 3 * PLANE + TOKEN + SMALL + GROUP * COLUMN
    q_width, out_width = GROUP * head_dim, out_weight.shape[1]
    return pl.pallas_call(
        functools.partial(layer_kernel, head_dim ** (-0.5)),
        out_shape=jax.ShapeDtypeStruct((rows, out_width), bf16),
        in_specs=[pl.BlockSpec(memory_space=pl.ANY)] * 4
        + [pl.BlockSpec(memory_space=pltpu.VMEM)] * 4,
        out_specs=pl.BlockSpec(memory_space=pl.ANY),
        scratch_shapes=[
            pltpu.VMEM((rows, n_col * width), bf16),
            pltpu.VMEM((16, n_col * width), bf16),
            pltpu.VMEM((n_row * qkv_weight.shape[0], qkv_weight.shape[1]), bf16),
            pltpu.VMEM((rows, n_col * width), bf16),
            pltpu.VMEM((rows, q_width), bf16),
            pltpu.VMEM((rows, head_dim), bf16),
            pltpu.VMEM((rows, head_dim), bf16),
            pltpu.VMEM((n_row * rows, head_dim), bf16),
            pltpu.VMEM((n_row * rows, head_dim), bf16),
            pltpu.VMEM((2, GROUP, half, 2 * head_dim), f32),
            pltpu.VMEM((2, GROUP, half, head_dim), f32),
            pltpu.VMEM((n_col * GROUP, rows, head_dim), bf16),
            pltpu.VMEM((n_row * out_weight.shape[0], out_width), bf16),
            pltpu.VMEM((rows, out_width), f32),
            pltpu.VMEM((rows, out_width), bf16),
            pltpu.SemaphoreType.DMA((copies,)),
            pltpu.SemaphoreType.DMA((copies,)),
        ],
        compiler_params=pltpu.CompilerParams(
            collective_id=1, has_side_effects=True, vmem_limit_bytes=60 * 1024 * 1024
        ),
        name="layer_kernel",
    )(
        tokens,
        jnp.broadcast_to(norm_gain[None, :], (16, width)),
        qkv_weight,
        out_weight,
        jnp.concatenate([cosine, cosine], axis=1),
        jnp.concatenate([-sine, sine], axis=1),
        q_gain[None, :],
        k_gain[None, :],
    )


def solution(mesh):
    placed = (P("row", "col"), P("col"), P("row", "col"), P(), P(), P("row", "col"))
    return jax.shard_map(
        functools.partial(per_device, (mesh.shape["row"], mesh.shape["col"])),
        mesh=mesh,
        in_specs=placed,
        out_specs=P("row", "col"),
        check_vma=False,
    )
```

```python
import functools
import math

import jax
import jax.numpy as jnp
from jax import lax
from jax.experimental import pallas as pl
from jax.experimental.pallas import tpu as pltpu
from jax.sharding import PartitionSpec as P

D = 4096
GROUP = 4
EPSILON = 1e-06
ROPE_BASE = 1000000.0
MESH = pl.DeviceIdType.MESH


def ring(value, shift):
    return (value + shift + 4) % 4


class Place:
    def __init__(self):
        row, col = lax.axis_index("row"), lax.axis_index("col")
        self.z_lo, self.x, self.core = row // 8, (row // 2) % 4, row % 2
        self.y, self.z_hi = col // 2, col % 2
        self.z = 2 * self.z_hi + self.z_lo

    def device(self, **at):
        z = at.get("z", self.z)
        z_lo, z_hi = at.get("z_lo", z % 2), at.get("z_hi", z // 2)
        x, y, core = at.get("x", self.x), at.get("y", self.y), at.get("core", self.core)
        return {"row": 8 * z_lo + 2 * x + core, "col": 2 * y + z_hi}

    def step(self, axis, shift):
        return self.device(**{axis: ring(getattr(self, axis), shift)})

    def other_core(self):
        return self.device(core=1 - self.core)

    def turned(self):
        return self.device(core=self.z_hi, z_hi=self.core, z_lo=self.z_lo)

    def mirrored(self, bit):
        return self.z_lo + bit - 2 * bit * self.z_lo, self.x + bit * (3 - 2 * self.x)

    def chunk_to(self, half):
        z_lo, x = self.mirrored(self.core)
        return self.device(z_lo=z_lo, x=x, core=self.z_hi, z_hi=(self.core + half) % 2)

    def chunk_from(self, half):
        core = (self.z_hi + half) % 2
        z_lo, x = self.mirrored(core)
        return self.device(z_lo=z_lo, x=x, core=core, z_hi=self.core)

    def column(self, y=None, core=None):
        y = self.y if y is None else y
        return 2 * y + (self.core if core is None else core)

    def location(self, x, z):
        return 8 * (z % 2) + 2 * x + z // 2

    def chunk(self, half, x, z):
        first = 16 * (z % 2) + 4 * x + z // 2
        return first if half == 0 else 31 - first


class Net:
    def __init__(self, sent, landed, base=0):
        self.sent, self.landed, self.base, self.copies = sent, landed, base, []

    def send(self, ref, to, target=None):
        i = self.base + len(self.copies)
        copy = pltpu.make_async_remote_copy(
            src_ref=ref,
            dst_ref=ref if target is None else target,
            send_sem=self.sent.at[i],
            recv_sem=self.landed.at[i],
            device_id=to,
            device_id_type=MESH,
        )
        copy.start()
        self.copies.append(copy)
        return copy

    def send_built(self, build):
        copy = Built(self, self.base + len(self.copies), build)
        copy.copy().start()
        self.copies.append(copy)
        return copy

    def finish(self):
        for copy in self.copies:
            copy.wait_send()


class Built:
    def __init__(self, net, i, build):
        self.net, self.i, self.build = net, i, build

    def copy(self):
        ref, to, target = self.build()
        return pltpu.make_async_remote_copy(
            src_ref=ref,
            dst_ref=target,
            send_sem=self.net.sent.at[self.i],
            recv_sem=self.net.landed.at[self.i],
            device_id=to,
            device_id_type=MESH,
        )

    def wait_recv(self):
        self.copy().wait_recv()

    def wait_send(self):
        self.copy().wait_send()


def greet(partners):
    barrier = pltpu.get_barrier_semaphore()
    for partner in partners:
        pl.semaphore_signal(barrier, inc=1, device_id=partner, device_id_type=MESH)
    pl.semaphore_wait(barrier, len(partners))


def plane_gather(net, here, full, rows, spot, own=None):
    axes = (("x", "z"), ("z", "x"))
    piece = rows // 2

    def at(half, first, second):
        x = ring(here.x, first if half == 0 else second)
        z = ring(here.z, second if half == 0 else first)
        return pl.multiple_of(spot(half, x, z), rows)

    def block(half, first, second):
        return full[half].at[pl.ds(at(half, first, second), rows), :]

    def part(half, first, second, way):
        start = at(half, first, second) + (0 if way == 1 else piece)
        return full[half].at[pl.ds(pl.multiple_of(start, piece), piece), :]

    def whole(half, where, way, axis=1):
        def build():
            target = block(half, where, 0)
            source = own[half] if where == 0 and own is not None else target
            return source, here.step(axes[half][axis], way), target

        return net.send_built(build)

    def share(half, first, second, way, axis):
        def build():
            ref = part(half, first, second, way)
            return ref, here.step(axes[half][axis], way), ref

        return net.send_built(build)

    one, two, onward, last = {}, {}, {}, {}
    both = [(half, way) for half in (0, 1) for way in (1, -1)]
    for half, way in both:
        one[half, way] = whole(half, 0, way, 0)
    for half, way in both:
        two[half, 0, way] = whole(half, 0, way)
    yield
    for half, way in both:
        one[half, way].wait_recv()
        onward[half, way] = share(half, -way, 0, way, 0)
    for half, way in both:
        for turn in (1, -1):
            two[half, -way, turn] = whole(half, -way, turn)
    for half, way in both:
        two[half, 0, way].wait_recv()
        last[half, 0, way] = share(half, 0, -way, way, 1)
    yield
    for half, way in both:
        onward[half, way].wait_recv()
    for half, way in both:
        two[half, 2, way] = whole(half, 2, way)
    yield
    for where in (-1, 1):
        for half, way in both:
            two[half, where, way].wait_recv()
            last[half, where, way] = share(half, where, -way, way, 1)
    yield
    for half, way in both:
        last[half, 0, way].wait_recv()
    for half, way in both:
        two[half, 2, way].wait_recv()
        last[half, 2, way] = share(half, 2, -way, way, 1)
    yield
    for where in (-1, 1):
        for half, way in both:
            last[half, where, way].wait_recv()
    yield
    for half, way in both:
        last[half, 2, way].wait_recv()


def column_gather(net, here, part):
    far = {1: 0, -1: 1}
    near, onward, across = {}, {}, []
    for late in (0, 1):
        for way in (1, -1):
            which = far[way] if late == 0 else 1 - far[way]
            near[way, late] = net.send(part(here.y, which), here.step("y", way))
    across.append(net.send(part(here.y, 2), here.other_core()))
    yield
    for way in (1, -1):
        near[way, 0].wait_recv()
        onward[way] = net.send(part(ring(here.y, -way), far[way]), here.step("y", way))
    yield
    for way in (1, -1):
        near[way, 1].wait_recv()
        across.append(net.send(part(ring(here.y, -way), 2), here.other_core()))
    yield
    for copy in across[:3]:
        copy.wait_recv()
    yield
    for way in (1, -1):
        onward[way].wait_recv()
        across.append(net.send(part(ring(here.y, 2), far[way]), here.other_core()))
    yield
    for copy in across[3:]:
        copy.wait_recv()


def token_gather(net, here, part, arrived):
    near, onward, across = {}, {}, []
    for piece in (0, 1):
        arrived(piece)
        for way in (1, -1):
            near[way, piece] = net.send(part(here.y, piece), here.step("y", way))
        across.append(net.send(part(here.y, piece), here.other_core()))
        yield
    for piece in (0, 1):
        for way in (1, -1):
            near[way, piece].wait_recv()
            if (way, piece) in ((1, 0), (-1, 1)):
                onward[way] = net.send(part(ring(here.y, -way), piece), here.step("y", way))
            across.append(net.send(part(ring(here.y, -way), piece), here.other_core()))
        yield
    for way, piece in ((1, 0), (-1, 1)):
        onward[way].wait_recv()
        across.append(net.send(part(ring(here.y, 2), piece), here.other_core()))
    yield
    for copy in across:
        copy.wait_recv()


def rows_of(rows, which):
    return slice(None) if which == 2 else slice(which * (rows // 2), (which + 1) * (rows // 2))


def together(*gathers):
    gathers = list(gathers)
    while gathers:
        for gather in list(gathers):
            if next(gather, gathers) is gathers:
                gathers.remove(gather)


def plane_partners(here):
    return [here.step(axis, way) for axis in ("x", "z") for way in (1, -1)]


def column_partners(here):
    return [here.step("y", 1), here.step("y", -1), here.other_core()]


def small_gather(net, here, full, width):
    def part(y):
        return full.at[:, pl.ds(pl.multiple_of(here.column(y) * width, width), width)]

    near = {way: net.send(part(here.y), here.step("y", way)) for way in (1, -1)}
    across = [net.send(part(here.y), here.other_core())]
    yield
    near[1].wait_recv()
    onward = net.send(part(ring(here.y, -1)), here.step("y", 1))
    near[-1].wait_recv()
    for way in (1, -1):
        across.append(net.send(part(ring(here.y, -way)), here.other_core()))
    yield
    onward.wait_recv()
    across.append(net.send(part(ring(here.y, 2)), here.other_core()))
    yield
    for copy in across:
        copy.wait_recv()


class Exchange:
    def __init__(self, moves, sent, landed, base=0):
        self.moves = []
        for n, (source, target, to, keep) in enumerate(moves):
            i = base + n
            copy = pltpu.make_async_remote_copy(
                src_ref=source,
                dst_ref=target,
                send_sem=sent.at[i],
                recv_sem=landed.at[i],
                device_id=to,
                device_id_type=MESH,
            )
            local = pltpu.make_async_copy(source, target, landed.at[i])
            self.moves.append((copy, local, keep))
            if keep is None:
                copy.start()
            else:
                pl.when(keep)(local.start)
                pl.when(jnp.logical_not(keep))(copy.start)

    def wait(self, i):
        copy, local, keep = self.moves[i]
        if keep is None:
            copy.wait()
        else:
            pl.when(keep)(local.wait)
            pl.when(jnp.logical_not(keep))(copy.wait)


def weight_move(here, weight, full):
    depth = weight.shape[0]
    mine = pl.multiple_of((8 * here.z_lo + 2 * here.x + here.core) * depth, depth)
    return weight, full.at[pl.ds(mine, depth), :], here.turned(), here.core == here.z_hi


def weight_gather(net, here, full, depth):
    half = depth // 2
    return plane_gather(
        net, here, (full, full), half,
        lambda which, x, z: here.location(x, z) * depth + which * half,
    )


PLANE, TOKEN, COLUMN, SMALL = 40, 14, 11, 7
SINGLE = 8


def layer_kernel(
    scale, tokens, gain, qkv_weight, weight, cosine, sine, q_gain, k_gain, home,
    tokens_full, gain_full, q_weight, kv_weight, normed,
    q_ref, k_ref, v_ref, keys, values, acc, top, heads, out_weight, total, result,
    sent, landed,
):
    rows, head_dim = k_ref.shape
    half_rows = rows // 2
    width, depth = tokens.shape[1], tokens_full.shape[1]
    q_width = GROUP * head_dim
    here = Place()
    factor_log2 = scale * math.log2(math.e)
    greet(
        plane_partners(here)
        + column_partners(here)
        + [here.turned()]
        + [f(half) for f in (here.chunk_to, here.chunk_from) for half in (0, 1)]
    )

    columns = pl.ds(pl.multiple_of((2 * here.y + here.z_hi) * width, width), width)
    rows_to = pl.ds(pl.multiple_of(here.core * half_rows, half_rows), half_rows)
    landing = tokens_full.at[rows_to, columns]
    stays = jnp.logical_and(here.core == 0, here.z_hi == 0)
    first = Exchange(
        [
            weight_move(here, qkv_weight.at[:, q_width:], kv_weight),
            (tokens.at[:half_rows, :], landing, here.chunk_to(0), stays),
            (tokens.at[half_rows:, :], landing, here.chunk_to(1), None),
            (gain, gain_full.at[:, columns], here.turned(), here.core == here.z_hi),
        ],
        sent,
        landed,
    )
    net = Net(sent, landed, SINGLE)

    def token_part(y, piece):
        slot = pl.multiple_of(((here.z_hi + piece) % 2) * half_rows, half_rows)
        start = pl.multiple_of(here.column(y) * width, width)
        return tokens_full.at[pl.ds(slot, half_rows), pl.ds(start, width)]

    first.wait(0)
    kv_side = weight_gather(net, here, kv_weight, qkv_weight.shape[0])
    next(kv_side)
    features = token_gather(net, here, token_part, lambda piece: first.wait(1 + piece))
    next(features)
    next(features)
    turn = Exchange([weight_move(here, qkv_weight.at[:, :q_width], q_weight)], sent, landed, 7)
    next(kv_side)
    first.wait(3)
    gains = small_gather(net, here, gain_full, width)
    next(gains)
    next(kv_side)
    turn.wait(0)
    q_side = weight_gather(net, here, q_weight, qkv_weight.shape[0])
    next(q_side)
    next(features)
    next(kv_side)
    next(features)
    next(q_side)
    turn = Exchange([weight_move(here, weight, out_weight)], sent, landed, 4)
    next(kv_side)
    next(gains)
    next(features)
    next(q_side)
    together(kv_side, gains)
    next(q_side)
    next(features, None)

    step, span = 64, 512
    spans = [slice(i, i + span) for i in range(0, depth, span)]

    @pl.loop(0, rows // step)
    def _(n):
        where = pl.ds(pl.multiple_of(n * step, step), step)
        squares = jnp.zeros((step, 128), jnp.float32)
        for cut in spans:
            part = tokens_full[where, cut].astype(jnp.float32)
            part = part * part
            for i in range(0, span, 128):
                squares = squares + part[:, i : i + 128]
        inverse = lax.rsqrt(jnp.sum(squares, axis=1, keepdims=True) / depth + EPSILON)
        for cut in spans:
            part = tokens_full[where, cut].astype(jnp.float32) * inverse
            normed[where, cut] = (part * gain_full[:1, cut].astype(jnp.float32)).astype(
                normed.dtype
            )

    next(q_side)

    def turned(u, head_gain, where):
        mean_sq = jnp.mean(u * u, axis=-1, keepdims=True)
        u = u * lax.rsqrt(mean_sq + EPSILON) * head_gain
        turn = pltpu.roll(u, head_dim // 2, 1)
        return (u * cosine[where, :] + turn * sine[where, :]).astype(jnp.bfloat16)

    block = half_rows // 2

    @pl.loop(0, rows // block)
    def _(n):
        where = pl.ds(pl.multiple_of(n * block, block), block)
        both = jnp.dot(
            normed[where, :], kv_weight[...], preferred_element_type=jnp.float32
        )
        k_ref[where, :] = turned(both[:, :head_dim], k_gain[...], where)
        v_ref[where, :] = both[:, head_dim:].astype(v_ref.dtype)

    arrivals = plane_gather(
        net, here, (keys, values), rows, lambda half, x, z: (4 * x + z) * rows, (k_ref, v_ref)
    )
    next(arrivals)
    together(q_side)

    @pl.loop(0, rows // block)
    def _(n):
        where = pl.ds(pl.multiple_of(n * block, block), block)
        four = jnp.dot(
            normed[where, :], q_weight[...], preferred_element_type=jnp.float32
        )
        for h in range(GROUP):
            cut = slice(h * head_dim, (h + 1) * head_dim)
            q_ref[where, cut] = turned(four[:, cut], q_gain[...], where)

    acc[...] = jnp.zeros_like(acc)
    top[...] = jnp.full_like(top, -1e30)

    def unit(which, key_parts, value_parts, allowed=None):
        key_block = [ref[...] for ref in key_parts]
        value_block = [ref[...] for ref in value_parts]
        key_block = key_block[0] if len(key_block) == 1 else jnp.concatenate(key_block, axis=0)
        value_block = (
            value_block[0] if len(value_block) == 1 else jnp.concatenate(value_block, axis=0)
        )
        wide = jnp.concatenate([value_block, jnp.ones_like(value_block)], axis=1)
        asked = q_ref.at[pl.ds(pl.multiple_of(which * half_rows, half_rows), half_rows), :]

        def scores(h):
            return lax.dot_general(
                asked[:, h * head_dim : (h + 1) * head_dim],
                key_block,
                (((1,), (1,)), ((), ())),
                preferred_element_type=jnp.float32,
            )

        following = scores(0)
        for h in range(GROUP):
            raw = following
            if h + 1 < GROUP:
                following = scores(h + 1)
            if allowed is not None:
                raw = jnp.where(allowed, raw, -1e30)
            before = top[which, h]
            now = jnp.maximum(before, jnp.max(raw, axis=-1, keepdims=True))
            shift = now[:, :1] * factor_log2
            weights = jnp.exp2(raw * factor_log2 - shift).astype(jnp.bfloat16)
            fade = jnp.exp2((before - now) * factor_log2)
            added = jnp.dot(weights, wide, preferred_element_type=jnp.float32)
            acc[which, h] = acc[which, h] * jnp.concatenate([fade, fade], axis=1) + added
            top[which, h] = now

    low, high = here.z_lo, 1 - here.z_lo

    def low_chunk(x, z):
        chunk = here.chunk(0, x, z)
        return chunk + (z % 2) * (31 - 2 * chunk)

    def part(full, x, z, which):
        start = (4 * x + z) * rows + which * half_rows
        return full.at[pl.ds(pl.multiple_of(start, half_rows), half_rows), :]

    def spots_of(places):
        return [(ring(here.x, dx), ring(here.z, dz)) for dx, dz in places]

    def their_low(places):
        spots = spots_of(places)
        unit(
            high,
            [part(keys, x, z, z % 2) for x, z in spots],
            [part(values, x, z, z % 2) for x, z in spots],
        )

    def their_other(places):
        for x, z in spots_of(places):
            before = (31 + low_chunk(here.x, here.z) - low_chunk(x, z)) // 32
            which = high + before * (low - high)
            theirs = 1 - z % 2 + before * (2 * (z % 2) - 1)
            unit(which, [part(keys, x, z, theirs)], [part(values, x, z, theirs)])

    def own(ref, which):
        return ref.at[pl.ds(pl.multiple_of(which * half_rows, half_rows), half_rows), :]

    square = (half_rows, half_rows)
    allowed = lax.broadcasted_iota(jnp.int32, square, 1) <= lax.broadcasted_iota(
        jnp.int32, square, 0
    )
    unit(low, [own(k_ref, low)], [own(v_ref, low)], allowed)
    unit(high, [own(k_ref, high)], [own(v_ref, high)], allowed)
    unit(high, [own(k_ref, low)], [own(v_ref, low)])
    pairs = [
        ((1, 0), (3, 0)), ((0, 1), (0, 3)), ((1, 1), (1, 3)), ((3, 1), (3, 3)),
        ((2, 0), (0, 2)), ((2, 1), (2, 3)),
    ]
    steps = (0, 1, 2, 4, 5)

    tables = tuple(
        sum(pair[i][j] * 4**n for n, pair in enumerate(pairs)) for i in (0, 1) for j in (0, 1)
    )

    def stage(n, rest):
        for when in steps:
            pl.when(n == when)(lambda: next(arrivals) and None)
        digits = [r % 4 for r in rest]
        their_low([digits[:2], digits[2:]])
        their_other([digits[:2], digits[2:]])
        return tuple(r // 4 for r in rest)

    turn.wait(0)
    out_side = weight_gather(net, here, out_weight, weight.shape[0])
    next(out_side)
    lax.fori_loop(0, len(pairs), stage, tuple(jnp.int32(t) for t in tables))

    next(arrivals, None)
    rest = [(1, 2), (3, 2), (2, 2)]

    def leave(which):
        where = pl.ds(pl.multiple_of(which * half_rows, half_rows), half_rows)
        for h in range(GROUP):
            heads[here.column() * GROUP + h, where, :] = (
                acc[which, h, :, :head_dim] / acc[which, h, :, head_dim:]
            ).astype(heads.dtype)

        def group(y, piece):
            first_head, count = (0, GROUP) if piece == 2 else (piece * (GROUP // 2), GROUP // 2)
            return heads.at[pl.ds(here.column(y) * GROUP + first_head, count), where, :]

        gather = column_gather(net, here, group)
        next(gather)
        return gather

    their_other(rest)
    early = leave(low)
    their_low(rest)
    late = leave(high)
    for side in (
        early, out_side, early, out_side, late, early, early, out_side, late, out_side,
        out_side, out_side, early,
    ):
        next(side, None)

    span = 2 * GROUP * head_dim

    def product(y, start):
        left = [
            heads[2 * GROUP * y + i, pl.ds(pl.multiple_of(start, block), block), :]
            for i in range(2 * GROUP)
        ]
        right = out_weight[pl.ds(pl.multiple_of(y * span, span), span), :]
        return jnp.dot(
            jnp.concatenate(left, axis=1), right, preferred_element_type=jnp.float32
        )

    def multiply(which, shifts, opens, closes):
        @pl.loop(0, half_rows // block)
        def _(n):
            start = which * half_rows + n * block
            where = pl.ds(pl.multiple_of(start, block), block)

            @pl.loop(0, len(shifts))
            def _(i):
                added = product(ring(here.y, shifts[0] + i), start)
                if opens:
                    pl.when(i == 0)(lambda: total.__setitem__((where, slice(None)), added))
                    pl.when(i > 0)(
                        lambda: total.__setitem__(
                            (where, slice(None)), total[where, :] + added
                        )
                    )
                else:
                    total[where, :] = total[where, :] + added

            if closes:
                result[where, :] = total[where, :].astype(result.dtype)

    def go_home(which):
        half = (which + here.z_hi) % 2
        return Exchange(
            [
                (
                    result.at[
                        pl.ds(pl.multiple_of(which * half_rows, half_rows), half_rows), :
                    ],
                    home.at[pl.ds(pl.multiple_of(half * half_rows, half_rows), half_rows), :],
                    here.chunk_from(half),
                    (1 - here.core) * (1 - here.z_hi) * (1 - half) == 1,
                )
            ],
            sent, landed, 5 + half,
        )

    multiply(low, (-1, 0, 1, 2), True, True)
    first_home = go_home(low)
    next(late)
    multiply(high, (-1, 0, 1), True, False)
    next(late)
    next(late, None)
    multiply(high, (2,), False, True)
    second_home = go_home(high)
    first_home.wait(0)
    second_home.wait(0)
    net.finish()


def per_device(sizes, tokens, norm_gain, qkv_weight, q_gain, k_gain, out_weight):
    n_row, n_col = sizes
    rows, width = tokens.shape
    half = rows // 2
    head_dim = q_gain.shape[0]
    here = Place()
    chunks = [here.chunk(which, here.x, here.z) for which in (0, 1)]
    within = jnp.arange(half, dtype=jnp.int32)
    positions = jnp.concatenate([chunk * half + within for chunk in chunks])
    freqs = jnp.power(
        jnp.float32(ROPE_BASE),
        -jnp.arange(head_dim // 2, dtype=jnp.float32) * 2.0 / head_dim,
    )
    angles = positions.astype(jnp.float32)[:, None] * freqs[None, :]
    cosine, sine = jnp.cos(angles), jnp.sin(angles)
    bf16, f32 = jnp.bfloat16, jnp.float32
    copies = SINGLE + 4 * PLANE + TOKEN + SMALL + 2 * COLUMN
    q_width, out_width = GROUP * head_dim, out_weight.shape[1]
    return pl.pallas_call(
        functools.partial(layer_kernel, head_dim ** (-0.5)),
        out_shape=jax.ShapeDtypeStruct((rows, out_width), bf16),
        in_specs=[pl.BlockSpec(memory_space=pl.ANY)] * 4
        + [pl.BlockSpec(memory_space=pltpu.VMEM)] * 4,
        out_specs=pl.BlockSpec(memory_space=pl.ANY),
        scratch_shapes=[
            pltpu.VMEM((rows, n_col * width), bf16),
            pltpu.VMEM((16, n_col * width), bf16),
            pltpu.VMEM((n_row * qkv_weight.shape[0], q_width), bf16),
            pltpu.VMEM((n_row * qkv_weight.shape[0], qkv_weight.shape[1] - q_width), bf16),
            pltpu.VMEM((rows, n_col * width), bf16),
            pltpu.VMEM((rows, q_width), bf16),
            pltpu.VMEM((rows, head_dim), bf16),
            pltpu.VMEM((rows, head_dim), bf16),
            pltpu.VMEM((n_row * rows, head_dim), bf16),
            pltpu.VMEM((n_row * rows, head_dim), bf16),
            pltpu.VMEM((2, GROUP, half, 2 * head_dim), f32),
            pltpu.VMEM((2, GROUP, half, head_dim), f32),
            pltpu.VMEM((n_col * GROUP, rows, head_dim), bf16),
            pltpu.VMEM((n_row * out_weight.shape[0], out_width), bf16),
            pltpu.VMEM((rows, out_width), f32),
            pltpu.VMEM((rows, out_width), bf16),
            pltpu.SemaphoreType.DMA((copies,)),
            pltpu.SemaphoreType.DMA((copies,)),
        ],
        compiler_params=pltpu.CompilerParams(
            collective_id=1, has_side_effects=True, vmem_limit_bytes=60 * 1024 * 1024
        ),
        name="layer_kernel",
    )(
        tokens,
        jnp.broadcast_to(norm_gain[None, :], (16, width)),
        qkv_weight,
        out_weight,
        jnp.concatenate([cosine, cosine], axis=1),
        jnp.concatenate([-sine, sine], axis=1),
        q_gain[None, :],
        k_gain[None, :],
    )


def solution(mesh):
    placed = (P("row", "col"), P("col"), P("row", "col"), P(), P(), P("row", "col"))
    return jax.shard_map(
        functools.partial(per_device, (mesh.shape["row"], mesh.shape["col"])),
        mesh=mesh,
        in_specs=placed,
        out_specs=P("row", "col"),
        check_vma=False,
    )
```

```python
import functools
import math

import jax
import jax.numpy as jnp
from jax import lax
from jax.experimental import pallas as pl
from jax.experimental.pallas import tpu as pltpu
from jax.sharding import PartitionSpec as P

D = 4096
GROUP = 4
EPSILON = 1e-06
ROPE_BASE = 1000000.0
MESH = pl.DeviceIdType.MESH


def ring(value, shift):
    return (value + shift + 4) % 4


class Place:
    def __init__(self):
        row, col = lax.axis_index("row"), lax.axis_index("col")
        self.z_lo, self.x, self.core = row // 8, (row // 2) % 4, row % 2
        self.y, self.z_hi = col // 2, col % 2
        self.z = 2 * self.z_hi + self.z_lo

    def device(self, **at):
        z = at.get("z", self.z)
        z_lo, z_hi = at.get("z_lo", z % 2), at.get("z_hi", z // 2)
        x, y, core = at.get("x", self.x), at.get("y", self.y), at.get("core", self.core)
        return {"row": 8 * z_lo + 2 * x + core, "col": 2 * y + z_hi}

    def step(self, axis, shift):
        return self.device(**{axis: ring(getattr(self, axis), shift)})

    def other_core(self):
        return self.device(core=1 - self.core)

    def turned(self):
        return self.device(core=self.z_hi, z_hi=self.core, z_lo=self.z_lo)

    def mirrored(self, bit):
        return self.z_lo + bit - 2 * bit * self.z_lo, self.x + bit * (3 - 2 * self.x)

    def chunk_to(self, half):
        z_lo, x = self.mirrored(self.core)
        return self.device(z_lo=z_lo, x=x, core=self.z_hi, z_hi=(self.core + half) % 2)

    def chunk_from(self, half):
        core = (self.z_hi + half) % 2
        z_lo, x = self.mirrored(core)
        return self.device(z_lo=z_lo, x=x, core=core, z_hi=self.core)

    def column(self, y=None, core=None):
        y = self.y if y is None else y
        return 2 * y + (self.core if core is None else core)

    def location(self, x, z):
        return 8 * (z % 2) + 2 * x + z // 2

    def chunk(self, half, x, z):
        first = 16 * (z % 2) + 4 * x + z // 2
        return first if half == 0 else 31 - first


class Net:
    def __init__(self, sent, landed, base=0):
        self.sent, self.landed, self.base, self.copies = sent, landed, base, []

    def send(self, ref, to, target=None):
        i = self.base + len(self.copies)
        copy = pltpu.make_async_remote_copy(
            src_ref=ref,
            dst_ref=ref if target is None else target,
            send_sem=self.sent.at[i],
            recv_sem=self.landed.at[i],
            device_id=to,
            device_id_type=MESH,
        )
        copy.start()
        self.copies.append(copy)
        return copy

    def send_built(self, build):
        copy = Built(self, self.base + len(self.copies), build)
        copy.copy().start()
        self.copies.append(copy)
        return copy

    def finish(self):
        for copy in self.copies:
            copy.wait_send()


class Built:
    def __init__(self, net, i, build):
        self.net, self.i, self.build = net, i, build

    def copy(self):
        ref, to, target = self.build()
        return pltpu.make_async_remote_copy(
            src_ref=ref,
            dst_ref=target,
            send_sem=self.net.sent.at[self.i],
            recv_sem=self.net.landed.at[self.i],
            device_id=to,
            device_id_type=MESH,
        )

    def wait_recv(self):
        self.copy().wait_recv()

    def wait_send(self):
        self.copy().wait_send()


def greet(partners):
    barrier = pltpu.get_barrier_semaphore()
    for partner in partners:
        pl.semaphore_signal(barrier, inc=1, device_id=partner, device_id_type=MESH)
    pl.semaphore_wait(barrier, len(partners))


def plane_gather(net, here, full, rows, spot, own=None):
    axes = (("x", "z"), ("z", "x"))
    piece = rows // 2

    def at(half, first, second):
        x = ring(here.x, first if half == 0 else second)
        z = ring(here.z, second if half == 0 else first)
        return pl.multiple_of(spot(half, x, z), rows)

    def block(half, first, second):
        return full[half].at[pl.ds(at(half, first, second), rows), :]

    def part(half, first, second, way):
        start = at(half, first, second) + (0 if way == 1 else piece)
        return full[half].at[pl.ds(pl.multiple_of(start, piece), piece), :]

    def whole(half, where, way, axis=1):
        def build():
            target = block(half, where, 0)
            source = own[half] if where == 0 and own is not None else target
            return source, here.step(axes[half][axis], way), target

        return net.send_built(build)

    def share(half, first, second, way, axis):
        def build():
            ref = part(half, first, second, way)
            return ref, here.step(axes[half][axis], way), ref

        return net.send_built(build)

    one, two, onward, last = {}, {}, {}, {}
    both = [(half, way) for half in (0, 1) for way in (1, -1)]
    for half, way in both:
        one[half, way] = whole(half, 0, way, 0)
    for half, way in both:
        two[half, 0, way] = whole(half, 0, way)
    yield
    for half, way in both:
        one[half, way].wait_recv()
        onward[half, way] = share(half, -way, 0, way, 0)
    for half, way in both:
        for turn in (1, -1):
            two[half, -way, turn] = whole(half, -way, turn)
    for half, way in both:
        two[half, 0, way].wait_recv()
        last[half, 0, way] = share(half, 0, -way, way, 1)
    yield
    for half, way in both:
        onward[half, way].wait_recv()
    for half, way in both:
        two[half, 2, way] = whole(half, 2, way)
    yield
    for where in (-1, 1):
        for half, way in both:
            two[half, where, way].wait_recv()
            last[half, where, way] = share(half, where, -way, way, 1)
    yield
    for half, way in both:
        last[half, 0, way].wait_recv()
    for half, way in both:
        two[half, 2, way].wait_recv()
        last[half, 2, way] = share(half, 2, -way, way, 1)
    yield
    for where in (-1, 1):
        for half, way in both:
            last[half, where, way].wait_recv()
    yield
    for half, way in both:
        last[half, 2, way].wait_recv()


def column_gather(net, here, part):
    far = {1: 0, -1: 1}
    near, onward, across = {}, {}, []
    for late in (0, 1):
        for way in (1, -1):
            which = far[way] if late == 0 else 1 - far[way]
            near[way, late] = net.send(part(here.y, which), here.step("y", way))
    across.append(net.send(part(here.y, 2), here.other_core()))
    yield
    for way in (1, -1):
        near[way, 0].wait_recv()
        onward[way] = net.send(part(ring(here.y, -way), far[way]), here.step("y", way))
    yield
    for way in (1, -1):
        near[way, 1].wait_recv()
        across.append(net.send(part(ring(here.y, -way), 2), here.other_core()))
    yield
    for copy in across[:3]:
        copy.wait_recv()
    yield
    for way in (1, -1):
        onward[way].wait_recv()
        across.append(net.send(part(ring(here.y, 2), far[way]), here.other_core()))
    yield
    for copy in across[3:]:
        copy.wait_recv()


def token_gather(net, here, part, arrived):
    near, onward, across = {}, {}, []
    for piece in (0, 1):
        arrived(piece)
        for way in (1, -1):
            near[way, piece] = net.send(part(here.y, piece), here.step("y", way))
        across.append(net.send(part(here.y, piece), here.other_core()))
        yield
    for piece in (0, 1):
        for way in (1, -1):
            near[way, piece].wait_recv()
            if (way, piece) in ((1, 0), (-1, 1)):
                onward[way] = net.send(part(ring(here.y, -way), piece), here.step("y", way))
            across.append(net.send(part(ring(here.y, -way), piece), here.other_core()))
        yield
    for way, piece in ((1, 0), (-1, 1)):
        onward[way].wait_recv()
        across.append(net.send(part(ring(here.y, 2), piece), here.other_core()))
    yield
    for copy in across:
        copy.wait_recv()


def rows_of(rows, which):
    return slice(None) if which == 2 else slice(which * (rows // 2), (which + 1) * (rows // 2))


def together(*gathers):
    gathers = list(gathers)
    while gathers:
        for gather in list(gathers):
            if next(gather, gathers) is gathers:
                gathers.remove(gather)


def plane_partners(here):
    return [here.step(axis, way) for axis in ("x", "z") for way in (1, -1)]


def column_partners(here):
    return [here.step("y", 1), here.step("y", -1), here.other_core()]


def small_gather(net, here, full, width):
    def part(y):
        return full.at[:, pl.ds(pl.multiple_of(here.column(y) * width, width), width)]

    near = {way: net.send(part(here.y), here.step("y", way)) for way in (1, -1)}
    across = [net.send(part(here.y), here.other_core())]
    yield
    near[1].wait_recv()
    onward = net.send(part(ring(here.y, -1)), here.step("y", 1))
    near[-1].wait_recv()
    for way in (1, -1):
        across.append(net.send(part(ring(here.y, -way)), here.other_core()))
    yield
    onward.wait_recv()
    across.append(net.send(part(ring(here.y, 2)), here.other_core()))
    yield
    for copy in across:
        copy.wait_recv()


class Exchange:
    def __init__(self, moves, sent, landed, base=0):
        self.moves = []
        for i, (source, target, to, keep) in enumerate(moves, base):
            copy = pltpu.make_async_remote_copy(
                src_ref=source,
                dst_ref=target,
                send_sem=sent.at[i],
                recv_sem=landed.at[i],
                device_id=to,
                device_id_type=MESH,
            )
            local = pltpu.make_async_copy(source, target, landed.at[i])
            self.moves.append((copy, local, keep))
            if keep is None:
                copy.start()
            else:
                pl.when(keep)(local.start)
                pl.when(jnp.logical_not(keep))(copy.start)

    def wait(self, i):
        copy, local, keep = self.moves[i]
        if keep is None:
            copy.wait()
        else:
            pl.when(keep)(local.wait)
            pl.when(jnp.logical_not(keep))(copy.wait)


def weight_move(here, weight, full):
    depth = weight.shape[0]
    mine = pl.multiple_of((8 * here.z_lo + 2 * here.x + here.core) * depth, depth)
    return weight, full.at[pl.ds(mine, depth), :], here.turned(), here.core == here.z_hi


def weight_gather(net, here, full, depth):
    half = depth // 2
    return plane_gather(
        net, here, (full, full), half,
        lambda which, x, z: here.location(x, z) * depth + which * half,
    )


PLANE, TOKEN, COLUMN, SMALL = 40, 14, 11, 7
SINGLE = 7


def layer_kernel(
    scale, tokens, qkv_weight, weight, gain_row, freqs, q_gain, k_gain, home,
    gain, cosine, sine, tokens_full, gain_full, qkv_full, normed,
    q_ref, k_ref, v_ref, keys, values, acc, top, heads, out_weight, total, result,
    sent, landed,
):
    rows, head_dim = k_ref.shape
    half_rows = rows // 2
    width, depth = tokens.shape[1], tokens_full.shape[1]
    here = Place()
    factor_log2 = scale * math.log2(math.e)
    gain[...] = jnp.broadcast_to(gain_row[...].astype(jnp.float32), gain.shape).astype(gain.dtype)
    greet(
        plane_partners(here)
        + column_partners(here)
        + [here.turned()]
        + [f(half) for f in (here.chunk_to, here.chunk_from) for half in (0, 1)]
    )

    columns = pl.ds(pl.multiple_of((2 * here.y + here.z_hi) * width, width), width)
    rows_to = pl.ds(pl.multiple_of(here.core * half_rows, half_rows), half_rows)
    landing = tokens_full.at[rows_to, columns]
    stays = jnp.logical_and(here.core == 0, here.z_hi == 0)
    first = Exchange(
        [
            weight_move(here, qkv_weight, qkv_full),
            (tokens.at[:half_rows, :], landing, here.chunk_to(0), stays),
            (tokens.at[half_rows:, :], landing, here.chunk_to(1), None),
            (gain, gain_full.at[:, columns], here.turned(), here.core == here.z_hi),
        ],
        sent,
        landed,
    )
    net = Net(sent, landed, SINGLE)

    def token_part(y, piece):
        slot = pl.multiple_of(((here.z_hi + piece) % 2) * half_rows, half_rows)
        start = pl.multiple_of(here.column(y) * width, width)
        return tokens_full.at[pl.ds(slot, half_rows), pl.ds(start, width)]

    for which in (0, 1):
        start = here.chunk(which, here.x, here.z) * half_rows

        @pl.loop(0, half_rows // 64)
        def _(n):
            shape = (64, head_dim)
            lane = lax.broadcasted_iota(jnp.int32, shape, 1)
            position = start + n * 64 + lax.broadcasted_iota(jnp.int32, shape, 0)
            angle = position.astype(jnp.float32) * freqs[...]
            where = pl.ds(pl.multiple_of(which * half_rows + n * 64, 64), 64)
            cosine[where, :] = jnp.cos(angle)
            sine[where, :] = jnp.where(lane < head_dim // 2, -1.0, 1.0) * jnp.sin(angle)

    first.wait(0)
    weights = weight_gather(net, here, qkv_full, qkv_weight.shape[0])
    next(weights)
    features = token_gather(net, here, token_part, lambda piece: first.wait(1 + piece))
    next(features)
    next(features)
    first.wait(3)
    together(features, weights, small_gather(net, here, gain_full, width))

    turn = Exchange([weight_move(here, weight, out_weight)], sent, landed, 4)

    step, span = 64, 512
    spans = [slice(i, i + span) for i in range(0, depth, span)]

    @pl.loop(0, rows // step)
    def _(n):
        where = pl.ds(pl.multiple_of(n * step, step), step)
        squares = jnp.zeros((step, 128), jnp.float32)
        for cut in spans:
            part = tokens_full[where, cut].astype(jnp.float32)
            part = part * part
            for i in range(0, span, 128):
                squares = squares + part[:, i : i + 128]
        inverse = lax.rsqrt(jnp.sum(squares, axis=1, keepdims=True) / depth + EPSILON)
        for cut in spans:
            part = tokens_full[where, cut].astype(jnp.float32) * inverse
            normed[where, cut] = (part * gain_full[:1, cut].astype(jnp.float32)).astype(
                normed.dtype
            )

    def turned(u, head_gain, where):
        mean_sq = jnp.mean(u * u, axis=-1, keepdims=True)
        u = u * lax.rsqrt(mean_sq + EPSILON) * head_gain
        turn = pltpu.roll(u, head_dim // 2, 1)
        return (u * cosine[where, :] + turn * sine[where, :]).astype(jnp.bfloat16)

    block = half_rows // 2
    q_width = GROUP * head_dim

    @pl.loop(0, rows // block)
    def _(n):
        where = pl.ds(pl.multiple_of(n * block, block), block)
        both = jnp.dot(
            normed[where, :], qkv_full[:, q_width:], preferred_element_type=jnp.float32
        )
        k_ref[where, :] = turned(both[:, :head_dim], k_gain[...], where)
        v_ref[where, :] = both[:, head_dim:].astype(v_ref.dtype)

    arrivals = plane_gather(
        net, here, (keys, values), rows, lambda half, x, z: (4 * x + z) * rows, (k_ref, v_ref)
    )
    next(arrivals)

    @pl.loop(0, rows // block)
    def _(n):
        where = pl.ds(pl.multiple_of(n * block, block), block)
        four = jnp.dot(
            normed[where, :], qkv_full[:, :q_width], preferred_element_type=jnp.float32
        )
        for h in range(GROUP):
            cut = slice(h * head_dim, (h + 1) * head_dim)
            q_ref[where, cut] = turned(four[:, cut], q_gain[...], where)

    acc[...] = jnp.zeros_like(acc)
    top[...] = jnp.full_like(top, -1e30)

    def unit(which, key_parts, value_parts, allowed=None, among=range(GROUP)):
        key_block = [ref[...] for ref in key_parts]
        value_block = [ref[...] for ref in value_parts]
        key_block = key_block[0] if len(key_block) == 1 else jnp.concatenate(key_block, axis=0)
        value_block = (
            value_block[0] if len(value_block) == 1 else jnp.concatenate(value_block, axis=0)
        )
        wide = jnp.concatenate([value_block, jnp.ones_like(value_block)], axis=1)
        asked = q_ref.at[pl.ds(pl.multiple_of(which * half_rows, half_rows), half_rows), :]

        def scores(h):
            return lax.dot_general(
                asked[:, h * head_dim : (h + 1) * head_dim],
                key_block,
                (((1,), (1,)), ((), ())),
                preferred_element_type=jnp.float32,
            )

        following = scores(among[0])
        for h in among:
            raw = following
            if h != among[-1]:
                following = scores(h + 1)
            if allowed is not None:
                raw = jnp.where(allowed, raw, -1e30)
            before = top[which, h]
            now = jnp.maximum(before, jnp.max(raw, axis=-1, keepdims=True))
            shift = now[:, :1] * factor_log2
            weights = jnp.exp2(raw * factor_log2 - shift).astype(jnp.bfloat16)
            fade = jnp.exp2((before - now) * factor_log2)
            added = jnp.dot(weights, wide, preferred_element_type=jnp.float32)
            acc[which, h] = acc[which, h] * jnp.concatenate([fade, fade], axis=1) + added
            top[which, h] = now

    low, high = here.z_lo, 1 - here.z_lo

    def low_chunk(x, z):
        chunk = here.chunk(0, x, z)
        return chunk + (z % 2) * (31 - 2 * chunk)

    def part(full, x, z, which):
        start = (4 * x + z) * rows + which * half_rows
        return full.at[pl.ds(pl.multiple_of(start, half_rows), half_rows), :]

    def at_once(places, among=range(GROUP)):
        spots = [(ring(here.x, dx), ring(here.z, dz)) for dx, dz in places]
        unit(
            high,
            [part(keys, x, z, z % 2) for x, z in spots],
            [part(values, x, z, z % 2) for x, z in spots],
            among=among,
        )
        for x, z in spots:
            before = (31 + low_chunk(here.x, here.z) - low_chunk(x, z)) // 32
            which = high + before * (low - high)
            theirs = 1 - z % 2 + before * (2 * (z % 2) - 1)
            unit(which, [part(keys, x, z, theirs)], [part(values, x, z, theirs)], among=among)

    def own(ref, which):
        return ref.at[pl.ds(pl.multiple_of(which * half_rows, half_rows), half_rows), :]

    square = (half_rows, half_rows)
    allowed = lax.broadcasted_iota(jnp.int32, square, 1) <= lax.broadcasted_iota(
        jnp.int32, square, 0
    )
    unit(low, [own(k_ref, low)], [own(v_ref, low)], allowed)
    unit(high, [own(k_ref, high)], [own(v_ref, high)], allowed)
    unit(high, [own(k_ref, low)], [own(v_ref, low)])
    pairs = [
        ((1, 0), (3, 0)), ((0, 1), (0, 3)), ((1, 1), (1, 3)), ((3, 1), (3, 3)),
        ((2, 0), (0, 2)), ((2, 1), (2, 3)),
    ]
    steps = (0, 1, 2, 4, 5)

    tables = tuple(
        sum(pair[i][j] * 4**n for n, pair in enumerate(pairs)) for i in (0, 1) for j in (0, 1)
    )

    def stage(n, rest):
        for when in steps:
            pl.when(n == when)(lambda: next(arrivals) and None)
        digits = [r % 4 for r in rest]
        at_once([digits[:2], digits[2:]])
        return tuple(r // 4 for r in rest)

    lax.fori_loop(0, len(pairs), stage, tuple(jnp.int32(t) for t in tables))

    turn.wait(0)
    next(arrivals, None)
    weights = weight_gather(net, here, out_weight, weight.shape[0])
    next(weights)
    spread = []
    for h in range(GROUP):
        at_once([(1, 2), (3, 2)], [h])
        at_once([(2, 2)], [h])
        for which in (0, 1):
            heads[here.column() * GROUP + h, which * half_rows : (which + 1) * half_rows, :] = (
                acc[which, h, :, :head_dim] / acc[which, h, :, head_dim:]
            ).astype(heads.dtype)
        spread.append(
            column_gather(
                net, here,
                lambda y, which, h=h: heads.at[
                    here.column(y) * GROUP + h, rows_of(rows, which), :
                ],
            )
        )
        next(spread[h])
    queue = [0, None, 1, 0, None, 2, 1, None, 3, 2, None, 3, None, 0, 1, None, 2, 3]
    for h in queue:
        next(weights if h is None else spread[h], None)

    span = 2 * GROUP * head_dim

    def product(y, start):
        left = [
            heads[2 * GROUP * y + i, pl.ds(pl.multiple_of(start, block), block), :]
            for i in range(2 * GROUP)
        ]
        right = out_weight[pl.ds(pl.multiple_of(y * span, span), span), :]
        return jnp.dot(
            jnp.concatenate(left, axis=1), right, preferred_element_type=jnp.float32
        )

    for h in (0, 1):
        next(spread[h])

    @pl.loop(0, rows // block)
    def _(n):
        where = pl.ds(pl.multiple_of(n * block, block), block)
        total[where, :] = product(here.y, n * block)

    for h in (2, 3):
        next(spread[h])
    for shift in (1, -1):

        @pl.loop(0, rows // block)
        def _(n):
            where = pl.ds(pl.multiple_of(n * block, block), block)
            total[where, :] = total[where, :] + product(ring(here.y, shift), n * block)

    for h in range(GROUP):
        next(spread[h], None)
    last = []
    for half in (0, 1):
        slot = pl.multiple_of(((here.z_hi + half) % 2) * half_rows, half_rows)

        @pl.loop(0, half_rows // block)
        def _(n):
            start = slot + n * block
            where = pl.ds(pl.multiple_of(start, block), block)
            added = product(ring(here.y, 2), start)
            result[where, :] = (total[where, :] + added).astype(result.dtype)

        stays = jnp.logical_and(here.core == 0, here.z_hi == 0) if half == 0 else None
        last.append(
            Exchange(
                [
                    (
                        result.at[pl.ds(slot, half_rows), :],
                        home.at[half * half_rows : (half + 1) * half_rows, :],
                        here.chunk_from(half),
                        stays,
                    )
                ],
                sent, landed, 5 + half,
            )
        )
    for half in (0, 1):
        last[half].wait(0)
    net.finish()


def per_device(sizes, tokens, norm_gain, qkv_weight, q_gain, k_gain, out_weight):
    n_row, n_col = sizes
    rows, width = tokens.shape
    half = rows // 2
    head_dim = q_gain.shape[0]
    freqs = jnp.power(
        jnp.float32(ROPE_BASE),
        -jnp.arange(head_dim // 2, dtype=jnp.float32) * 2.0 / head_dim,
    )
    bf16, f32 = jnp.bfloat16, jnp.float32
    copies = SINGLE + 3 * PLANE + TOKEN + SMALL + GROUP * COLUMN
    q_width, out_width = GROUP * head_dim, out_weight.shape[1]
    return pl.pallas_call(
        functools.partial(layer_kernel, head_dim ** (-0.5)),
        out_shape=jax.ShapeDtypeStruct((rows, out_width), bf16),
        in_specs=[pl.BlockSpec(memory_space=pl.ANY)] * 3
        + [pl.BlockSpec(memory_space=pltpu.VMEM)] * 4,
        out_specs=pl.BlockSpec(memory_space=pl.ANY),
        scratch_shapes=[
            pltpu.VMEM((16, width), bf16),
            pltpu.VMEM((rows, head_dim), f32),
            pltpu.VMEM((rows, head_dim), f32),
            pltpu.VMEM((rows, n_col * width), bf16),
            pltpu.VMEM((16, n_col * width), bf16),
            pltpu.VMEM((n_row * qkv_weight.shape[0], qkv_weight.shape[1]), bf16),
            pltpu.VMEM((rows, n_col * width), bf16),
            pltpu.VMEM((rows, q_width), bf16),
            pltpu.VMEM((rows, head_dim), bf16),
            pltpu.VMEM((rows, head_dim), bf16),
            pltpu.VMEM((n_row * rows, head_dim), bf16),
            pltpu.VMEM((n_row * rows, head_dim), bf16),
            pltpu.VMEM((2, GROUP, half, 2 * head_dim), f32),
            pltpu.VMEM((2, GROUP, half, head_dim), f32),
            pltpu.VMEM((n_col * GROUP, rows, head_dim), bf16),
            pltpu.VMEM((n_row * out_weight.shape[0], out_width), bf16),
            pltpu.VMEM((rows, out_width), f32),
            pltpu.VMEM((rows, out_width), bf16),
            pltpu.SemaphoreType.DMA((copies,)),
            pltpu.SemaphoreType.DMA((copies,)),
        ],
        compiler_params=pltpu.CompilerParams(
            collective_id=1, has_side_effects=True, vmem_limit_bytes=54 * 1024 * 1024
        ),
        name="layer_kernel",
    )(
        tokens,
        qkv_weight,
        out_weight,
        norm_gain[None, :],
        jnp.concatenate([freqs, freqs])[None, :],
        q_gain[None, :],
        k_gain[None, :],
    )


def solution(mesh):
    placed = (P("row", "col"), P("col"), P("row", "col"), P(), P(), P("row", "col"))
    return jax.shard_map(
        functools.partial(per_device, (mesh.shape["row"], mesh.shape["col"])),
        mesh=mesh,
        in_specs=placed,
        out_specs=P("row", "col"),
        check_vma=False,
    )
```

```python
import functools
import math

import jax
import jax.numpy as jnp
from jax import lax
from jax.experimental import pallas as pl
from jax.experimental.pallas import tpu as pltpu
from jax.sharding import PartitionSpec as P

D = 4096
GROUP = 4
EPSILON = 1e-06
ROPE_BASE = 1000000.0
MESH = pl.DeviceIdType.MESH


def ring(value, shift):
    return (value + shift + 4) % 4


class Place:
    def __init__(self):
        row, col = lax.axis_index("row"), lax.axis_index("col")
        self.z_lo, self.x, self.core = row // 8, (row // 2) % 4, row % 2
        self.y, self.z_hi = col // 2, col % 2
        self.z = 2 * self.z_hi + self.z_lo

    def device(self, **at):
        z = at.get("z", self.z)
        z_lo, z_hi = at.get("z_lo", z % 2), at.get("z_hi", z // 2)
        x, y, core = at.get("x", self.x), at.get("y", self.y), at.get("core", self.core)
        return {"row": 8 * z_lo + 2 * x + core, "col": 2 * y + z_hi}

    def step(self, axis, shift):
        return self.device(**{axis: ring(getattr(self, axis), shift)})

    def other_core(self):
        return self.device(core=1 - self.core)

    def turned(self):
        return self.device(core=self.z_hi, z_hi=self.core, z_lo=self.z_lo)

    def mirrored(self, bit):
        return self.z_lo + bit - 2 * bit * self.z_lo, self.x + bit * (3 - 2 * self.x)

    def chunk_to(self, half):
        z_lo, x = self.mirrored(self.core)
        return self.device(z_lo=z_lo, x=x, core=self.z_hi, z_hi=(self.core + half) % 2)

    def chunk_from(self, half):
        core = (self.z_hi + half) % 2
        z_lo, x = self.mirrored(core)
        return self.device(z_lo=z_lo, x=x, core=core, z_hi=self.core)

    def column(self, y=None, core=None):
        y = self.y if y is None else y
        return 2 * y + (self.core if core is None else core)

    def location(self, x, z):
        return 8 * (z % 2) + 2 * x + z // 2

    def chunk(self, half, x, z):
        first = 16 * (z % 2) + 4 * x + z // 2
        return first if half == 0 else 31 - first


class Net:
    def __init__(self, sent, landed, base=0):
        self.sent, self.landed, self.base, self.copies = sent, landed, base, []

    def send(self, ref, to, target=None):
        i = self.base + len(self.copies)
        copy = pltpu.make_async_remote_copy(
            src_ref=ref,
            dst_ref=ref if target is None else target,
            send_sem=self.sent.at[i],
            recv_sem=self.landed.at[i],
            device_id=to,
            device_id_type=MESH,
        )
        copy.start()
        self.copies.append(copy)
        return copy

    def send_built(self, build):
        copy = Built(self, self.base + len(self.copies), build)
        copy.copy().start()
        self.copies.append(copy)
        return copy

    def finish(self):
        for copy in self.copies:
            copy.wait_send()


class Built:
    def __init__(self, net, i, build):
        self.net, self.i, self.build = net, i, build

    def copy(self):
        ref, to, target = self.build()
        return pltpu.make_async_remote_copy(
            src_ref=ref,
            dst_ref=target,
            send_sem=self.net.sent.at[self.i],
            recv_sem=self.net.landed.at[self.i],
            device_id=to,
            device_id_type=MESH,
        )

    def wait_recv(self):
        self.copy().wait_recv()

    def wait_send(self):
        self.copy().wait_send()


def greet(partners):
    barrier = pltpu.get_barrier_semaphore()
    for partner in partners:
        pl.semaphore_signal(barrier, inc=1, device_id=partner, device_id_type=MESH)
    pl.semaphore_wait(barrier, len(partners))


def plane_gather(net, here, full, rows, spot, own=None):
    axes = (("x", "z"), ("z", "x"))
    piece = rows // 2

    def at(half, first, second):
        x = ring(here.x, first if half == 0 else second)
        z = ring(here.z, second if half == 0 else first)
        return pl.multiple_of(spot(half, x, z), rows)

    def block(half, first, second):
        return full[half].at[pl.ds(at(half, first, second), rows), :]

    def part(half, first, second, way):
        start = at(half, first, second) + (0 if way == 1 else piece)
        return full[half].at[pl.ds(pl.multiple_of(start, piece), piece), :]

    def whole(half, where, way, axis=1):
        def build():
            target = block(half, where, 0)
            source = own[half] if where == 0 and own is not None else target
            return source, here.step(axes[half][axis], way), target

        return net.send_built(build)

    def share(half, first, second, way, axis):
        def build():
            ref = part(half, first, second, way)
            return ref, here.step(axes[half][axis], way), ref

        return net.send_built(build)

    one, two, onward, last = {}, {}, {}, {}
    both = [(half, way) for half in (0, 1) for way in (1, -1)]
    for half, way in both:
        one[half, way] = whole(half, 0, way, 0)
    for half, way in both:
        two[half, 0, way] = whole(half, 0, way)
    yield
    for half, way in both:
        one[half, way].wait_recv()
        onward[half, way] = share(half, -way, 0, way, 0)
    for half, way in both:
        for turn in (1, -1):
            two[half, -way, turn] = whole(half, -way, turn)
    for half, way in both:
        two[half, 0, way].wait_recv()
        last[half, 0, way] = share(half, 0, -way, way, 1)
    yield
    for half, way in both:
        onward[half, way].wait_recv()
    for half, way in both:
        two[half, 2, way] = whole(half, 2, way)
    yield
    for where in (-1, 1):
        for half, way in both:
            two[half, where, way].wait_recv()
            last[half, where, way] = share(half, where, -way, way, 1)
    yield
    for half, way in both:
        last[half, 0, way].wait_recv()
    for half, way in both:
        two[half, 2, way].wait_recv()
        last[half, 2, way] = share(half, 2, -way, way, 1)
    yield
    for where in (-1, 1):
        for half, way in both:
            last[half, where, way].wait_recv()
    yield
    for half, way in both:
        last[half, 2, way].wait_recv()


def column_gather(net, here, part):
    far = {1: 0, -1: 1}
    near, onward, across = {}, {}, []
    for late in (0, 1):
        for way in (1, -1):
            which = far[way] if late == 0 else 1 - far[way]
            near[way, late] = net.send(part(here.y, which), here.step("y", way))
    across.append(net.send(part(here.y, 2), here.other_core()))
    yield
    for way in (1, -1):
        near[way, 0].wait_recv()
        onward[way] = net.send(part(ring(here.y, -way), far[way]), here.step("y", way))
    yield
    for way in (1, -1):
        near[way, 1].wait_recv()
        across.append(net.send(part(ring(here.y, -way), 2), here.other_core()))
    yield
    for copy in across[:3]:
        copy.wait_recv()
    yield
    for way in (1, -1):
        onward[way].wait_recv()
        across.append(net.send(part(ring(here.y, 2), far[way]), here.other_core()))
    yield
    for copy in across[3:]:
        copy.wait_recv()


def token_gather(net, here, part, arrived):
    near, onward, across = {}, {}, []
    for piece in (0, 1):
        arrived(piece)
        for way in (1, -1):
            near[way, piece] = net.send(part(here.y, piece), here.step("y", way))
        across.append(net.send(part(here.y, piece), here.other_core()))
        yield
    for piece in (0, 1):
        for way in (1, -1):
            near[way, piece].wait_recv()
            if (way, piece) in ((1, 0), (-1, 1)):
                onward[way] = net.send(part(ring(here.y, -way), piece), here.step("y", way))
            across.append(net.send(part(ring(here.y, -way), piece), here.other_core()))
        yield
    for way, piece in ((1, 0), (-1, 1)):
        onward[way].wait_recv()
        across.append(net.send(part(ring(here.y, 2), piece), here.other_core()))
    yield
    for copy in across:
        copy.wait_recv()


def rows_of(rows, which):
    return slice(None) if which == 2 else slice(which * (rows // 2), (which + 1) * (rows // 2))


def together(*gathers):
    gathers = list(gathers)
    while gathers:
        for gather in list(gathers):
            if next(gather, gathers) is gathers:
                gathers.remove(gather)


def plane_partners(here):
    return [here.step(axis, way) for axis in ("x", "z") for way in (1, -1)]


def column_partners(here):
    return [here.step("y", 1), here.step("y", -1), here.other_core()]


def small_gather(net, here, full, width):
    def part(y):
        return full.at[:, pl.ds(pl.multiple_of(here.column(y) * width, width), width)]

    near = {way: net.send(part(here.y), here.step("y", way)) for way in (1, -1)}
    across = [net.send(part(here.y), here.other_core())]
    yield
    near[1].wait_recv()
    onward = net.send(part(ring(here.y, -1)), here.step("y", 1))
    near[-1].wait_recv()
    for way in (1, -1):
        across.append(net.send(part(ring(here.y, -way)), here.other_core()))
    yield
    onward.wait_recv()
    across.append(net.send(part(ring(here.y, 2)), here.other_core()))
    yield
    for copy in across:
        copy.wait_recv()


class Exchange:
    def __init__(self, moves, sent, landed, base=0):
        self.moves = []
        for i, (source, target, to, keep) in enumerate(moves, base):
            copy = pltpu.make_async_remote_copy(
                src_ref=source,
                dst_ref=target,
                send_sem=sent.at[i],
                recv_sem=landed.at[i],
                device_id=to,
                device_id_type=MESH,
            )
            local = pltpu.make_async_copy(source, target, landed.at[i])
            self.moves.append((copy, local, keep))
            if keep is None:
                copy.start()
            else:
                pl.when(keep)(local.start)
                pl.when(jnp.logical_not(keep))(copy.start)

    def wait(self, i):
        copy, local, keep = self.moves[i]
        if keep is None:
            copy.wait()
        else:
            pl.when(keep)(local.wait)
            pl.when(jnp.logical_not(keep))(copy.wait)


def weight_move(here, weight, full):
    depth = weight.shape[0]
    mine = pl.multiple_of((8 * here.z_lo + 2 * here.x + here.core) * depth, depth)
    return weight, full.at[pl.ds(mine, depth), :], here.turned(), here.core == here.z_hi


def weight_gather(net, here, full, depth):
    half = depth // 2
    return plane_gather(
        net, here, (full, full), half,
        lambda which, x, z: here.location(x, z) * depth + which * half,
    )


PLANE, TOKEN, COLUMN, SMALL = 40, 14, 11, 7
SINGLE = 7


def layer_kernel(
    scale, tokens, qkv_weight, weight, gain_row, freqs, q_gain, k_gain, home,
    gain, cosine, sine, tokens_full, gain_full, qkv_full, normed,
    q_ref, k_ref, v_ref, keys, values, acc, top, heads, out_weight, total, result,
    sent, landed,
):
    rows, head_dim = k_ref.shape
    half_rows = rows // 2
    width, depth = tokens.shape[1], tokens_full.shape[1]
    here = Place()
    factor_log2 = scale * math.log2(math.e)
    gain[...] = jnp.broadcast_to(gain_row[...].astype(jnp.float32), gain.shape).astype(gain.dtype)
    greet(
        plane_partners(here)
        + column_partners(here)
        + [here.turned()]
        + [f(half) for f in (here.chunk_to, here.chunk_from) for half in (0, 1)]
    )

    columns = pl.ds(pl.multiple_of((2 * here.y + here.z_hi) * width, width), width)
    rows_to = pl.ds(pl.multiple_of(here.core * half_rows, half_rows), half_rows)
    landing = tokens_full.at[rows_to, columns]
    stays = jnp.logical_and(here.core == 0, here.z_hi == 0)
    first = Exchange(
        [
            weight_move(here, qkv_weight, qkv_full),
            (tokens.at[:half_rows, :], landing, here.chunk_to(0), stays),
            (tokens.at[half_rows:, :], landing, here.chunk_to(1), None),
            (gain, gain_full.at[:, columns], here.turned(), here.core == here.z_hi),
        ],
        sent,
        landed,
    )
    net = Net(sent, landed, SINGLE)

    def token_part(y, piece):
        slot = pl.multiple_of(((here.z_hi + piece) % 2) * half_rows, half_rows)
        start = pl.multiple_of(here.column(y) * width, width)
        return tokens_full.at[pl.ds(slot, half_rows), pl.ds(start, width)]

    for which in (0, 1):
        start = here.chunk(which, here.x, here.z) * half_rows

        @pl.loop(0, half_rows // 64)
        def _(n):
            shape = (64, head_dim)
            lane = lax.broadcasted_iota(jnp.int32, shape, 1)
            position = start + n * 64 + lax.broadcasted_iota(jnp.int32, shape, 0)
            angle = position.astype(jnp.float32) * freqs[...]
            where = pl.ds(pl.multiple_of(which * half_rows + n * 64, 64), 64)
            cosine[where, :] = jnp.cos(angle)
            sine[where, :] = jnp.where(lane < head_dim // 2, -1.0, 1.0) * jnp.sin(angle)

    first.wait(0)
    weights = weight_gather(net, here, qkv_full, qkv_weight.shape[0])
    next(weights)
    features = token_gather(net, here, token_part, lambda piece: first.wait(1 + piece))
    next(features)
    next(features)
    first.wait(3)
    together(features, weights, small_gather(net, here, gain_full, width))

    turn = Exchange([weight_move(here, weight, out_weight)], sent, landed, 4)

    step, span = 64, 512
    spans = [slice(i, i + span) for i in range(0, depth, span)]

    @pl.loop(0, rows // step)
    def _(n):
        where = pl.ds(pl.multiple_of(n * step, step), step)
        squares = jnp.zeros((step, 128), jnp.float32)
        for cut in spans:
            part = tokens_full[where, cut].astype(jnp.float32)
            part = part * part
            for i in range(0, span, 128):
                squares = squares + part[:, i : i + 128]
        inverse = lax.rsqrt(jnp.sum(squares, axis=1, keepdims=True) / depth + EPSILON)
        for cut in spans:
            part = tokens_full[where, cut].astype(jnp.float32) * inverse
            normed[where, cut] = (part * gain_full[:1, cut].astype(jnp.float32)).astype(
                normed.dtype
            )

    def turned(u, head_gain, where):
        mean_sq = jnp.mean(u * u, axis=-1, keepdims=True)
        u = u * lax.rsqrt(mean_sq + EPSILON) * head_gain
        turn = pltpu.roll(u, head_dim // 2, 1)
        return (u * cosine[where, :] + turn * sine[where, :]).astype(jnp.bfloat16)

    block = half_rows // 2
    q_width = GROUP * head_dim

    @pl.loop(0, rows // block)
    def _(n):
        where = pl.ds(pl.multiple_of(n * block, block), block)
        both = jnp.dot(
            normed[where, :], qkv_full[:, q_width:], preferred_element_type=jnp.float32
        )
        k_ref[where, :] = turned(both[:, :head_dim], k_gain[...], where)
        v_ref[where, :] = both[:, head_dim:].astype(v_ref.dtype)

    arrivals = plane_gather(
        net, here, (keys, values), rows, lambda half, x, z: (4 * x + z) * rows, (k_ref, v_ref)
    )
    next(arrivals)

    @pl.loop(0, rows // block)
    def _(n):
        where = pl.ds(pl.multiple_of(n * block, block), block)
        four = jnp.dot(
            normed[where, :], qkv_full[:, :q_width], preferred_element_type=jnp.float32
        )
        for h in range(GROUP):
            cut = slice(h * head_dim, (h + 1) * head_dim)
            q_ref[where, cut] = turned(four[:, cut], q_gain[...], where)

    acc[...] = jnp.zeros_like(acc)
    top[...] = jnp.full_like(top, -1e30)

    def unit(which, key_parts, value_parts, allowed=None, among=range(GROUP)):
        key_block = [ref[...] for ref in key_parts]
        value_block = [ref[...] for ref in value_parts]
        key_block = key_block[0] if len(key_block) == 1 else jnp.concatenate(key_block, axis=0)
        value_block = (
            value_block[0] if len(value_block) == 1 else jnp.concatenate(value_block, axis=0)
        )
        wide = jnp.concatenate([value_block, jnp.ones_like(value_block)], axis=1)
        asked = q_ref.at[pl.ds(pl.multiple_of(which * half_rows, half_rows), half_rows), :]

        def scores(h):
            return lax.dot_general(
                asked[:, h * head_dim : (h + 1) * head_dim],
                key_block,
                (((1,), (1,)), ((), ())),
                preferred_element_type=jnp.float32,
            )

        following = scores(among[0])
        for h in among:
            raw = following
            if h != among[-1]:
                following = scores(h + 1)
            if allowed is not None:
                raw = jnp.where(allowed, raw, -1e30)
            before = top[which, h]
            now = jnp.maximum(before, jnp.max(raw, axis=-1, keepdims=True))
            shift = jnp.concatenate([now * factor_log2] * (raw.shape[1] // head_dim), axis=1)
            weights = jnp.exp2(raw * factor_log2 - shift).astype(jnp.bfloat16)
            fade = jnp.exp2((before - now) * factor_log2)
            added = jnp.dot(weights, wide, preferred_element_type=jnp.float32)
            acc[which, h] = acc[which, h] * jnp.concatenate([fade, fade], axis=1) + added
            top[which, h] = now

    low, high = here.z_lo, 1 - here.z_lo

    def low_chunk(x, z):
        chunk = here.chunk(0, x, z)
        return chunk + (z % 2) * (31 - 2 * chunk)

    def part(full, x, z, which):
        start = (4 * x + z) * rows + which * half_rows
        return full.at[pl.ds(pl.multiple_of(start, half_rows), half_rows), :]

    def at_once(places, among=range(GROUP)):
        spots = [(ring(here.x, dx), ring(here.z, dz)) for dx, dz in places]
        unit(
            high,
            [part(keys, x, z, z % 2) for x, z in spots],
            [part(values, x, z, z % 2) for x, z in spots],
            among=among,
        )
        for x, z in spots:
            before = (31 + low_chunk(here.x, here.z) - low_chunk(x, z)) // 32
            which = high + before * (low - high)
            theirs = 1 - z % 2 + before * (2 * (z % 2) - 1)
            unit(which, [part(keys, x, z, theirs)], [part(values, x, z, theirs)], among=among)

    def own(ref, which):
        return ref.at[pl.ds(pl.multiple_of(which * half_rows, half_rows), half_rows), :]

    square = (half_rows, half_rows)
    allowed = lax.broadcasted_iota(jnp.int32, square, 1) <= lax.broadcasted_iota(
        jnp.int32, square, 0
    )
    unit(low, [own(k_ref, low)], [own(v_ref, low)], allowed)
    unit(high, [own(k_ref, high)], [own(v_ref, high)], allowed)
    unit(high, [own(k_ref, low)], [own(v_ref, low)])
    pairs = [
        ((1, 0), (3, 0)), ((0, 1), (0, 3)), ((1, 1), (1, 3)), ((3, 1), (3, 3)),
        ((2, 0), (0, 2)), ((2, 1), (2, 3)),
    ]
    steps = (0, 1, 2, 4, 5)

    tables = tuple(
        sum(pair[i][j] * 4**n for n, pair in enumerate(pairs)) for i in (0, 1) for j in (0, 1)
    )

    def stage(n, rest):
        for when in steps:
            pl.when(n == when)(lambda: next(arrivals) and None)
        digits = [r % 4 for r in rest]
        at_once([digits[:2], digits[2:]])
        return tuple(r // 4 for r in rest)

    lax.fori_loop(0, len(pairs), stage, tuple(jnp.int32(t) for t in tables))

    turn.wait(0)
    next(arrivals, None)
    weights = weight_gather(net, here, out_weight, weight.shape[0])
    next(weights)
    spread = []
    for h in range(GROUP):
        at_once([(1, 2), (3, 2)], [h])
        at_once([(2, 2)], [h])
        for which in (0, 1):
            heads[here.column() * GROUP + h, which * half_rows : (which + 1) * half_rows, :] = (
                acc[which, h, :, :head_dim] / acc[which, h, :, head_dim:]
            ).astype(heads.dtype)
        spread.append(
            column_gather(
                net, here,
                lambda y, which, h=h: heads.at[
                    here.column(y) * GROUP + h, rows_of(rows, which), :
                ],
            )
        )
        next(spread[h])
    queue = [0, None, 1, 0, None, 2, 1, None, 3, 2, None, 3, None, 0, 1, None, 2, 3]
    for h in queue:
        next(weights if h is None else spread[h], None)

    span = 2 * GROUP * head_dim

    def product(y, start):
        left = [
            heads[2 * GROUP * y + i, pl.ds(pl.multiple_of(start, block), block), :]
            for i in range(2 * GROUP)
        ]
        right = out_weight[pl.ds(pl.multiple_of(y * span, span), span), :]
        return jnp.dot(
            jnp.concatenate(left, axis=1), right, preferred_element_type=jnp.float32
        )

    for h in (0, 1):
        next(spread[h])

    @pl.loop(0, rows // block)
    def _(n):
        where = pl.ds(pl.multiple_of(n * block, block), block)
        total[where, :] = product(here.y, n * block)

    for h in (2, 3):
        next(spread[h])
    for shift in (1, -1):

        @pl.loop(0, rows // block)
        def _(n):
            where = pl.ds(pl.multiple_of(n * block, block), block)
            total[where, :] = total[where, :] + product(ring(here.y, shift), n * block)

    for h in range(GROUP):
        next(spread[h], None)
    last = []
    for half in (0, 1):
        slot = pl.multiple_of(((here.z_hi + half) % 2) * half_rows, half_rows)

        @pl.loop(0, half_rows // block)
        def _(n):
            start = slot + n * block
            where = pl.ds(pl.multiple_of(start, block), block)
            added = product(ring(here.y, 2), start)
            result[where, :] = (total[where, :] + added).astype(result.dtype)

        stays = jnp.logical_and(here.core == 0, here.z_hi == 0) if half == 0 else None
        last.append(
            Exchange(
                [
                    (
                        result.at[pl.ds(slot, half_rows), :],
                        home.at[half * half_rows : (half + 1) * half_rows, :],
                        here.chunk_from(half),
                        stays,
                    )
                ],
                sent, landed, 5 + half,
            )
        )
    for half in (0, 1):
        last[half].wait(0)
    net.finish()


def per_device(sizes, tokens, norm_gain, qkv_weight, q_gain, k_gain, out_weight):
    n_row, n_col = sizes
    rows, width = tokens.shape
    half = rows // 2
    head_dim = q_gain.shape[0]
    freqs = jnp.power(
        jnp.float32(ROPE_BASE),
        -jnp.arange(head_dim // 2, dtype=jnp.float32) * 2.0 / head_dim,
    )
    bf16, f32 = jnp.bfloat16, jnp.float32
    copies = SINGLE + 3 * PLANE + TOKEN + SMALL + GROUP * COLUMN
    q_width, out_width = GROUP * head_dim, out_weight.shape[1]
    return pl.pallas_call(
        functools.partial(layer_kernel, head_dim ** (-0.5)),
        out_shape=jax.ShapeDtypeStruct((rows, out_width), bf16),
        in_specs=[pl.BlockSpec(memory_space=pl.ANY)] * 3
        + [pl.BlockSpec(memory_space=pltpu.VMEM)] * 4,
        out_specs=pl.BlockSpec(memory_space=pl.ANY),
        scratch_shapes=[
            pltpu.VMEM((16, width), bf16),
            pltpu.VMEM((rows, head_dim), f32),
            pltpu.VMEM((rows, head_dim), f32),
            pltpu.VMEM((rows, n_col * width), bf16),
            pltpu.VMEM((16, n_col * width), bf16),
            pltpu.VMEM((n_row * qkv_weight.shape[0], qkv_weight.shape[1]), bf16),
            pltpu.VMEM((rows, n_col * width), bf16),
            pltpu.VMEM((rows, q_width), bf16),
            pltpu.VMEM((rows, head_dim), bf16),
            pltpu.VMEM((rows, head_dim), bf16),
            pltpu.VMEM((n_row * rows, head_dim), bf16),
            pltpu.VMEM((n_row * rows, head_dim), bf16),
            pltpu.VMEM((2, GROUP, half, 2 * head_dim), f32),
            pltpu.VMEM((2, GROUP, half, head_dim), f32),
            pltpu.VMEM((n_col * GROUP, rows, head_dim), bf16),
            pltpu.VMEM((n_row * out_weight.shape[0], out_width), bf16),
            pltpu.VMEM((rows, out_width), f32),
            pltpu.VMEM((rows, out_width), bf16),
            pltpu.SemaphoreType.DMA((copies,)),
            pltpu.SemaphoreType.DMA((copies,)),
        ],
        compiler_params=pltpu.CompilerParams(
            collective_id=1, has_side_effects=True, vmem_limit_bytes=54 * 1024 * 1024
        ),
        name="layer_kernel",
    )(
        tokens,
        qkv_weight,
        out_weight,
        norm_gain[None, :],
        jnp.concatenate([freqs, freqs])[None, :],
        q_gain[None, :],
        k_gain[None, :],
    )


def solution(mesh):
    placed = (P("row", "col"), P("col"), P("row", "col"), P(), P(), P("row", "col"))
    return jax.shard_map(
        functools.partial(per_device, (mesh.shape["row"], mesh.shape["col"])),
        mesh=mesh,
        in_specs=placed,
        out_specs=P("row", "col"),
        check_vma=False,
    )
```

```python
import functools
import math

import jax
import jax.numpy as jnp
from jax import lax
from jax.experimental import pallas as pl
from jax.experimental.pallas import tpu as pltpu
from jax.sharding import PartitionSpec as P

D = 4096
GROUP = 4
EPSILON = 1e-06
ROPE_BASE = 1000000.0
MESH = pl.DeviceIdType.MESH


def ring(value, shift):
    return (value + shift + 4) % 4


class Place:
    def __init__(self):
        row, col = lax.axis_index("row"), lax.axis_index("col")
        self.z_lo, self.x, self.core = row // 8, (row // 2) % 4, row % 2
        self.y, self.z_hi = col // 2, col % 2
        self.z = 2 * self.z_hi + self.z_lo

    def device(self, **at):
        z = at.get("z", self.z)
        z_lo, z_hi = at.get("z_lo", z % 2), at.get("z_hi", z // 2)
        x, y, core = at.get("x", self.x), at.get("y", self.y), at.get("core", self.core)
        return {"row": 8 * z_lo + 2 * x + core, "col": 2 * y + z_hi}

    def step(self, axis, shift):
        return self.device(**{axis: ring(getattr(self, axis), shift)})

    def other_core(self):
        return self.device(core=1 - self.core)

    def turned(self):
        return self.device(core=self.z_hi, z_hi=self.core, z_lo=self.z_lo)

    def mirrored(self, bit):
        return self.z_lo + bit - 2 * bit * self.z_lo, self.x + bit * (3 - 2 * self.x)

    def chunk_to(self, half):
        z_lo, x = self.mirrored(self.core)
        return self.device(z_lo=z_lo, x=x, core=self.z_hi, z_hi=(self.core + half) % 2)

    def chunk_from(self, half):
        core = (self.z_hi + half) % 2
        z_lo, x = self.mirrored(core)
        return self.device(z_lo=z_lo, x=x, core=core, z_hi=self.core)

    def column(self, y=None, core=None):
        y = self.y if y is None else y
        return 2 * y + (self.core if core is None else core)

    def location(self, x, z):
        return 8 * (z % 2) + 2 * x + z // 2

    def chunk(self, half, x, z):
        first = 16 * (z % 2) + 4 * x + z // 2
        return first if half == 0 else 31 - first


class Net:
    def __init__(self, sent, landed, base=0):
        self.sent, self.landed, self.base, self.copies = sent, landed, base, []

    def send(self, ref, to, target=None):
        i = self.base + len(self.copies)
        copy = pltpu.make_async_remote_copy(
            src_ref=ref,
            dst_ref=ref if target is None else target,
            send_sem=self.sent.at[i],
            recv_sem=self.landed.at[i],
            device_id=to,
            device_id_type=MESH,
        )
        copy.start()
        self.copies.append(copy)
        return copy

    def send_built(self, build):
        copy = Built(self, self.base + len(self.copies), build)
        copy.copy().start()
        self.copies.append(copy)
        return copy

    def finish(self):
        for copy in self.copies:
            copy.wait_send()


class Built:
    def __init__(self, net, i, build):
        self.net, self.i, self.build = net, i, build

    def copy(self):
        ref, to, target = self.build()
        return pltpu.make_async_remote_copy(
            src_ref=ref,
            dst_ref=target,
            send_sem=self.net.sent.at[self.i],
            recv_sem=self.net.landed.at[self.i],
            device_id=to,
            device_id_type=MESH,
        )

    def wait_recv(self):
        self.copy().wait_recv()

    def wait_send(self):
        self.copy().wait_send()


def greet(partners):
    barrier = pltpu.get_barrier_semaphore()
    for partner in partners:
        pl.semaphore_signal(barrier, inc=1, device_id=partner, device_id_type=MESH)
    pl.semaphore_wait(barrier, len(partners))


def plane_gather(net, here, full, rows, spot, own=None):
    axes = (("x", "z"), ("z", "x"))
    piece = rows // 2

    def at(half, first, second):
        x = ring(here.x, first if half == 0 else second)
        z = ring(here.z, second if half == 0 else first)
        return pl.multiple_of(spot(half, x, z), rows)

    def block(half, first, second):
        return full[half].at[pl.ds(at(half, first, second), rows), :]

    def part(half, first, second, way):
        start = at(half, first, second) + (0 if way == 1 else piece)
        return full[half].at[pl.ds(pl.multiple_of(start, piece), piece), :]

    def whole(half, where, way, axis=1):
        def build():
            target = block(half, where, 0)
            source = own[half] if where == 0 and own is not None else target
            return source, here.step(axes[half][axis], way), target

        return net.send_built(build)

    def share(half, first, second, way, axis):
        def build():
            ref = part(half, first, second, way)
            return ref, here.step(axes[half][axis], way), ref

        return net.send_built(build)

    one, two, onward, last = {}, {}, {}, {}
    both = [(half, way) for half in (0, 1) for way in (1, -1)]
    for half, way in both:
        one[half, way] = whole(half, 0, way, 0)
    for half, way in both:
        two[half, 0, way] = whole(half, 0, way)
    yield
    for half, way in both:
        one[half, way].wait_recv()
        onward[half, way] = share(half, -way, 0, way, 0)
    for half, way in both:
        for turn in (1, -1):
            two[half, -way, turn] = whole(half, -way, turn)
    for half, way in both:
        two[half, 0, way].wait_recv()
        last[half, 0, way] = share(half, 0, -way, way, 1)
    yield
    for half, way in both:
        onward[half, way].wait_recv()
    for half, way in both:
        two[half, 2, way] = whole(half, 2, way)
    yield
    for where in (-1, 1):
        for half, way in both:
            two[half, where, way].wait_recv()
            last[half, where, way] = share(half, where, -way, way, 1)
    yield
    for half, way in both:
        last[half, 0, way].wait_recv()
    for half, way in both:
        two[half, 2, way].wait_recv()
        last[half, 2, way] = share(half, 2, -way, way, 1)
    yield
    for where in (-1, 1):
        for half, way in both:
            last[half, where, way].wait_recv()
    yield
    for half, way in both:
        last[half, 2, way].wait_recv()


def column_gather(net, here, part):
    far = {1: 0, -1: 1}
    near, onward, across = {}, {}, []
    for late in (0, 1):
        for way in (1, -1):
            which = far[way] if late == 0 else 1 - far[way]
            near[way, late] = net.send(part(here.y, which), here.step("y", way))
    across.append(net.send(part(here.y, 2), here.other_core()))
    yield
    for way in (1, -1):
        near[way, 0].wait_recv()
        onward[way] = net.send(part(ring(here.y, -way), far[way]), here.step("y", way))
    yield
    for way in (1, -1):
        near[way, 1].wait_recv()
        across.append(net.send(part(ring(here.y, -way), 2), here.other_core()))
    yield
    for copy in across[:3]:
        copy.wait_recv()
    yield
    for way in (1, -1):
        onward[way].wait_recv()
        across.append(net.send(part(ring(here.y, 2), far[way]), here.other_core()))
    yield
    for copy in across[3:]:
        copy.wait_recv()


def token_gather(net, here, part, arrived):
    near, onward, across = {}, {}, []
    for piece in (0, 1):
        arrived(piece)
        for way in (1, -1):
            near[way, piece] = net.send(part(here.y, piece), here.step("y", way))
        across.append(net.send(part(here.y, piece), here.other_core()))
        yield
    for piece in (0, 1):
        for way in (1, -1):
            near[way, piece].wait_recv()
            if (way, piece) in ((1, 0), (-1, 1)):
                onward[way] = net.send(part(ring(here.y, -way), piece), here.step("y", way))
            across.append(net.send(part(ring(here.y, -way), piece), here.other_core()))
        yield
    for way, piece in ((1, 0), (-1, 1)):
        onward[way].wait_recv()
        across.append(net.send(part(ring(here.y, 2), piece), here.other_core()))
    yield
    for copy in across:
        copy.wait_recv()


def rows_of(rows, which):
    return slice(None) if which == 2 else slice(which * (rows // 2), (which + 1) * (rows // 2))


def together(*gathers):
    gathers = list(gathers)
    while gathers:
        for gather in list(gathers):
            if next(gather, gathers) is gathers:
                gathers.remove(gather)


def plane_partners(here):
    return [here.step(axis, way) for axis in ("x", "z") for way in (1, -1)]


def column_partners(here):
    return [here.step("y", 1), here.step("y", -1), here.other_core()]


def small_gather(net, here, full, width):
    def part(y):
        return full.at[:, pl.ds(pl.multiple_of(here.column(y) * width, width), width)]

    near = {way: net.send(part(here.y), here.step("y", way)) for way in (1, -1)}
    across = [net.send(part(here.y), here.other_core())]
    yield
    near[1].wait_recv()
    onward = net.send(part(ring(here.y, -1)), here.step("y", 1))
    near[-1].wait_recv()
    for way in (1, -1):
        across.append(net.send(part(ring(here.y, -way)), here.other_core()))
    yield
    onward.wait_recv()
    across.append(net.send(part(ring(here.y, 2)), here.other_core()))
    yield
    for copy in across:
        copy.wait_recv()


class Exchange:
    def __init__(self, moves, sent, landed, base=0):
        self.moves = []
        for i, (source, target, to, keep) in enumerate(moves, base):
            copy = pltpu.make_async_remote_copy(
                src_ref=source,
                dst_ref=target,
                send_sem=sent.at[i],
                recv_sem=landed.at[i],
                device_id=to,
                device_id_type=MESH,
            )
            local = pltpu.make_async_copy(source, target, landed.at[i])
            self.moves.append((copy, local, keep))
            if keep is None:
                copy.start()
            else:
                pl.when(keep)(local.start)
                pl.when(jnp.logical_not(keep))(copy.start)

    def wait(self, i):
        copy, local, keep = self.moves[i]
        if keep is None:
            copy.wait()
        else:
            pl.when(keep)(local.wait)
            pl.when(jnp.logical_not(keep))(copy.wait)


def weight_move(here, weight, full):
    depth = weight.shape[0]
    mine = pl.multiple_of((8 * here.z_lo + 2 * here.x + here.core) * depth, depth)
    return weight, full.at[pl.ds(mine, depth), :], here.turned(), here.core == here.z_hi


def weight_gather(net, here, full, depth):
    half = depth // 2
    return plane_gather(
        net, here, (full, full), half,
        lambda which, x, z: here.location(x, z) * depth + which * half,
    )


PLANE, TOKEN, COLUMN, SMALL = 40, 14, 11, 7
SINGLE = 7


def layer_kernel(
    scale, tokens, qkv_weight, weight, gain_row, freqs, q_gain, k_gain, home,
    gain, cosine, sine, tokens_full, gain_full, qkv_full, normed,
    q_ref, k_ref, v_ref, keys, values, acc, top, heads, out_weight, total, result,
    sent, landed,
):
    rows, head_dim = k_ref.shape
    half_rows = rows // 2
    width, depth = tokens.shape[1], tokens_full.shape[1]
    here = Place()
    factor_log2 = scale * math.log2(math.e)
    gain[...] = jnp.broadcast_to(gain_row[...].astype(jnp.float32), gain.shape).astype(gain.dtype)
    greet(
        plane_partners(here)
        + column_partners(here)
        + [here.turned()]
        + [f(half) for f in (here.chunk_to, here.chunk_from) for half in (0, 1)]
    )

    columns = pl.ds(pl.multiple_of((2 * here.y + here.z_hi) * width, width), width)
    rows_to = pl.ds(pl.multiple_of(here.core * half_rows, half_rows), half_rows)
    landing = tokens_full.at[rows_to, columns]
    stays = jnp.logical_and(here.core == 0, here.z_hi == 0)
    first = Exchange(
        [
            weight_move(here, qkv_weight, qkv_full),
            (tokens.at[:half_rows, :], landing, here.chunk_to(0), stays),
            (tokens.at[half_rows:, :], landing, here.chunk_to(1), None),
            (gain, gain_full.at[:, columns], here.turned(), here.core == here.z_hi),
        ],
        sent,
        landed,
    )
    net = Net(sent, landed, SINGLE)

    def token_part(y, piece):
        slot = pl.multiple_of(((here.z_hi + piece) % 2) * half_rows, half_rows)
        start = pl.multiple_of(here.column(y) * width, width)
        return tokens_full.at[pl.ds(slot, half_rows), pl.ds(start, width)]

    for which in (0, 1):
        start = here.chunk(which, here.x, here.z) * half_rows

        @pl.loop(0, half_rows // 64)
        def _(n):
            shape = (64, head_dim)
            lane = lax.broadcasted_iota(jnp.int32, shape, 1)
            position = start + n * 64 + lax.broadcasted_iota(jnp.int32, shape, 0)
            angle = position.astype(jnp.float32) * freqs[...]
            where = pl.ds(pl.multiple_of(which * half_rows + n * 64, 64), 64)
            cosine[where, :] = jnp.cos(angle)
            sine[where, :] = jnp.where(lane < head_dim // 2, -1.0, 1.0) * jnp.sin(angle)

    first.wait(0)
    weights = weight_gather(net, here, qkv_full, qkv_weight.shape[0])
    next(weights)
    features = token_gather(net, here, token_part, lambda piece: first.wait(1 + piece))
    next(features)
    next(features)
    first.wait(3)
    together(features, weights, small_gather(net, here, gain_full, width))

    turn = Exchange([weight_move(here, weight, out_weight)], sent, landed, 4)

    step, span = 64, 512
    spans = [slice(i, i + span) for i in range(0, depth, span)]

    @pl.loop(0, rows // step)
    def _(n):
        where = pl.ds(pl.multiple_of(n * step, step), step)
        squares = jnp.zeros((step, 128), jnp.float32)
        for cut in spans:
            part = tokens_full[where, cut].astype(jnp.float32)
            part = part * part
            for i in range(0, span, 128):
                squares = squares + part[:, i : i + 128]
        inverse = lax.rsqrt(jnp.sum(squares, axis=1, keepdims=True) / depth + EPSILON)
        for cut in spans:
            part = tokens_full[where, cut].astype(jnp.float32) * inverse
            normed[where, cut] = (part * gain_full[:1, cut].astype(jnp.float32)).astype(
                normed.dtype
            )

    def turned(u, head_gain, where):
        mean_sq = jnp.mean(u * u, axis=-1, keepdims=True)
        u = u * lax.rsqrt(mean_sq + EPSILON) * head_gain
        turn = pltpu.roll(u, head_dim // 2, 1)
        return (u * cosine[where, :] + turn * sine[where, :]).astype(jnp.bfloat16)

    block = half_rows // 2
    q_width = GROUP * head_dim

    @pl.loop(0, rows // block)
    def _(n):
        where = pl.ds(pl.multiple_of(n * block, block), block)
        both = jnp.dot(
            normed[where, :], qkv_full[:, q_width:], preferred_element_type=jnp.float32
        )
        k_ref[where, :] = turned(both[:, :head_dim], k_gain[...], where)
        v_ref[where, :] = both[:, head_dim:].astype(v_ref.dtype)

    arrivals = plane_gather(
        net, here, (keys, values), rows, lambda half, x, z: (4 * x + z) * rows, (k_ref, v_ref)
    )
    next(arrivals)

    @pl.loop(0, rows // block)
    def _(n):
        where = pl.ds(pl.multiple_of(n * block, block), block)
        four = jnp.dot(
            normed[where, :], qkv_full[:, :q_width], preferred_element_type=jnp.float32
        )
        for h in range(GROUP):
            cut = slice(h * head_dim, (h + 1) * head_dim)
            q_ref[where, cut] = turned(four[:, cut], q_gain[...], where)

    acc[...] = jnp.zeros_like(acc)
    top[...] = jnp.full_like(top, -1e30)

    def unit(which, key_parts, value_parts, allowed=None, among=range(GROUP)):
        key_block = [ref[...] for ref in key_parts]
        value_block = [ref[...] for ref in value_parts]
        key_block = key_block[0] if len(key_block) == 1 else jnp.concatenate(key_block, axis=0)
        value_block = (
            value_block[0] if len(value_block) == 1 else jnp.concatenate(value_block, axis=0)
        )
        wide = jnp.concatenate([value_block, jnp.ones_like(value_block)], axis=1)
        asked = q_ref.at[pl.ds(pl.multiple_of(which * half_rows, half_rows), half_rows), :]

        def scores(h):
            return lax.dot_general(
                asked[:, h * head_dim : (h + 1) * head_dim],
                key_block,
                (((1,), (1,)), ((), ())),
                preferred_element_type=jnp.float32,
            )

        following = scores(among[0])
        for h in among:
            raw = following
            if h != among[-1]:
                following = scores(h + 1)
            if allowed is not None:
                raw = jnp.where(allowed, raw, -1e30)
            before = top[which, h]
            now = jnp.maximum(before, jnp.max(raw, axis=-1, keepdims=True))
            shift = jnp.concatenate([now * factor_log2] * (raw.shape[1] // head_dim), axis=1)
            weights = jnp.exp2(raw * factor_log2 - shift).astype(jnp.bfloat16)
            fade = jnp.exp2((before - now) * factor_log2)
            added = jnp.dot(weights, wide, preferred_element_type=jnp.float32)
            acc[which, h] = acc[which, h] * jnp.concatenate([fade, fade], axis=1) + added
            top[which, h] = now

    low, high = here.z_lo, 1 - here.z_lo

    def low_chunk(x, z):
        chunk = here.chunk(0, x, z)
        return chunk + (z % 2) * (31 - 2 * chunk)

    def part(full, x, z, which):
        start = (4 * x + z) * rows + which * half_rows
        return full.at[pl.ds(pl.multiple_of(start, half_rows), half_rows), :]

    def at_once(places, among=range(GROUP)):
        spots = [(ring(here.x, dx), ring(here.z, dz)) for dx, dz in places]
        unit(
            high,
            [part(keys, x, z, z % 2) for x, z in spots],
            [part(values, x, z, z % 2) for x, z in spots],
            among=among,
        )
        for x, z in spots:
            before = (31 + low_chunk(here.x, here.z) - low_chunk(x, z)) // 32
            which = high + before * (low - high)
            theirs = 1 - z % 2 + before * (2 * (z % 2) - 1)
            unit(which, [part(keys, x, z, theirs)], [part(values, x, z, theirs)], among=among)

    def own(ref, which):
        return ref.at[pl.ds(pl.multiple_of(which * half_rows, half_rows), half_rows), :]

    square = (half_rows, half_rows)
    allowed = lax.broadcasted_iota(jnp.int32, square, 1) <= lax.broadcasted_iota(
        jnp.int32, square, 0
    )
    unit(low, [own(k_ref, low)], [own(v_ref, low)], allowed)
    unit(high, [own(k_ref, high)], [own(v_ref, high)], allowed)
    unit(high, [own(k_ref, low)], [own(v_ref, low)])
    pairs = [
        ((1, 0), (3, 0)), ((0, 1), (0, 3)), ((1, 1), (1, 3)), ((3, 1), (3, 3)),
        ((2, 0), (0, 2)), ((2, 1), (2, 3)),
    ]
    steps = (0, 1, 2, 4, 5)

    tables = tuple(
        sum(pair[i][j] * 4**n for n, pair in enumerate(pairs)) for i in (0, 1) for j in (0, 1)
    )

    def stage(n, rest):
        for when in steps:
            pl.when(n == when)(lambda: next(arrivals) and None)
        digits = [r % 4 for r in rest]
        at_once([digits[:2], digits[2:]])
        return tuple(r // 4 for r in rest)

    lax.fori_loop(0, len(pairs), stage, tuple(jnp.int32(t) for t in tables))

    turn.wait(0)
    next(arrivals, None)
    weights = weight_gather(net, here, out_weight, weight.shape[0])
    next(weights)
    spread = []
    for h in range(GROUP):
        at_once([(1, 2), (3, 2)], [h])
        at_once([(2, 2)], [h])
        for which in (0, 1):
            heads[here.column() * GROUP + h, which * half_rows : (which + 1) * half_rows, :] = (
                acc[which, h, :, :head_dim] / acc[which, h, :, head_dim:]
            ).astype(heads.dtype)
        spread.append(
            column_gather(
                net, here,
                lambda y, which, h=h: heads.at[
                    here.column(y) * GROUP + h, rows_of(rows, which), :
                ],
            )
        )
        next(spread[h])
    queue = [0, None, 1, 0, None, 2, 1, None, 3, 2, None, 3, None, 0, 1, None, 2, 3]
    for h in queue:
        next(weights if h is None else spread[h], None)

    span = 2 * GROUP * head_dim

    def product(y, start):
        left = [
            heads[2 * GROUP * y + i, pl.ds(pl.multiple_of(start, block), block), :]
            for i in range(2 * GROUP)
        ]
        right = out_weight[pl.ds(pl.multiple_of(y * span, span), span), :]
        return jnp.dot(
            jnp.concatenate(left, axis=1), right, preferred_element_type=jnp.float32
        )

    for h in (0, 1):
        next(spread[h])

    @pl.loop(0, rows // block)
    def _(n):
        where = pl.ds(pl.multiple_of(n * block, block), block)
        total[where, :] = product(here.y, n * block)

    for h in (2, 3):
        next(spread[h])
    for shift in (1, -1):

        @pl.loop(0, rows // block)
        def _(n):
            where = pl.ds(pl.multiple_of(n * block, block), block)
            total[where, :] = total[where, :] + product(ring(here.y, shift), n * block)

    for h in range(GROUP):
        next(spread[h], None)
    last = []
    for half in (0, 1):
        slot = pl.multiple_of(((here.z_hi + half) % 2) * half_rows, half_rows)

        @pl.loop(0, half_rows // block)
        def _(n):
            start = slot + n * block
            where = pl.ds(pl.multiple_of(start, block), block)
            added = product(ring(here.y, 2), start)
            result[where, :] = (total[where, :] + added).astype(result.dtype)

        stays = jnp.logical_and(here.core == 0, here.z_hi == 0) if half == 0 else None
        last.append(
            Exchange(
                [
                    (
                        result.at[pl.ds(slot, half_rows), :],
                        home.at[half * half_rows : (half + 1) * half_rows, :],
                        here.chunk_from(half),
                        stays,
                    )
                ],
                sent, landed, 5 + half,
            )
        )
    for half in (0, 1):
        last[half].wait(0)
    net.finish()


def per_device(sizes, tokens, norm_gain, qkv_weight, q_gain, k_gain, out_weight):
    n_row, n_col = sizes
    rows, width = tokens.shape
    half = rows // 2
    head_dim = q_gain.shape[0]
    freqs = jnp.power(
        jnp.float32(ROPE_BASE),
        -jnp.arange(head_dim // 2, dtype=jnp.float32) * 2.0 / head_dim,
    )
    bf16, f32 = jnp.bfloat16, jnp.float32
    copies = SINGLE + 3 * PLANE + TOKEN + SMALL + GROUP * COLUMN
    q_width, out_width = GROUP * head_dim, out_weight.shape[1]
    return pl.pallas_call(
        functools.partial(layer_kernel, head_dim ** (-0.5)),
        out_shape=jax.ShapeDtypeStruct((rows, out_width), bf16),
        in_specs=[pl.BlockSpec(memory_space=pl.ANY)] * 3
        + [pl.BlockSpec(memory_space=pltpu.VMEM)] * 4,
        out_specs=pl.BlockSpec(memory_space=pl.ANY),
        scratch_shapes=[
            pltpu.VMEM((16, width), bf16),
            pltpu.VMEM((rows, head_dim), f32),
            pltpu.VMEM((rows, head_dim), f32),
            pltpu.VMEM((rows, n_col * width), bf16),
            pltpu.VMEM((16, n_col * width), bf16),
            pltpu.VMEM((n_row * qkv_weight.shape[0], qkv_weight.shape[1]), bf16),
            pltpu.VMEM((rows, n_col * width), bf16),
            pltpu.VMEM((rows, q_width), bf16),
            pltpu.VMEM((rows, head_dim), bf16),
            pltpu.VMEM((rows, head_dim), bf16),
            pltpu.VMEM((n_row * rows, head_dim), bf16),
            pltpu.VMEM((n_row * rows, head_dim), bf16),
            pltpu.VMEM((2, GROUP, half, 2 * head_dim), f32),
            pltpu.VMEM((2, GROUP, half, head_dim), f32),
            pltpu.VMEM((n_col * GROUP, rows, head_dim), bf16),
            pltpu.VMEM((n_row * out_weight.shape[0], out_width), bf16),
            pltpu.VMEM((rows, out_width), f32),
            pltpu.VMEM((rows, out_width), bf16),
            pltpu.SemaphoreType.DMA((copies,)),
            pltpu.SemaphoreType.DMA((copies,)),
        ],
        compiler_params=pltpu.CompilerParams(
            collective_id=1, has_side_effects=True, vmem_limit_bytes=52 * 1024 * 1024
        ),
        name="layer_kernel",
    )(
        tokens,
        qkv_weight,
        out_weight,
        norm_gain[None, :],
        jnp.concatenate([freqs, freqs])[None, :],
        q_gain[None, :],
        k_gain[None, :],
    )


def solution(mesh):
    placed = (P("row", "col"), P("col"), P("row", "col"), P(), P(), P("row", "col"))
    return jax.shard_map(
        functools.partial(per_device, (mesh.shape["row"], mesh.shape["col"])),
        mesh=mesh,
        in_specs=placed,
        out_specs=P("row", "col"),
        check_vma=False,
    )
```
